32 devices in a mesh: dp: 4 (over y, core), tensor: 8 (over z, x).
Axes of the slice: x: 2, y: 2, z: 4, core: 2. Of those that a mesh axis runs over, the one named last changes fastest.
Arguments:
- tokens: bfloat16 [4, 2048, 1024], P('dp', 'tensor'), may hold values from -6 to 6
- cotangent: bfloat16 [4, 2048, 1024], P('dp', 'tensor'), may hold values from -6 to 6
- segments: int32 [4, 2048], P('dp'), may hold values from 0 to 2, as said below
- positions: int32 [4, 2048], P('dp'), may hold values from 0 to 1535, as said below
- attngain: float32 [1024], replicated, may hold values from 0.5 to 1.5
- ffngain: float32 [1024], replicated, may hold values from 0.5 to 1.5
- queryheads: bfloat16 [1024, 96], replicated, may hold values from -0.25 to 0.25
- querydims: bfloat16 [1024, 384], replicated, may hold values from -0.25 to 0.25
- keyheads: bfloat16 [1024, 32], replicated, may hold values from -0.25 to 0.25
- keydims: bfloat16 [1024, 128], replicated, may hold values from -0.25 to 0.25
- valueheads: bfloat16 [1024, 32], replicated, may hold values from -0.25 to 0.25
- valuedims: bfloat16 [1024, 128], replicated, may hold values from -0.25 to 0.25
- outproj: bfloat16 [1024, 1024], replicated, may hold values from -1 to 1
- gateproj: bfloat16 [1024, 2816], P(None, 'tensor'), may hold values from -0.1875 to 0.1875
- upproj: bfloat16 [1024, 2816], P(None, 'tensor'), may hold values from -0.1875 to 0.1875
- downproj: bfloat16 [2816, 1024], P('tensor'), may hold values from -0.109375 to 0.109375
Outputs:
- mixed: bfloat16 [4, 2048, 1024], P('dp', 'tensor')
- tokens_grad: bfloat16 [4, 2048, 1024], P('dp', 'tensor')
- attngain_grad: float32 [1024], replicated
- ffngain_grad: float32 [1024], replicated
- queryheads_grad: float32 [1024, 96], replicated
- querydims_grad: float32 [1024, 384], replicated
- keyheads_grad: float32 [1024, 32], replicated
- keydims_grad: float32 [1024, 128], replicated
- valueheads_grad: float32 [1024, 32], replicated
- valuedims_grad: float32 [1024, 128], replicated
- outproj_grad: float32 [1024, 1024], replicated
- gateproj_grad: float32 [1024, 2816], P(None, 'tensor')
- upproj_grad: float32 [1024, 2816], P(None, 'tensor')
- downproj_grad: float32 [2816, 1024], P('tensor')
The draws below stay inside these ranges and needn't reach their ends.
Inputs may be any that keep to these rules, and one draw needn't show every extreme that they name: `segments`: within a row the numbers never fall and every number is one contiguous document; every row holds exactly 3 documents: one of exactly 1536 tokens, and the others of 128 to 384 tokens. `positions`: each token's place within its document: 0 at a document's first token, rising by one along it.
All inputs are finite; a program needn't handle non-finite values.
Results may differ from the reference program's by a relative error of at most 0.022.
The reference program's roundings to bfloat16 on the way count: a program that leaves them out, or rounds other values in their place, can miss the bound.
Values may be sent and summed in bfloat16 or wider, within the bound.
No kernel may reach another device: no remote copies, remote signals or barrier semaphores. Data moves between devices by JAX's collectives and lax.ppermute only.
A program may use at most 256 MiB of HBM per device.

```python
import math
from functools import partial
import jax
import jax.numpy as jnp
from jax import lax

D = 1024
HEADS = 16
HEAD_DIM = 64
QRANK = 6
KRANK = 2
FF = 2816
DOC_LO = 128
ROWS = 4
ROW = 2048
DOC_MAX = 1536


def layout_row(key):
    first_key, second_key = jax.random.split(key)
    pairs = ROW // 4 // (4 * DOC_LO)
    shorts = 2 * pairs
    offsets = jax.random.randint(first_key, (pairs,), 0, DOC_LO + 1, dtype=jnp.int32)
    short_len = jnp.stack([2 * DOC_LO + offsets, 2 * DOC_LO - offsets], axis=1).reshape(shorts).astype(jnp.int32)
    chosen = jax.random.randint(second_key, (), 0, pairs + 1, dtype=jnp.int32)
    long_at = 2 * chosen
    count = shorts + 1
    index = jnp.arange(count, dtype=jnp.int32)
    below = jnp.clip(index, 0, shorts - 1)
    above = jnp.clip(index - 1, 0, shorts - 1)
    doc_len = jnp.where(index < long_at, short_len[below], jnp.where(index == long_at, DOC_MAX, short_len[above])).astype(jnp.int32)
    openings = jnp.concatenate([jnp.zeros((1,), jnp.int32), jnp.cumsum(doc_len)[:-1].astype(jnp.int32)])
    places = jnp.arange(ROW, dtype=jnp.int32)
    covered = (openings[None, :] <= places[:, None]).astype(jnp.int32)
    segment = (jnp.sum(covered, axis=1) - 1).astype(jnp.int32)
    opening = jnp.max(jnp.where(covered > 0, openings[None, :], 0), axis=1).astype(jnp.int32)
    position = (places - opening).astype(jnp.int32)
    return (segment, position)


def layout(key):
    base = jax.random.fold_in(key, 7)
    return jax.vmap(lambda number: layout_row(jax.random.fold_in(base, number)))(jnp.arange(ROWS, dtype=jnp.int32))


def draw_segments(key, part):
    return layout(key)[0]


def draw_positions(key, part):
    return layout(key)[1]


def levels(own_key, shape, pieces, smallest, largest):
    level = 1.0
    for dim, parts in pieces:
        steps = jax.random.uniform(jax.random.fold_in(jax.random.fold_in(own_key, 6), dim), (parts,), jnp.float32, smallest / len(pieces), largest / len(pieces))
        level = level * jnp.repeat(jnp.exp(steps), shape[dim] // parts).reshape((-1,) + (1,) * (len(shape) - 1 - dim))
    return level


def normal_values(own_key, extent, spread, limit, cuts=(), held_as=jnp.bfloat16):
    factor_of = levels(own_key, extent, cuts, -0.22, 0.18) if cuts else 1.0
    drawn = jax.random.normal(own_key, extent, jnp.float32) * spread * factor_of
    return jnp.minimum(jnp.maximum(drawn, -limit), limit).astype(held_as)


def setup_inputs(seed: int = 0) -> dict:
    arg_keys = jax.random.split(jax.random.key(seed), 17)
    tokens = normal_values(arg_keys[0], (ROWS, ROW, D), 1.0, 6.0, ((0, 4), (1, 8)))
    cotangent = normal_values(arg_keys[1], (ROWS, ROW, D), 1.0, 6.0, ((0, 4), (1, 8)))
    segments = draw_segments(jax.random.fold_in(arg_keys[16], 71), 0)
    positions = draw_positions(jax.random.fold_in(arg_keys[16], 71), 0)
    attngain = jnp.clip(1.0 + 0.1 * jax.random.normal(arg_keys[4], (D,), jnp.float32), 0.5, 1.5)
    ffngain = jnp.clip(1.0 + 0.1 * jax.random.normal(arg_keys[5], (D,), jnp.float32), 0.5, 1.5)
    queryheads = normal_values(arg_keys[6], (D, HEADS * QRANK), (D // 2) ** -0.5, 0.25)
    querydims = normal_values(arg_keys[7], (D, QRANK * HEAD_DIM), (D // 2) ** -0.5, 0.25)
    keyheads = normal_values(arg_keys[8], (D, HEADS * KRANK), (D // 2) ** -0.5, 0.25)
    keydims = normal_values(arg_keys[9], (D, KRANK * HEAD_DIM), (D // 2) ** -0.5, 0.25)
    valueheads = normal_values(arg_keys[10], (D, HEADS * KRANK), (D // 2) ** -0.5, 0.25)
    valuedims = normal_values(arg_keys[11], (D, KRANK * HEAD_DIM), (D // 2) ** -0.5, 0.25)
    outproj = normal_values(arg_keys[12], (HEADS * HEAD_DIM, D), (D // 32) ** -0.5, 1.0)
    gateproj = normal_values(arg_keys[13], (D, FF), D ** -0.5, 0.1875, ((1, 8),))
    upproj = normal_values(arg_keys[14], (D, FF), D ** -0.5, 0.1875, ((1, 8),))
    downproj = normal_values(arg_keys[15], (FF, D), FF ** -0.5, 0.109375, ((0, 8),))
    return dict(tokens=tokens, cotangent=cotangent, segments=segments, positions=positions, attngain=attngain, ffngain=ffngain, queryheads=queryheads, querydims=querydims, keyheads=keyheads, keydims=keydims, valueheads=valueheads, valuedims=valuedims, outproj=outproj, gateproj=gateproj, upproj=upproj, downproj=downproj)


highest = lax.Precision.HIGHEST
epsilon = 1e-06

@jax.custom_vjp
def low(v):
    return lax.optimization_barrier(v.astype(jnp.bfloat16)).astype(jnp.float32)

@jax.custom_vjp
def low_back(v):
    return v

def low_keep(v):
    return (low(v), None)

def low_pass(kept, grad):
    return (grad,)

def back_keep(v):
    return (v, None)

def back_low(kept, grad):
    return (low(grad),)
low.defvjp(low_keep, low_pass)
low_back.defvjp(back_keep, back_low)

def matmul(left, right):
    return jnp.dot(left, right, precision=highest)

def normalize(values):
    return values * lax.rsqrt(lax.optimization_barrier(jnp.mean(values * values, axis=-1, keepdims=True)) + epsilon)

def rotate(values, places, sign):
    half = values.shape[-1] // 2
    freqs = 10000.0 ** (-jnp.arange(half, dtype=jnp.float32) * 2.0 / values.shape[-1])
    angles = places.astype(jnp.float32)[:, None] * freqs[None, :]
    cosine = jnp.cos(angles)[:, None, :]
    sine = jnp.sin(angles)[:, None, :]
    first = values[..., :half]
    second = values[..., half:]
    return jnp.concatenate([first * cosine - sign * second * sine, second * cosine + sign * first * sine], axis=-1)

def attend(query, keys, values, segment, begin, size):
    rows = lax.dynamic_slice_in_dim(query, begin, size, 0)
    scores = low_back(jnp.einsum('qhd,khd->hqk', rows, keys, precision=highest) * query.shape[-1] ** (-0.5))
    query_index = begin + jnp.arange(size, dtype=jnp.int32)
    key_index = jnp.arange(keys.shape[0], dtype=jnp.int32)
    query_seg = lax.dynamic_slice_in_dim(segment, begin, size, 0)
    allowed = (query_seg[:, None] == segment[None, :]) & (key_index[None, :] <= query_index[:, None])
    masked = jnp.where(allowed[None], scores, -1e+30)
    topmost = lax.optimization_barrier(jnp.max(masked, axis=-1, keepdims=True))
    expo = jnp.exp(masked - topmost)
    probs = low(expo / lax.optimization_barrier(jnp.sum(expo, axis=-1, keepdims=True)))
    return jnp.einsum('hqk,khd->qhd', probs, values, precision=highest)

def forward_row(row, weights, segment, places):
    attngain, ffngain, queryheads, querydims, keyheads, keydims, valueheads, valuedims, outproj, gateproj, upproj, downproj = weights
    length = row.shape[0]
    input_one = low(normalize(row) * attngain)
    qheads_f = low(low_back(matmul(input_one, queryheads))).reshape(length, HEADS, QRANK)
    qdims_f = low(rotate(low_back(matmul(input_one, querydims)).reshape(length, QRANK, HEAD_DIM), places, 1.0))
    kheads_f = low(low_back(matmul(input_one, keyheads))).reshape(length, HEADS, KRANK)
    kdims_f = low(rotate(low_back(matmul(input_one, keydims)).reshape(length, KRANK, HEAD_DIM), places, 1.0))
    vheads_f = low(low_back(matmul(input_one, valueheads))).reshape(length, HEADS, KRANK)
    vdims_f = low(low_back(matmul(input_one, valuedims))).reshape(length, KRANK, HEAD_DIM)
    query = low(jnp.einsum('thr,trd->thd', qheads_f, qdims_f, precision=highest) / QRANK)
    keys = low(jnp.einsum('thr,trd->thd', kheads_f, kdims_f, precision=highest) / KRANK)
    values = low(jnp.einsum('thr,trd->thd', vheads_f, vdims_f, precision=highest) / KRANK)
    size = math.gcd(length, 512)
    blockwise = jax.checkpoint(partial(attend, size=size))
    begins = jnp.arange(length // size, dtype=jnp.int32) * size
    attended = lax.map(lambda begin: blockwise(query, keys, values, segment, begin), begins)
    merged = low(low_back(attended.reshape(length, HEADS * HEAD_DIM)))
    residual = row + low_back(matmul(merged, outproj))
    input_two = low(normalize(residual) * ffngain)
    gate = low_back(matmul(input_two, gateproj))
    upper = low_back(matmul(input_two, upproj))
    inner = low(gate * jax.nn.sigmoid(gate) * upper)
    return residual + matmul(inner, downproj)

def reference(tokens, cotangent, segments, positions, attngain, ffngain, queryheads, querydims, keyheads, keydims, valueheads, valuedims, outproj, gateproj, upproj, downproj):
    params = tuple((w.astype(jnp.float32) for w in (attngain, ffngain, queryheads, querydims, keyheads, keydims, valueheads, valuedims, outproj, gateproj, upproj, downproj)))

    def row_step(totals, item):
        row_x, row_dy, row_seg, row_pos = item

        def forward(xrow, weights):
            return forward_row(xrow, weights, row_seg, row_pos)
        result, pullback = jax.vjp(forward, row_x, params)
        grad_x, grad_w = pullback(row_dy)
        totals = jax.tree.map(jnp.add, totals, grad_w)
        return (totals, (result.astype(jnp.bfloat16), grad_x.astype(jnp.bfloat16)))
    zeros = jax.tree.map(jnp.zeros_like, params)
    totals, outputs = lax.scan(row_step, zeros, (tokens.astype(jnp.float32), cotangent.astype(jnp.float32), segments, positions))
    return (outputs[0], outputs[1], totals[0], totals[1], totals[2], totals[3], totals[4], totals[5], totals[6], totals[7], totals[8], totals[9], totals[10], totals[11])
```

```python
import functools
import jax
import jax.numpy as jnp
from jax import lax
from jax.experimental import pallas as pl
from jax.experimental.pallas import tpu as pltpu

from jax.sharding import PartitionSpec as P

HEADS = 16
HEAD_DIM = 64
QRANK = 6
KRANK = 2
PAIRS = HEADS // 2
QHW = HEADS * QRANK
QDW = QRANK * HEAD_DIM
KDW = KRANK * HEAD_DIM
KHW = HEADS * KRANK
FACW = 2 * KDW + 2 * KHW
QFW = QHW + QDW
LOG2E = 1.4426950408889634
EPS = 1e-06
BF = jnp.bfloat16
F32 = jnp.float32


def mm(a, b, ca=1, cb=0):
    return lax.dot_general(a, b, (((ca,), (cb,)), ((), ())), preferred_element_type=F32)


def expand_pair(bk0, bk1, rows):
    first = rows[0] * bk0 + rows[1] * bk1
    second = rows[2] * bk0 + rows[3] * bk1
    return jnp.concatenate([first, second], axis=0) * (1.0 / KRANK)


def query_pair(qfac_ref, aq_s, pair):
    halves = []
    for h in range(2):
        acc = None
        for r in range(QRANK):
            row = aq_s[pl.ds(pair * (2 * QRANK) + h * QRANK + r, 1), :]
            term = row * qfac_ref[QHW + r * HEAD_DIM : QHW + (r + 1) * HEAD_DIM, :].astype(F32)
            acc = term if acc is None else acc + term
        halves.append(acc * (1.0 / QRANK))
    return jnp.concatenate(halves, axis=0).astype(BF)


def fill_tables(scal_ref, qfac_ref, fac_ref, start_ref, aq_s, kv_s, bias_s):
    length = qfac_ref.shape[1]
    me = scal_ref[1]
    aq_s[...] = qfac_ref[0:QHW, :].astype(F32)
    row = lax.broadcasted_iota(jnp.int32, (length, length), 0) + me * length
    column = lax.broadcasted_iota(jnp.int32, (length, length), 1)
    begin = start_ref[...]

    def fill(c, carry):
        kv_s[c] = fac_ref[c, 2 * KDW :, :].astype(F32)
        key = column + c * length
        keep = (key >= begin) & (key <= row)
        bias_s[c] = jnp.where(keep, 0.0, -1e30)
        return carry

    lax.fori_loop(scal_ref[0], me + 1, fill, 0)


def key_pair(fac_ref, kv_s, c, pair, which):
    base = which * KDW
    b0 = fac_ref[c, base : base + HEAD_DIM, :].astype(F32)
    b1 = fac_ref[c, base + HEAD_DIM : base + 2 * HEAD_DIM, :].astype(F32)
    rows = [kv_s[c, pl.ds(which * KHW + pair * 4 + j, 1), :] for j in range(4)]
    return expand_pair(b0, b1, rows), b0, b1, rows


def forward_kernel(scal_ref, qfac_ref, fac_ref, start_ref, o_ref, lse_ref, aq_s, kv_s, bias_s, s_s):
    pair = pl.program_id(0)
    length = qfac_ref.shape[1]
    lo, me = scal_ref[0], scal_ref[1]

    @pl.when(pair == 0)
    def _():
        fill_tables(scal_ref, qfac_ref, fac_ref, start_ref, aq_s, kv_s, bias_s)

    query = jnp.transpose(query_pair(qfac_ref, aq_s, pair).astype(F32)) * (HEAD_DIM**-0.5)
    low_half = lax.broadcasted_iota(jnp.int32, (length, 2 * HEAD_DIM), 1) < HEAD_DIM
    queries = [
        jnp.where(low_half, query, 0.0).astype(BF),
        jnp.where(low_half, 0.0, query).astype(BF),
    ]
    lanes = 128
    pieces = length // lanes

    def score(c, tops):
        keys = key_pair(fac_ref, kv_s, c, pair, 0)[0].astype(BF)
        bias = bias_s[c]
        new = []
        for h in range(2):
            s = mm(queries[h], keys) * LOG2E + bias
            s_s[h, c] = s
            top = tops[h]
            for i in range(pieces):
                top = jnp.maximum(top, s[:, i * lanes : (i + 1) * lanes])
            new.append(top)
        return tuple(new)

    start = jnp.full((length, lanes), -1e30, F32)
    tops = lax.fori_loop(lo, me + 1, score, (start, start))
    tops = [jnp.max(top, axis=1, keepdims=True) for top in tops]

    def value(c, carry):
        values = key_pair(fac_ref, kv_s, c, pair, 1)[0].astype(BF)
        new = []
        for h in range(2):
            p = jnp.exp2(s_s[h, c] - tops[h])
            total = carry[2 * h]
            for i in range(pieces):
                total = total + p[:, i * lanes : (i + 1) * lanes]
            new += [total, carry[2 * h + 1] + mm(p.astype(BF), values, 1, 1)]
        return tuple(new)

    zero = jnp.zeros((length, lanes), F32)
    wide = jnp.zeros((length, 2 * HEAD_DIM), F32)
    done = lax.fori_loop(lo, me + 1, value, (zero, wide, zero, wide))
    outs = []
    for h in range(2):
        total = jnp.sum(done[2 * h], axis=1, keepdims=True)
        outs.append(done[2 * h + 1] / total)
        lse_ref[h] = jnp.broadcast_to(tops[h] + jnp.log2(total), (length, lanes))
    o_ref[...] = jnp.where(low_half, outs[0], outs[1]).astype(BF)


def full(shape):
    return pl.BlockSpec(shape, lambda p, s: (0,) * len(shape))


def attention_forward(scal, qfac, fac, start):
    n, unused, length = fac.shape
    return pl.pallas_call(
        forward_kernel,
        out_shape=(
            jax.ShapeDtypeStruct((length, HEADS * HEAD_DIM), BF),
            jax.ShapeDtypeStruct((HEADS, length, 128), F32),
        ),
        grid_spec=pltpu.PrefetchScalarGridSpec(
            num_scalar_prefetch=1,
            grid=(PAIRS,),
            in_specs=[full(qfac.shape), full(fac.shape), full(start.shape)],
            out_specs=[
                pl.BlockSpec((length, 2 * HEAD_DIM), lambda p, s: (0, p)),
                pl.BlockSpec((2, length, 128), lambda p, s: (p, 0, 0)),
            ],
            scratch_shapes=[
                pltpu.VMEM((QHW, length), F32),
                pltpu.VMEM((n, 2 * KHW, length), F32),
                pltpu.VMEM((n, length, length), F32),
                pltpu.VMEM((2, n, length, length), F32),
            ],
        ),
        compiler_params=pltpu.CompilerParams(
            dimension_semantics=("arbitrary",), vmem_limit_bytes=58 << 20
        ),
        name="attention_forward",
    )(scal, qfac, fac, start)


def backward_kernel(
    scal_ref,
    qfac_ref,
    fac_ref,
    start_ref,
    o_ref,
    do_ref,
    lse_ref,
    cos_ref,
    sin_ref,
    terms_ref,
    dq_ref,
    aq_s,
    kv_s,
    bias_s,
    acc_s,
    heads_s,
    dbq_s,
    daq_s,
):
    pair = pl.program_id(0)
    length = qfac_ref.shape[1]
    n = fac_ref.shape[0]
    lo, me = scal_ref[0], scal_ref[1]
    pieces = length // 128

    @pl.when(pair == 0)
    def _():
        fill_tables(scal_ref, qfac_ref, fac_ref, start_ref, aq_s, kv_s, bias_s)
        dbq_s[...] = jnp.zeros_like(dbq_s)

        def clear(c, carry):
            acc_s[c] = jnp.zeros((2 * KDW, length), F32)
            return carry

        lax.fori_loop(lo, me + 1, clear, 0)

    query_t = query_pair(qfac_ref, aq_s, pair).astype(F32) * (HEAD_DIM**-0.5)
    query = jnp.transpose(query_t)
    query_t = query_t.astype(BF)
    do = do_ref[...].astype(F32)
    do_t = jnp.transpose(do).astype(BF)
    low_half = lax.broadcasted_iota(jnp.int32, (length, 2 * HEAD_DIM), 1) < HEAD_DIM
    product = do * o_ref[...].astype(F32)
    queries, grads, deltas, stats = [], [], [], []
    for h in range(2):
        keep = low_half if h == 0 else jnp.logical_not(low_half)
        queries.append(jnp.where(keep, query, 0.0).astype(BF))
        grads.append(jnp.where(keep, do, 0.0).astype(BF))
        deltas.append(jnp.sum(jnp.where(keep, product, 0.0), axis=1, keepdims=True))
        stats.append(lse_ref[h])

    def step(c, dqs):
        keys, kb0, kb1, krows = key_pair(fac_ref, kv_s, c, pair, 0)
        values, vb0, vb1, vrows = key_pair(fac_ref, kv_s, c, pair, 1)
        keys, values = keys.astype(BF), values.astype(BF)
        bias = bias_s[c]
        new, sums, rows = [], [None] * 4, []
        for h in range(2):
            s = mm(queries[h], keys) * LOG2E + bias
            lse = jnp.concatenate([stats[h]] * pieces, axis=1)
            p = jnp.exp2(s - lse)
            dp = mm(grads[h], values)
            ds = (p * (dp - deltas[h])).astype(BF)
            pb = p.astype(BF)
            new.append(dqs[h] + mm(ds, keys, 1, 1))
            half = slice(h * HEAD_DIM, (h + 1) * HEAD_DIM)
            dk = mm(query_t[half, :], ds)
            dv = mm(do_t[half, :], pb)
            for which, d, b0, b1, a in ((0, dk, kb0, kb1, krows), (1, dv, vb0, vb1, vrows)):
                for r, b in ((0, b0), (1, b1)):
                    term = d * a[2 * h + r]
                    k = 2 * which + r
                    sums[k] = term if sums[k] is None else sums[k] + term
                    rows.append((which * 4 + 2 * h + r, jnp.sum(d * b, axis=0, keepdims=True)))
        for k in range(4):
            part = slice(k * HEAD_DIM, (k + 1) * HEAD_DIM)
            acc_s[c, part, :] = acc_s[c, part, :] + sums[k]
        for k, row in rows:
            where = (k // 4) * KHW + pair * 4 + k % 4
            heads_s[c, pl.ds(where, 1), :] = row
        return tuple(new)

    zero = jnp.zeros((length, 2 * HEAD_DIM), F32)
    dqs = lax.fori_loop(lo, me + 1, step, (zero, zero))
    dq_t = jnp.transpose(jnp.where(low_half, dqs[0], dqs[1])) * (HEAD_DIM**-0.5 / QRANK)
    for h in range(2):
        d = dq_t[h * HEAD_DIM : (h + 1) * HEAD_DIM, :]
        for r in range(QRANK):
            part = slice(r * HEAD_DIM, (r + 1) * HEAD_DIM)
            b = qfac_ref[QHW + r * HEAD_DIM : QHW + (r + 1) * HEAD_DIM, :].astype(F32)
            k = pl.ds(pair * (2 * QRANK) + h * QRANK + r, 1)
            daq_s[k, :] = jnp.sum(d * b, axis=0, keepdims=True)
            dbq_s[part, :] = dbq_s[part, :] + d * aq_s[k, :]

    @pl.when(pair == PAIRS - 1)
    def _():
        cosine, sine = cos_ref[...], sin_ref[...]
        half = HEAD_DIM // 2
        dq_ref[0:QHW, :] = daq_s[...].astype(BF)
        for r in range(QRANK):
            first = dbq_s[r * HEAD_DIM : r * HEAD_DIM + half, :]
            second = dbq_s[r * HEAD_DIM + half : (r + 1) * HEAD_DIM, :]
            turned = jnp.concatenate(
                [first * cosine + second * sine, second * cosine - first * sine], axis=0
            )
            dq_ref[QHW + r * HEAD_DIM : QHW + (r + 1) * HEAD_DIM, :] = turned.astype(BF)

        def flush(c, carry):
            inside = (c >= lo) & (c <= me)

            @pl.when(inside)
            def _():
                terms_ref[c, 0 : 2 * KDW, :] = (acc_s[c] * (1.0 / KRANK)).astype(BF)
                terms_ref[c, 2 * KDW :, :] = (heads_s[c] * (1.0 / KRANK)).astype(BF)

            @pl.when(jnp.logical_not(inside))
            def _():
                terms_ref[c] = jnp.zeros((FACW, length), BF)

            return carry

        lax.fori_loop(0, n, flush, 0)


def attention_backward(scal, qfac, fac, start, o, do, lse, cosine, sine):
    n, unused, length = fac.shape
    return pl.pallas_call(
        backward_kernel,
        out_shape=(
            jax.ShapeDtypeStruct((n, FACW, length), BF),
            jax.ShapeDtypeStruct((QFW, length), BF),
        ),
        grid_spec=pltpu.PrefetchScalarGridSpec(
            num_scalar_prefetch=1,
            grid=(PAIRS,),
            in_specs=[
                full(qfac.shape),
                full(fac.shape),
                full(start.shape),
                pl.BlockSpec((length, 2 * HEAD_DIM), lambda p, s: (0, p)),
                pl.BlockSpec((length, 2 * HEAD_DIM), lambda p, s: (0, p)),
                pl.BlockSpec((2, length, 128), lambda p, s: (p, 0, 0)),
                full(cosine.shape),
                full(sine.shape),
            ],
            out_specs=[full((n, FACW, length)), full((QFW, length))],
            scratch_shapes=[
                pltpu.VMEM((QHW, length), F32),
                pltpu.VMEM((n, 2 * KHW, length), F32),
                pltpu.VMEM((n, length, length), F32),
                pltpu.VMEM((n, 2 * KDW, length), F32),
                pltpu.VMEM((n, 2 * KHW, length), F32),
                pltpu.VMEM((QDW, length), F32),
                pltpu.VMEM((QHW, length), F32),
            ],
        ),
        compiler_params=pltpu.CompilerParams(
            dimension_semantics=("arbitrary",), vmem_limit_bytes=58 << 20
        ),
        name="attention_backward",
    )(scal, qfac, fac, start, o, do, lse, cosine, sine)


def norm_of(values):
    inverse = lax.rsqrt(jnp.mean(values * values, axis=-1, keepdims=True) + EPS)
    return values * inverse, inverse


def turn(values, cosine, sine, sign):
    half = HEAD_DIM // 2
    parts = []
    for r in range(values.shape[0] // HEAD_DIM):
        first = values[r * HEAD_DIM : r * HEAD_DIM + half, :]
        second = values[r * HEAD_DIM + half : (r + 1) * HEAD_DIM, :]
        parts.append(first * cosine - sign * second * sine)
        parts.append(second * cosine + sign * first * sine)
    return jnp.concatenate(parts, axis=0)


def enter_kernel(x_ref, gain_ref, qh, qd, kh, kd, vh, vd, cos_ref, sin_ref, xa_ref, qfac_ref, fac_ref):
    normed = norm_of(x_ref[...].astype(F32))[0]
    xa = (normed * gain_ref[...]).astype(BF)
    xa_ref[...] = xa
    cosine, sine = cos_ref[...], sin_ref[...]
    kdims = turn(jnp.transpose(mm(xa, kd[...])), cosine, sine, 1.0)
    fac_ref[0:KDW, :] = kdims.astype(BF)
    fac_ref[KDW : 2 * KDW, :] = jnp.transpose(mm(xa, vd[...])).astype(BF)
    fac_ref[2 * KDW : 2 * KDW + KHW, :] = jnp.transpose(mm(xa, kh[...])).astype(BF)
    fac_ref[2 * KDW + KHW :, :] = jnp.transpose(mm(xa, vh[...])).astype(BF)
    qfac_ref[0:QHW, :] = jnp.transpose(mm(xa, qh[...])).astype(BF)
    qdims = turn(jnp.transpose(mm(xa, qd[...])), cosine, sine, 1.0)
    qfac_ref[QHW:, :] = qdims.astype(BF)


def enter(x, gain, weights, cosine, sine):
    length, width = x.shape
    return pl.pallas_call(
        enter_kernel,
        out_shape=(
            jax.ShapeDtypeStruct((length, width), BF),
            jax.ShapeDtypeStruct((QFW, length), BF),
            jax.ShapeDtypeStruct((FACW, length), BF),
        ),
        compiler_params=pltpu.CompilerParams(vmem_limit_bytes=40 << 20),
        name="enter",
    )(x, gain, *weights, cosine, sine)


def leave_query_kernel(xa_ref, dq_ref, fgain_ref, out_ref):
    xa_t = jnp.transpose(xa_ref[...].astype(F32)).astype(BF)
    d = dq_ref[...].astype(F32)
    out_ref[:, 0:QHW] = mm(xa_t, d[0:QHW, :].astype(BF), 1, 1).astype(BF)
    out_ref[:, QHW:QFW] = mm(xa_t, d[QHW:, :].astype(BF), 1, 1).astype(BF)
    out_ref[:, QFW:] = jnp.transpose(jnp.concatenate([fgain_ref[...]] * (512 - QFW), axis=0)).astype(BF)


def leave_key_kernel(
    x_ref, xa_ref, gain_ref, dres_ref, dq_ref, kg_ref, cos_ref, sin_ref, qh, qd, kh, kd, vh, vd, tg_ref, out_ref
):
    normed, inverse = norm_of(x_ref[...].astype(F32))
    g = kg_ref[...]
    dkd = turn(g[0:KDW, :], cos_ref[...], sin_ref[...], -1.0)
    d_kd = jnp.transpose(dkd).astype(BF)
    d_vd = jnp.transpose(g[KDW : 2 * KDW, :]).astype(BF)
    d_kh = jnp.transpose(g[2 * KDW : 2 * KDW + KHW, :]).astype(BF)
    d_vh = jnp.transpose(g[2 * KDW + KHW :, :]).astype(BF)
    dq = dq_ref[...].astype(F32)
    d_qh = jnp.transpose(dq[0:QHW, :]).astype(BF)
    d_qd = jnp.transpose(dq[QHW:, :]).astype(BF)
    xa_t = jnp.transpose(xa_ref[...].astype(F32)).astype(BF)
    dxa = mm(d_qd, qd[...], 1, 1) + mm(d_qh, qh[...], 1, 1)
    dxa = dxa + mm(d_kd, kd[...], 1, 1) + mm(d_vd, vd[...], 1, 1)
    dxa = dxa + mm(d_kh, kh[...], 1, 1) + mm(d_vh, vh[...], 1, 1)
    scaled = dxa * gain_ref[...]
    product = dxa * normed
    mean = jnp.mean(scaled * normed, axis=-1, keepdims=True)
    tg_ref[...] = (dres_ref[...] + inverse * (scaled - normed * mean)).astype(BF)
    gain_part = jnp.sum(product, axis=0, keepdims=True)
    out_ref[:, 0:KDW] = mm(xa_t, d_kd).astype(BF)
    out_ref[:, KDW : 2 * KDW] = mm(xa_t, d_vd).astype(BF)
    out_ref[:, 2 * KDW : 2 * KDW + KHW] = mm(xa_t, d_kh).astype(BF)
    out_ref[:, 2 * KDW + KHW : FACW] = mm(xa_t, d_vh).astype(BF)
    out_ref[:, FACW:] = jnp.transpose(jnp.concatenate([gain_part] * (384 - FACW), axis=0)).astype(BF)


def leave_query(xa, dq, fgain):
    width = xa.shape[1]
    return pl.pallas_call(
        leave_query_kernel,
        out_shape=jax.ShapeDtypeStruct((width, 512), BF),
        compiler_params=pltpu.CompilerParams(vmem_limit_bytes=40 << 20),
        name="leave_query",
    )(xa, dq, fgain)


def leave_key(x, xa, gain, dres, dq, kg, cosine, sine, weights):
    length, width = x.shape
    return pl.pallas_call(
        leave_key_kernel,
        out_shape=(
            jax.ShapeDtypeStruct((length, width), BF),
            jax.ShapeDtypeStruct((width, 384), BF),
        ),
        compiler_params=pltpu.CompilerParams(vmem_limit_bytes=40 << 20),
        name="leave_key",
    )(x, xa, gain, dres, dq, kg, cosine, sine, *weights)


class Grid:
    def __init__(self, dp, tensor):
        self.c = 2 if dp % 2 == 0 else 1
        self.y = dp // self.c
        self.x = self.y if tensor % self.y == 0 else 1
        self.z = tensor // self.x
        self.dp, self.tensor = dp, tensor
        self.axes = {
            "c": ("dp", 1, self.c),
            "y": ("dp", self.c, self.y),
            "x": ("tensor", 1, self.x),
            "z": ("tensor", self.x, self.z),
        }

    def size(self, g):
        return self.axes[g][2]

    def place(self, g):
        axis, stride, size = self.axes[g]
        return (lax.axis_index(axis) // stride) % size

    def swap(self, v, g, r):
        axis, stride, size = self.axes[g]
        total = self.dp if axis == "dp" else self.tensor
        return lax.ppermute(v, axis, [(i, i ^ (r * stride)) for i in range(total)])

    def scatter_sum(self, v, g, last=BF):
        size = self.size(g)
        if size == 1:
            return v.astype(last)
        me = self.place(g)
        rows = v.shape[0] // size
        got = []
        for r in range(1, size):
            got.append(self.swap(lax.dynamic_slice_in_dim(v, (me ^ r) * rows, rows, 0), g, r))
        total = lax.dynamic_slice_in_dim(v, me * rows, rows, 0).astype(F32)
        for piece in got:
            total = total + piece.astype(F32)
        return total.astype(last)

    def gather(self, v, g):
        size = self.size(g)
        if size == 1:
            return v
        me = self.place(g)
        rows = v.shape[0]
        got = [v] + [self.swap(v, g, r) for r in range(1, size)]
        if size == 2:
            return jnp.concatenate(
                [jnp.where(me == 0, got[0], got[1]), jnp.where(me == 0, got[1], got[0])], axis=0
            )
        out = jnp.zeros((rows * size,) + v.shape[1:], v.dtype)
        for r in range(size):
            out = lax.dynamic_update_slice_in_dim(out, got[r], (me ^ r) * rows, 0)
        return out

    def sum_all(self, v, order):
        for g in order:
            v = self.scatter_sum(v, g)
        for g in reversed(order):
            v = self.gather(v, g)
        return v


def contract(left, right, left_dim, right_dim):
    return lax.dot_general(
        left, right, (((left_dim,), (right_dim,)), ((), ())), preferred_element_type=jnp.float32
    )


def norm_back(grad_out, normed, inverse, gain):
    scaled = grad_out * gain
    gain_part = jnp.sum(grad_out * normed, axis=0)
    grad_in = inverse * (scaled - normed * jnp.mean(scaled * normed, axis=-1, keepdims=True))
    return (grad_in, gain_part)


def body(
    grid,
    tokens,
    cotangent,
    segments,
    positions,
    attngain,
    ffngain,
    queryheads,
    querydims,
    keyheads,
    keydims,
    valueheads,
    valuedims,
    outproj,
    gateproj,
    upproj,
    downproj,
):
    x = tokens[0]
    upstream = cotangent[0]
    length = x.shape[0]
    me = lax.axis_index("tensor")
    offset = me * length
    places = lax.dynamic_slice_in_dim(positions[0], offset, length)
    half = HEAD_DIM // 2
    freqs = 10000.0 ** (-jnp.arange(half, dtype=F32) * 2.0 / HEAD_DIM)
    angles = freqs[:, None] * places.astype(F32)[None, :]
    cosine, sine = jnp.cos(angles), jnp.sin(angles)
    start = (offset + jnp.arange(length, dtype=jnp.int32) - places)[:, None]
    scal = jnp.stack([jnp.maximum(offset - places[0], 0) // length, me]).astype(jnp.int32)
    weights = (queryheads, querydims, keyheads, keydims, valueheads, valuedims)
    xa, qfac, fac = enter(x, attngain[None, :], weights, cosine, sine)

    fac_z = grid.gather(fac[None, None], "z")
    fac_x = [fac_z] + [grid.swap(fac_z, "x", r) for r in range(1, grid.x)]
    mine = grid.place("x")
    facs = jnp.zeros((grid.z, grid.x) + fac.shape, BF)
    for r in range(grid.x):
        facs = lax.dynamic_update_slice_in_dim(facs, fac_x[r], mine ^ r, 1)
    facs = facs.reshape((grid.tensor,) + fac.shape)

    attn_out, lse = attention_forward(scal, qfac, facs, start)

    local = x.astype(F32)
    residual = local + jnp.dot(attn_out, outproj, preferred_element_type=jnp.float32)
    inverse_two = lax.rsqrt(jnp.mean(residual * residual, axis=-1, keepdims=True) + EPS)
    normed_two = residual * inverse_two
    input_two = (normed_two * ffngain).astype(jnp.bfloat16)
    shard = gateproj.shape[1]
    whole_two = lax.all_gather(input_two, "tensor", axis=0, tiled=True)
    paired = jnp.concatenate([gateproj, upproj], axis=1)
    joined = jnp.dot(whole_two, paired, preferred_element_type=jnp.float32)
    gate = joined[:, :shard]
    upper = joined[:, shard:]
    sigma = jax.nn.sigmoid(gate)
    active = gate * sigma
    inner = (active * upper).astype(jnp.bfloat16)
    ffn_out = lax.psum_scatter(
        jnp.dot(inner, downproj, preferred_element_type=jnp.float32).astype(jnp.bfloat16),
        "tensor",
        scatter_dimension=0,
        tiled=True,
    ).astype(jnp.float32)
    piece = lax.all_gather(upstream, "tensor", axis=0, tiled=True)
    down_part = contract(inner, piece, 0, 0)
    held = contract(piece, downproj, 1, 1)
    d_gate = (held * upper * sigma * (1.0 + gate * (1.0 - sigma))).astype(jnp.bfloat16)
    d_upper = (held * active).astype(jnp.bfloat16)
    d_paired = jnp.concatenate([d_gate, d_upper], axis=1)
    pair_part = contract(whole_two, d_paired, 0, 0)
    gate_part = pair_part[:, :shard]
    up_part = pair_part[:, shard:]
    d_norm_two = lax.psum_scatter(
        contract(d_paired, paired, 1, 1).astype(jnp.bfloat16),
        "tensor",
        scatter_dimension=0,
        tiled=True,
    ).astype(jnp.float32)
    gate_part, up_part, down_part = (
        lax.psum(gate_part.astype(jnp.bfloat16), "dp").astype(jnp.float32),
        lax.psum(up_part.astype(jnp.bfloat16), "dp").astype(jnp.float32),
        lax.psum(down_part.astype(jnp.bfloat16), "dp").astype(jnp.float32),
    )
    mixed = (residual + ffn_out).astype(jnp.bfloat16)
    grad_through, ffngain_part = norm_back(d_norm_two, normed_two, inverse_two, ffngain)
    d_residual = upstream.astype(jnp.float32) + grad_through
    d_res_low = d_residual.astype(jnp.bfloat16)
    outproj_part = contract(attn_out, d_res_low, 0, 0).astype(BF)
    d_attended = contract(d_res_low, outproj, 1, 1).astype(jnp.bfloat16)

    terms, dq = attention_backward(
        scal, qfac, facs, start, attn_out, d_attended, lse, cosine, sine
    )
    terms = terms.reshape((grid.z, grid.x) + fac.shape)
    near = lax.dynamic_slice_in_dim(terms, mine, 1, 1).astype(F32)
    for r in range(1, grid.x):
        near = near + grid.swap(lax.dynamic_slice_in_dim(terms, mine ^ r, 1, 1), "x", r).astype(F32)
    key_grads = grid.scatter_sum(near[:, 0].astype(BF), "z", F32)[0]

    query_part = leave_query(xa, dq, ffngain_part[None, :])
    tokens_grad, key_part = leave_key(
        x, xa, attngain[None, :], d_residual, dq, key_grads, cosine, sine, weights
    )
    order = ("c", "x", "y", "z")
    outproj_sum = grid.sum_all(outproj_part, order).astype(F32)
    query_sum = grid.sum_all(query_part, order).astype(F32)
    key_sum = grid.sum_all(key_part, order).astype(F32)
    return (
        mixed[None],
        tokens_grad[None],
        key_sum[:, FACW],
        query_sum[:, QFW],
        query_sum[:, :QHW],
        query_sum[:, QHW:QFW],
        key_sum[:, 2 * KDW : 2 * KDW + KHW],
        key_sum[:, :KDW],
        key_sum[:, 2 * KDW + KHW : FACW],
        key_sum[:, KDW : 2 * KDW],
        outproj_sum,
        gate_part,
        up_part,
        down_part,
    )


def solution(mesh):
    grid = Grid(mesh.shape["dp"], mesh.shape["tensor"])
    rows = P("dp", "tensor", None)
    placed = (rows, rows, P("dp", None), P("dp", None)) + (P(),) * 9
    halves = (P(None, "tensor"), P(None, "tensor"), P("tensor", None))
    return jax.shard_map(
        functools.partial(body, grid),
        mesh=mesh,
        in_specs=placed + halves,
        out_specs=(rows, rows) + (P(),) * 9 + halves,
        check_vma=False,
    )
```

```python
import functools
import jax
import jax.numpy as jnp
from jax import lax
from jax.experimental import pallas as pl
from jax.experimental.pallas import tpu as pltpu

from jax.sharding import PartitionSpec as P

HEADS = 16
HEAD_DIM = 64
QRANK = 6
KRANK = 2
PAIRS = HEADS // 2
QHW = HEADS * QRANK
QDW = QRANK * HEAD_DIM
KDW = KRANK * HEAD_DIM
KHW = HEADS * KRANK
FACW = 2 * KDW + 2 * KHW
QFW = QHW + QDW
LOG2E = 1.4426950408889634
EPS = 1e-06
BF = jnp.bfloat16
F32 = jnp.float32


def mm(a, b, ca=1, cb=0):
    return lax.dot_general(a, b, (((ca,), (cb,)), ((), ())), preferred_element_type=F32)


def expand_pair(bk0, bk1, rows):
    first = rows[0] * bk0 + rows[1] * bk1
    second = rows[2] * bk0 + rows[3] * bk1
    return jnp.concatenate([first, second], axis=0) * (1.0 / KRANK)


def query_pair(qfac_ref, aq_s, pair):
    halves = []
    for h in range(2):
        acc = None
        for r in range(QRANK):
            row = aq_s[pl.ds(pair * (2 * QRANK) + h * QRANK + r, 1), :]
            term = row * qfac_ref[QHW + r * HEAD_DIM : QHW + (r + 1) * HEAD_DIM, :].astype(F32)
            acc = term if acc is None else acc + term
        halves.append(acc * (1.0 / QRANK))
    return jnp.concatenate(halves, axis=0).astype(BF)


def fill_tables(scal_ref, qfac_ref, fac_ref, start_ref, aq_s, kv_s, bias_s):
    length = qfac_ref.shape[1]
    me = scal_ref[1]
    aq_s[...] = qfac_ref[0:QHW, :].astype(F32)
    row = lax.broadcasted_iota(jnp.int32, (length, length), 0) + me * length
    column = lax.broadcasted_iota(jnp.int32, (length, length), 1)
    begin = start_ref[...]

    def fill(c, carry):
        kv_s[c] = fac_ref[c, 2 * KDW :, :].astype(F32)
        key = column + c * length
        keep = (key >= begin) & (key <= row)
        bias_s[c] = jnp.where(keep, 0.0, -1e30)
        return carry

    lax.fori_loop(scal_ref[0], me + 1, fill, 0)


def key_pair(fac_ref, kv_s, c, pair, which):
    base = which * KDW
    b0 = fac_ref[c, base : base + HEAD_DIM, :].astype(F32)
    b1 = fac_ref[c, base + HEAD_DIM : base + 2 * HEAD_DIM, :].astype(F32)
    rows = [kv_s[c, pl.ds(which * KHW + pair * 4 + j, 1), :] for j in range(4)]
    return expand_pair(b0, b1, rows), b0, b1, rows


def forward_kernel(scal_ref, qfac_ref, fac_ref, start_ref, o_ref, lse_ref, aq_s, kv_s, bias_s, s_s):
    pair = pl.program_id(0)
    length = qfac_ref.shape[1]
    lo, me = scal_ref[0], scal_ref[1]

    @pl.when(pair == 0)
    def _():
        fill_tables(scal_ref, qfac_ref, fac_ref, start_ref, aq_s, kv_s, bias_s)

    query = jnp.transpose(query_pair(qfac_ref, aq_s, pair).astype(F32)) * (HEAD_DIM**-0.5)
    low_half = lax.broadcasted_iota(jnp.int32, (length, 2 * HEAD_DIM), 1) < HEAD_DIM
    queries = [
        jnp.where(low_half, query, 0.0).astype(BF),
        jnp.where(low_half, 0.0, query).astype(BF),
    ]
    lanes = 128
    pieces = length // lanes

    def score(c, tops):
        keys = key_pair(fac_ref, kv_s, c, pair, 0)[0].astype(BF)
        bias = bias_s[c]
        new = []
        for h in range(2):
            s = mm(queries[h], keys) * LOG2E + bias
            s_s[h, c] = s
            top = tops[h]
            for i in range(pieces):
                top = jnp.maximum(top, s[:, i * lanes : (i + 1) * lanes])
            new.append(top)
        return tuple(new)

    start = jnp.full((length, lanes), -1e30, F32)
    tops = lax.fori_loop(lo, me + 1, score, (start, start))
    tops = [jnp.max(top, axis=1, keepdims=True) for top in tops]

    def value(c, carry):
        values = key_pair(fac_ref, kv_s, c, pair, 1)[0].astype(BF)
        new = []
        for h in range(2):
            p = jnp.exp2(s_s[h, c] - tops[h])
            total = carry[2 * h]
            for i in range(pieces):
                total = total + p[:, i * lanes : (i + 1) * lanes]
            new += [total, carry[2 * h + 1] + mm(p.astype(BF), values, 1, 1)]
        return tuple(new)

    zero = jnp.zeros((length, lanes), F32)
    wide = jnp.zeros((length, 2 * HEAD_DIM), F32)
    done = lax.fori_loop(lo, me + 1, value, (zero, wide, zero, wide))
    outs = []
    for h in range(2):
        total = jnp.sum(done[2 * h], axis=1, keepdims=True)
        outs.append(done[2 * h + 1] / total)
        lse_ref[h] = jnp.broadcast_to(tops[h] + jnp.log2(total), (length, lanes))
    o_ref[...] = jnp.where(low_half, outs[0], outs[1]).astype(BF)


def full(shape):
    return pl.BlockSpec(shape, lambda p, s: (0,) * len(shape))


def attention_forward(scal, qfac, fac, start):
    n, unused, length = fac.shape
    return pl.pallas_call(
        forward_kernel,
        out_shape=(
            jax.ShapeDtypeStruct((length, HEADS * HEAD_DIM), BF),
            jax.ShapeDtypeStruct((HEADS, length, 128), F32),
        ),
        grid_spec=pltpu.PrefetchScalarGridSpec(
            num_scalar_prefetch=1,
            grid=(PAIRS,),
            in_specs=[full(qfac.shape), full(fac.shape), full(start.shape)],
            out_specs=[
                pl.BlockSpec((length, 2 * HEAD_DIM), lambda p, s: (0, p)),
                pl.BlockSpec((2, length, 128), lambda p, s: (p, 0, 0)),
            ],
            scratch_shapes=[
                pltpu.VMEM((QHW, length), F32),
                pltpu.VMEM((n, 2 * KHW, length), F32),
                pltpu.VMEM((n, length, length), F32),
                pltpu.VMEM((2, n, length, length), F32),
            ],
        ),
        compiler_params=pltpu.CompilerParams(
            dimension_semantics=("arbitrary",), vmem_limit_bytes=58 << 20
        ),
        name="attention_forward",
    )(scal, qfac, fac, start)


def backward_kernel(
    scal_ref,
    qfac_ref,
    fac_ref,
    start_ref,
    o_ref,
    do_ref,
    lse_ref,
    cos_ref,
    sin_ref,
    terms_ref,
    dq_ref,
    aq_s,
    kv_s,
    bias_s,
    acc_s,
    heads_s,
    dbq_s,
    daq_s,
):
    pair = pl.program_id(0)
    length = qfac_ref.shape[1]
    n = fac_ref.shape[0]
    lo, me = scal_ref[0], scal_ref[1]
    pieces = length // 128

    @pl.when(pair == 0)
    def _():
        fill_tables(scal_ref, qfac_ref, fac_ref, start_ref, aq_s, kv_s, bias_s)
        dbq_s[...] = jnp.zeros_like(dbq_s)

        def clear(c, carry):
            acc_s[c] = jnp.zeros((2 * KDW, length), F32)
            return carry

        lax.fori_loop(lo, me + 1, clear, 0)

    query_t = query_pair(qfac_ref, aq_s, pair).astype(F32) * (HEAD_DIM**-0.5)
    query = jnp.transpose(query_t)
    query_t = query_t.astype(BF)
    do = do_ref[...].astype(F32)
    do_t = jnp.transpose(do).astype(BF)
    low_half = lax.broadcasted_iota(jnp.int32, (length, 2 * HEAD_DIM), 1) < HEAD_DIM
    product = do * o_ref[...].astype(F32)
    queries, grads, deltas, stats = [], [], [], []
    for h in range(2):
        keep = low_half if h == 0 else jnp.logical_not(low_half)
        queries.append(jnp.where(keep, query, 0.0).astype(BF))
        grads.append(jnp.where(keep, do, 0.0).astype(BF))
        deltas.append(jnp.sum(jnp.where(keep, product, 0.0), axis=1, keepdims=True))
        stats.append(lse_ref[h])

    def step(c, dqs):
        keys, kb0, kb1, krows = key_pair(fac_ref, kv_s, c, pair, 0)
        values, vb0, vb1, vrows = key_pair(fac_ref, kv_s, c, pair, 1)
        keys, values = keys.astype(BF), values.astype(BF)
        bias = bias_s[c]
        new, sums, rows = [], [None] * 4, []
        for h in range(2):
            s = mm(queries[h], keys) * LOG2E + bias
            lse = jnp.concatenate([stats[h]] * pieces, axis=1)
            p = jnp.exp2(s - lse)
            dp = mm(grads[h], values)
            ds = (p * (dp - deltas[h])).astype(BF)
            pb = p.astype(BF)
            new.append(dqs[h] + mm(ds, keys, 1, 1))
            half = slice(h * HEAD_DIM, (h + 1) * HEAD_DIM)
            dk = mm(query_t[half, :], ds)
            dv = mm(do_t[half, :], pb)
            for which, d, b0, b1, a in ((0, dk, kb0, kb1, krows), (1, dv, vb0, vb1, vrows)):
                for r, b in ((0, b0), (1, b1)):
                    term = d * a[2 * h + r]
                    k = 2 * which + r
                    sums[k] = term if sums[k] is None else sums[k] + term
                    rows.append((which * 4 + 2 * h + r, jnp.sum(d * b, axis=0, keepdims=True)))
        for k in range(4):
            part = slice(k * HEAD_DIM, (k + 1) * HEAD_DIM)
            acc_s[c, part, :] = acc_s[c, part, :] + sums[k]
        for k, row in rows:
            where = (k // 4) * KHW + pair * 4 + k % 4
            heads_s[c, pl.ds(where, 1), :] = row
        return tuple(new)

    zero = jnp.zeros((length, 2 * HEAD_DIM), F32)
    dqs = lax.fori_loop(lo, me + 1, step, (zero, zero))
    dq_t = jnp.transpose(jnp.where(low_half, dqs[0], dqs[1])) * (HEAD_DIM**-0.5 / QRANK)
    for h in range(2):
        d = dq_t[h * HEAD_DIM : (h + 1) * HEAD_DIM, :]
        for r in range(QRANK):
            part = slice(r * HEAD_DIM, (r + 1) * HEAD_DIM)
            b = qfac_ref[QHW + r * HEAD_DIM : QHW + (r + 1) * HEAD_DIM, :].astype(F32)
            k = pl.ds(pair * (2 * QRANK) + h * QRANK + r, 1)
            daq_s[k, :] = jnp.sum(d * b, axis=0, keepdims=True)
            dbq_s[part, :] = dbq_s[part, :] + d * aq_s[k, :]

    @pl.when(pair == PAIRS - 1)
    def _():
        cosine, sine = cos_ref[...], sin_ref[...]
        half = HEAD_DIM // 2
        dq_ref[0:QHW, :] = daq_s[...].astype(BF)
        for r in range(QRANK):
            first = dbq_s[r * HEAD_DIM : r * HEAD_DIM + half, :]
            second = dbq_s[r * HEAD_DIM + half : (r + 1) * HEAD_DIM, :]
            turned = jnp.concatenate(
                [first * cosine + second * sine, second * cosine - first * sine], axis=0
            )
            dq_ref[QHW + r * HEAD_DIM : QHW + (r + 1) * HEAD_DIM, :] = turned.astype(BF)

        def flush(c, carry):
            inside = (c >= lo) & (c <= me)

            @pl.when(inside)
            def _():
                terms_ref[c, 0 : 2 * KDW, :] = (acc_s[c] * (1.0 / KRANK)).astype(BF)
                terms_ref[c, 2 * KDW :, :] = (heads_s[c] * (1.0 / KRANK)).astype(BF)

            @pl.when(jnp.logical_not(inside))
            def _():
                terms_ref[c] = jnp.zeros((FACW, length), BF)

            return carry

        lax.fori_loop(0, n, flush, 0)


def attention_backward(scal, qfac, fac, start, o, do, lse, cosine, sine):
    n, unused, length = fac.shape
    return pl.pallas_call(
        backward_kernel,
        out_shape=(
            jax.ShapeDtypeStruct((n, FACW, length), BF),
            jax.ShapeDtypeStruct((QFW, length), BF),
        ),
        grid_spec=pltpu.PrefetchScalarGridSpec(
            num_scalar_prefetch=1,
            grid=(PAIRS,),
            in_specs=[
                full(qfac.shape),
                full(fac.shape),
                full(start.shape),
                pl.BlockSpec((length, 2 * HEAD_DIM), lambda p, s: (0, p)),
                pl.BlockSpec((length, 2 * HEAD_DIM), lambda p, s: (0, p)),
                pl.BlockSpec((2, length, 128), lambda p, s: (p, 0, 0)),
                full(cosine.shape),
                full(sine.shape),
            ],
            out_specs=[full((n, FACW, length)), full((QFW, length))],
            scratch_shapes=[
                pltpu.VMEM((QHW, length), F32),
                pltpu.VMEM((n, 2 * KHW, length), F32),
                pltpu.VMEM((n, length, length), F32),
                pltpu.VMEM((n, 2 * KDW, length), F32),
                pltpu.VMEM((n, 2 * KHW, length), F32),
                pltpu.VMEM((QDW, length), F32),
                pltpu.VMEM((QHW, length), F32),
            ],
        ),
        compiler_params=pltpu.CompilerParams(
            dimension_semantics=("arbitrary",), vmem_limit_bytes=58 << 20
        ),
        name="attention_backward",
    )(scal, qfac, fac, start, o, do, lse, cosine, sine)


def norm_of(values):
    inverse = lax.rsqrt(jnp.mean(values * values, axis=-1, keepdims=True) + EPS)
    return values * inverse, inverse


def turn(values, cosine, sine, sign):
    half = HEAD_DIM // 2
    parts = []
    for r in range(values.shape[0] // HEAD_DIM):
        first = values[r * HEAD_DIM : r * HEAD_DIM + half, :]
        second = values[r * HEAD_DIM + half : (r + 1) * HEAD_DIM, :]
        parts.append(first * cosine - sign * second * sine)
        parts.append(second * cosine + sign * first * sine)
    return jnp.concatenate(parts, axis=0)


def enter_kernel(x_ref, gain_ref, qh, qd, kh, kd, vh, vd, cos_ref, sin_ref, xa_ref, qfac_ref, fac_ref):
    normed = norm_of(x_ref[...].astype(F32))[0]
    xa = (normed * gain_ref[...]).astype(BF)
    xa_ref[...] = xa
    cosine, sine = cos_ref[...], sin_ref[...]
    kdims = turn(jnp.transpose(mm(xa, kd[...])), cosine, sine, 1.0)
    fac_ref[0:KDW, :] = kdims.astype(BF)
    fac_ref[KDW : 2 * KDW, :] = jnp.transpose(mm(xa, vd[...])).astype(BF)
    fac_ref[2 * KDW : 2 * KDW + KHW, :] = jnp.transpose(mm(xa, kh[...])).astype(BF)
    fac_ref[2 * KDW + KHW :, :] = jnp.transpose(mm(xa, vh[...])).astype(BF)
    qfac_ref[0:QHW, :] = jnp.transpose(mm(xa, qh[...])).astype(BF)
    qdims = turn(jnp.transpose(mm(xa, qd[...])), cosine, sine, 1.0)
    qfac_ref[QHW:, :] = qdims.astype(BF)


def enter(x, gain, weights, cosine, sine):
    length, width = x.shape
    return pl.pallas_call(
        enter_kernel,
        out_shape=(
            jax.ShapeDtypeStruct((length, width), BF),
            jax.ShapeDtypeStruct((QFW, length), BF),
            jax.ShapeDtypeStruct((FACW, length), BF),
        ),
        compiler_params=pltpu.CompilerParams(vmem_limit_bytes=40 << 20),
        name="enter",
    )(x, gain, *weights, cosine, sine)


def leave_query_kernel(xa_ref, dq_ref, fgain_ref, out_ref):
    xa_t = jnp.transpose(xa_ref[...].astype(F32)).astype(BF)
    d = dq_ref[...].astype(F32)
    out_ref[:, 0:QHW] = mm(xa_t, d[0:QHW, :].astype(BF), 1, 1).astype(BF)
    out_ref[:, QHW:QFW] = mm(xa_t, d[QHW:, :].astype(BF), 1, 1).astype(BF)
    out_ref[:, QFW:] = jnp.transpose(jnp.concatenate([fgain_ref[...]] * (512 - QFW), axis=0)).astype(BF)


def leave_key_kernel(
    x_ref, xa_ref, gain_ref, dres_ref, dq_ref, kg_ref, cos_ref, sin_ref, qh, qd, kh, kd, vh, vd, tg_ref, out_ref
):
    normed, inverse = norm_of(x_ref[...].astype(F32))
    g = kg_ref[...]
    dkd = turn(g[0:KDW, :], cos_ref[...], sin_ref[...], -1.0)
    d_kd = jnp.transpose(dkd).astype(BF)
    d_vd = jnp.transpose(g[KDW : 2 * KDW, :]).astype(BF)
    d_kh = jnp.transpose(g[2 * KDW : 2 * KDW + KHW, :]).astype(BF)
    d_vh = jnp.transpose(g[2 * KDW + KHW :, :]).astype(BF)
    dq = dq_ref[...].astype(F32)
    d_qh = jnp.transpose(dq[0:QHW, :]).astype(BF)
    d_qd = jnp.transpose(dq[QHW:, :]).astype(BF)
    xa_t = jnp.transpose(xa_ref[...].astype(F32)).astype(BF)
    dxa = mm(d_qd, qd[...], 1, 1) + mm(d_qh, qh[...], 1, 1)
    dxa = dxa + mm(d_kd, kd[...], 1, 1) + mm(d_vd, vd[...], 1, 1)
    dxa = dxa + mm(d_kh, kh[...], 1, 1) + mm(d_vh, vh[...], 1, 1)
    scaled = dxa * gain_ref[...]
    product = dxa * normed
    mean = jnp.mean(scaled * normed, axis=-1, keepdims=True)
    tg_ref[...] = (dres_ref[...] + inverse * (scaled - normed * mean)).astype(BF)
    gain_part = jnp.sum(product, axis=0, keepdims=True)
    out_ref[:, 0:KDW] = mm(xa_t, d_kd).astype(BF)
    out_ref[:, KDW : 2 * KDW] = mm(xa_t, d_vd).astype(BF)
    out_ref[:, 2 * KDW : 2 * KDW + KHW] = mm(xa_t, d_kh).astype(BF)
    out_ref[:, 2 * KDW + KHW : FACW] = mm(xa_t, d_vh).astype(BF)
    out_ref[:, FACW:] = jnp.transpose(jnp.concatenate([gain_part] * (384 - FACW), axis=0)).astype(BF)


def leave_query(xa, dq, fgain):
    width = xa.shape[1]
    return pl.pallas_call(
        leave_query_kernel,
        out_shape=jax.ShapeDtypeStruct((width, 512), BF),
        compiler_params=pltpu.CompilerParams(vmem_limit_bytes=40 << 20),
        name="leave_query",
    )(xa, dq, fgain)


def leave_key(x, xa, gain, dres, dq, kg, cosine, sine, weights):
    length, width = x.shape
    return pl.pallas_call(
        leave_key_kernel,
        out_shape=(
            jax.ShapeDtypeStruct((length, width), BF),
            jax.ShapeDtypeStruct((width, 384), BF),
        ),
        compiler_params=pltpu.CompilerParams(vmem_limit_bytes=40 << 20),
        name="leave_key",
    )(x, xa, gain, dres, dq, kg, cosine, sine, *weights)


class Grid:
    def __init__(self, dp, tensor):
        self.c = 2 if dp % 2 == 0 else 1
        self.y = dp // self.c
        self.x = self.y if tensor % self.y == 0 else 1
        self.z = tensor // self.x
        self.dp, self.tensor = dp, tensor
        self.axes = {
            "c": ("dp", 1, self.c),
            "y": ("dp", self.c, self.y),
            "x": ("tensor", 1, self.x),
            "z": ("tensor", self.x, self.z),
        }

    def size(self, g):
        return self.axes[g][2]

    def place(self, g):
        axis, stride, size = self.axes[g]
        return (lax.axis_index(axis) // stride) % size

    def swap(self, v, g, r):
        axis, stride, size = self.axes[g]
        total = self.dp if axis == "dp" else self.tensor
        return lax.ppermute(v, axis, [(i, i ^ (r * stride)) for i in range(total)])

    def scatter_sum(self, v, g, last=BF):
        size = self.size(g)
        if size == 1:
            return v.astype(last)
        me = self.place(g)
        rows = v.shape[0] // size
        got = []
        for r in range(1, size):
            got.append(self.swap(lax.dynamic_slice_in_dim(v, (me ^ r) * rows, rows, 0), g, r))
        total = lax.dynamic_slice_in_dim(v, me * rows, rows, 0).astype(F32)
        for piece in got:
            total = total + piece.astype(F32)
        return total.astype(last)

    def gather(self, v, g):
        size = self.size(g)
        if size == 1:
            return v
        me = self.place(g)
        rows = v.shape[0]
        got = [v] + [self.swap(v, g, r) for r in range(1, size)]
        if size == 2:
            return jnp.concatenate(
                [jnp.where(me == 0, got[0], got[1]), jnp.where(me == 0, got[1], got[0])], axis=0
            )
        out = jnp.zeros((rows * size,) + v.shape[1:], v.dtype)
        for r in range(size):
            out = lax.dynamic_update_slice_in_dim(out, got[r], (me ^ r) * rows, 0)
        return out

    def sum_all(self, v, order):
        for g in order:
            v = self.scatter_sum(v, g)
        for g in reversed(order):
            v = self.gather(v, g)
        return v


def pad_lanes(width):
    return -(-width // 128) * 128


def pack_kernel(scal_ref, gate_ref, up_ref, down_ref, out_ref):
    width = gate_ref.shape[1]
    rows, padded = out_ref.shape[2:]
    down = jnp.transpose(down_ref[...].astype(F32)).astype(BF)
    for k, piece in enumerate((gate_ref[...], up_ref[...], down)):
        out_ref[0, k, :, 0:width] = piece
        if padded > width:
            out_ref[0, k, :, width:padded] = jnp.zeros((rows, padded - width), BF)


def pack(mine, gate, up, down, parts):
    depth, width = gate.shape
    rows = depth // parts
    return pl.pallas_call(
        pack_kernel,
        out_shape=jax.ShapeDtypeStruct((parts, 3, rows, pad_lanes(width)), BF),
        grid_spec=pltpu.PrefetchScalarGridSpec(
            num_scalar_prefetch=1,
            grid=(parts,),
            in_specs=[
                pl.BlockSpec((rows, width), lambda q, s: (s[0] ^ q, 0)),
                pl.BlockSpec((rows, width), lambda q, s: (s[0] ^ q, 0)),
                pl.BlockSpec((width, rows), lambda q, s: (0, s[0] ^ q)),
            ],
            out_specs=pl.BlockSpec((1, 3, rows, pad_lanes(width)), lambda q, s: (q, 0, 0, 0)),
        ),
        compiler_params=pltpu.CompilerParams(dimension_semantics=("arbitrary",)),
        name="pack",
    )(mine, gate, up, down)


def ffn_kernel(parts, pieces, scal_ref, xf_ref, dy_ref, *refs):
    own_ref, others = refs[0], refs[1 : 1 + pieces]
    mixed_ref, dxf_ref, inner_ref, dgate_ref, dup_ref, w_s, sem = refs[1 + pieces :]
    rows, padded = own_ref.shape[2:]
    zs = 1 + pieces // parts
    copies = []
    for r in range(zs):
        for q in range(parts):
            source = own_ref.at[q] if r == 0 else others[(r - 1) * parts + q]
            place = pl.multiple_of((scal_ref[0] ^ q) * rows, rows)
            target = w_s.at[:, pl.ds(place, rows), pl.ds(r * padded, padded)]
            copies.append(pltpu.make_async_copy(source, target, sem.at[r * parts + q]))
    for copy in copies:
        copy.start()
    for copy in copies:
        copy.wait()
    group = 2 if zs % 2 == 0 else 1
    xf, dy = xf_ref[...], dy_ref[...]
    for g in range(zs // group):
        span = slice(g * group * padded, (g + 1) * group * padded)
        wg, wu, wd = w_s[0, :, span], w_s[1, :, span], w_s[2, :, span]
        gate = mm(xf, wg)
        up = mm(xf, wu)
        d_inner = mm(dy, wd)
        sig = 1.0 / (1.0 + jnp.exp(-gate))
        act = gate * sig
        inner = (act * up).astype(BF)
        d_gate = (d_inner * up * sig * (1.0 + gate * (1.0 - sig))).astype(BF)
        d_up = (d_inner * act).astype(BF)
        inner_ref[:, span] = inner
        dgate_ref[:, span] = d_gate
        dup_ref[:, span] = d_up
        dxf = mm(d_gate, wg, 1, 1) + mm(d_up, wu, 1, 1)
        mixed = mm(inner, wd, 1, 1)
        if g == 0:
            dxf_ref[...] = dxf.astype(dxf_ref.dtype)
            mixed_ref[...] = mixed.astype(mixed_ref.dtype)
        else:
            dxf_ref[...] = dxf_ref[...] + dxf
            mixed_ref[...] = mixed_ref[...] + mixed


def ffn(mine, xf, dy, own, others, name):
    length, depth = xf.shape
    parts, unused, rows, padded = own.shape
    zs = 1 + len(others) // parts
    hidden = zs * padded
    whole = pl.BlockSpec(memory_space=pltpu.VMEM)
    raw = pl.BlockSpec(memory_space=pl.ANY)
    return pl.pallas_call(
        functools.partial(ffn_kernel, parts, len(others)),
        out_shape=(jax.ShapeDtypeStruct((length, depth), F32),) * 2
        + (jax.ShapeDtypeStruct((length, hidden), BF),) * 3,
        in_specs=[pl.BlockSpec(memory_space=pltpu.SMEM), whole, whole] + [raw] * (1 + len(others)),
        out_specs=[whole] * 5,
        scratch_shapes=[
            pltpu.VMEM((3, depth, hidden), BF),
            pltpu.SemaphoreType.DMA((zs * parts,)),
        ],
        compiler_params=pltpu.CompilerParams(vmem_limit_bytes=58 << 20),
        name=name,
    )(mine, xf, dy, own, *others)


def weight_kernel(blocks, zs, scal_ref, *refs):
    xfs, dys = refs[:blocks], refs[blocks : 2 * blocks]
    inner, dgate, dup = (refs[(2 + k) * blocks : (3 + k) * blocks] for k in range(3))
    outs = refs[5 * blocks :]
    padded = outs[0].shape[3]
    second = pl.program_id(1)
    xf_t = [jnp.transpose(ref[...].astype(F32)).astype(BF) for ref in xfs]
    dy_t = [jnp.transpose(ref[...].astype(F32)).astype(BF) for ref in dys]
    for k, (left, right) in enumerate(((xf_t, dgate), (xf_t, dup), (dy_t, inner))):
        total = None
        for b in range(blocks):
            term = mm(left[b], right[b][...])
            total = term if total is None else total + term
        total = total.astype(BF)
        for side in range(2):

            @pl.when(second == side)
            def _(side=side, k=k, total=total):
                for r in range(zs):
                    outs[2 * k + side][0, r] = total[:, r * padded : (r + 1) * padded]


def weight_grads(mine, xfs, dys, inner, dgate, dup, parts, zs):
    length, depth = xfs[0].shape
    hidden = inner[0].shape[1]
    padded = hidden // zs
    rows = depth // parts
    blocks = len(xfs)
    column = pl.BlockSpec((length, rows), lambda i, k, s: (0, s[0] ^ (2 * i + k)))
    whole = pl.BlockSpec((length, hidden), lambda i, k, s: (0, 0))
    return pl.pallas_call(
        functools.partial(weight_kernel, blocks, zs),
        out_shape=(jax.ShapeDtypeStruct((parts // 2, zs, rows, padded), BF),) * 6,
        grid_spec=pltpu.PrefetchScalarGridSpec(
            num_scalar_prefetch=1,
            grid=(parts // 2, 2),
            in_specs=[column] * (2 * blocks) + [whole] * (3 * blocks),
            out_specs=[pl.BlockSpec((1, zs, rows, padded), lambda i, k, s: (i, 0, 0, 0))] * 6,
        ),
        compiler_params=pltpu.CompilerParams(
            dimension_semantics=("arbitrary", "arbitrary"), vmem_limit_bytes=58 << 20
        ),
        name="weight_grads",
    )(mine, *xfs, *dys, *inner, *dgate, *dup)


def unpack_kernel(scal_ref, *refs):
    g, u, d = (ref[...].astype(F32) for ref in refs[:3])
    gate_ref, up_ref, down_ref = refs[3:]
    width = gate_ref.shape[1]
    gate_ref[...] = g[0, :, 0:width]
    up_ref[...] = u[0, :, 0:width]
    down_ref[...] = jnp.transpose(d[0])[0:width, :]


def unpack(mine, grads, width):
    parts, rows, padded = grads[0].shape
    block = pl.BlockSpec((1, rows, padded), lambda q, s: (q, 0, 0))
    return pl.pallas_call(
        unpack_kernel,
        out_shape=(
            jax.ShapeDtypeStruct((parts * rows, width), F32),
            jax.ShapeDtypeStruct((parts * rows, width), F32),
            jax.ShapeDtypeStruct((width, parts * rows), F32),
        ),
        grid_spec=pltpu.PrefetchScalarGridSpec(
            num_scalar_prefetch=1,
            grid=(parts,),
            in_specs=[block] * 3,
            out_specs=[
                pl.BlockSpec((rows, width), lambda q, s: (s[0] ^ q, 0)),
                pl.BlockSpec((rows, width), lambda q, s: (s[0] ^ q, 0)),
                pl.BlockSpec((width, rows), lambda q, s: (0, s[0] ^ q)),
            ],
        ),
        compiler_params=pltpu.CompilerParams(dimension_semantics=("arbitrary",)),
        name="unpack",
    )(mine, *grads)


def spread_weights(grid, own):
    pieces = []
    for r in range(1, grid.z):
        first = grid.swap(own[0], "z", r)
        column = [first] + [grid.swap(first, "y", k) for k in range(1, grid.y)]
        for piece in column:
            pieces += [piece] + [grid.swap(piece, "c", k) for k in range(1, grid.c)]
    return pieces


def reduce_weight(grid, even, odd):
    held = even.astype(F32) + grid.swap(odd, "c", 1).astype(F32)
    total = held[0]
    for k in range(1, grid.y):
        total = total + grid.swap(held[k].astype(BF), "y", k).astype(F32)
    mine = total[0]
    for r in range(1, grid.z):
        mine = mine + grid.swap(total[r].astype(BF), "z", r).astype(F32)
    mine = mine.astype(BF)
    column = [mine] + [grid.swap(mine, "y", k) for k in range(1, grid.y)]
    pieces = []
    for piece in column:
        pieces += [piece, grid.swap(piece, "c", 1)]
    return jnp.stack(pieces)


def contract(left, right, left_dim, right_dim):
    return lax.dot_general(
        left, right, (((left_dim,), (right_dim,)), ((), ())), preferred_element_type=jnp.float32
    )


def norm_back(grad_out, normed, inverse, gain):
    scaled = grad_out * gain
    gain_part = jnp.sum(grad_out * normed, axis=0)
    grad_in = inverse * (scaled - normed * jnp.mean(scaled * normed, axis=-1, keepdims=True))
    return (grad_in, gain_part)


def body(
    grid,
    tokens,
    cotangent,
    segments,
    positions,
    attngain,
    ffngain,
    queryheads,
    querydims,
    keyheads,
    keydims,
    valueheads,
    valuedims,
    outproj,
    gateproj,
    upproj,
    downproj,
):
    x = tokens[0]
    upstream = cotangent[0]
    length = x.shape[0]
    me = lax.axis_index("tensor")
    offset = me * length
    places = lax.dynamic_slice_in_dim(positions[0], offset, length)
    half = HEAD_DIM // 2
    freqs = 10000.0 ** (-jnp.arange(half, dtype=F32) * 2.0 / HEAD_DIM)
    angles = freqs[:, None] * places.astype(F32)[None, :]
    cosine, sine = jnp.cos(angles), jnp.sin(angles)
    start = (offset + jnp.arange(length, dtype=jnp.int32) - places)[:, None]
    scal = jnp.stack([jnp.maximum(offset - places[0], 0) // length, me]).astype(jnp.int32)
    weights = (queryheads, querydims, keyheads, keydims, valueheads, valuedims)
    spot = lax.axis_index("dp").astype(jnp.int32)[None]
    own = pack(spot, gateproj, upproj, downproj, grid.dp)
    others = spread_weights(grid, own)
    dys = [upstream] + [grid.swap(upstream, "x", r) for r in range(1, grid.x)]
    xa, qfac, fac = enter(x, attngain[None, :], weights, cosine, sine)

    fac_z = grid.gather(fac[None, None], "z")
    fac_x = [fac_z] + [grid.swap(fac_z, "x", r) for r in range(1, grid.x)]
    mine = grid.place("x")
    facs = jnp.zeros((grid.z, grid.x) + fac.shape, BF)
    for r in range(grid.x):
        facs = lax.dynamic_update_slice_in_dim(facs, fac_x[r], mine ^ r, 1)
    facs = facs.reshape((grid.tensor,) + fac.shape)

    attn_out, lse = attention_forward(scal, qfac, facs, start)

    local = x.astype(F32)
    residual = local + jnp.dot(attn_out, outproj, preferred_element_type=jnp.float32)
    inverse_two = lax.rsqrt(jnp.mean(residual * residual, axis=-1, keepdims=True) + EPS)
    normed_two = residual * inverse_two
    input_two = (normed_two * ffngain).astype(jnp.bfloat16)
    xfs = [input_two] + [grid.swap(input_two, "x", r) for r in range(1, grid.x)]
    results = [
        ffn(spot, xfs[k], dys[k], own, others, "ffn_" + str(k)) for k in range(grid.x)
    ]
    d_norm_two, ffn_out = results[0][1], results[0][0]
    for r in range(1, grid.x):
        d_norm_two = d_norm_two + grid.swap(results[r][1].astype(BF), "x", r).astype(F32)
        ffn_out = ffn_out + grid.swap(results[r][0].astype(BF), "x", r).astype(F32)
    partial = weight_grads(
        spot,
        xfs,
        dys,
        [v[2] for v in results],
        [v[3] for v in results],
        [v[4] for v in results],
        grid.dp,
        grid.z,
    )
    reduced = [reduce_weight(grid, partial[2 * k], partial[2 * k + 1]) for k in range(3)]
    gate_part, up_part, down_part = unpack(spot, reduced, gateproj.shape[1])
    mixed = (residual + ffn_out).astype(jnp.bfloat16)
    grad_through, ffngain_part = norm_back(d_norm_two, normed_two, inverse_two, ffngain)
    d_residual = upstream.astype(jnp.float32) + grad_through
    d_res_low = d_residual.astype(jnp.bfloat16)
    outproj_part = contract(attn_out, d_res_low, 0, 0).astype(BF)
    d_attended = contract(d_res_low, outproj, 1, 1).astype(jnp.bfloat16)

    terms, dq = attention_backward(
        scal, qfac, facs, start, attn_out, d_attended, lse, cosine, sine
    )
    terms = terms.reshape((grid.z, grid.x) + fac.shape)
    near = lax.dynamic_slice_in_dim(terms, mine, 1, 1).astype(F32)
    for r in range(1, grid.x):
        near = near + grid.swap(lax.dynamic_slice_in_dim(terms, mine ^ r, 1, 1), "x", r).astype(F32)
    key_grads = grid.scatter_sum(near[:, 0].astype(BF), "z", F32)[0]

    query_part = leave_query(xa, dq, ffngain_part[None, :])
    tokens_grad, key_part = leave_key(
        x, xa, attngain[None, :], d_residual, dq, key_grads, cosine, sine, weights
    )
    order = ("c", "x", "y", "z")
    outproj_sum = grid.sum_all(outproj_part, order).astype(F32)
    query_sum = grid.sum_all(query_part, order).astype(F32)
    key_sum = grid.sum_all(key_part, order).astype(F32)
    return (
        mixed[None],
        tokens_grad[None],
        key_sum[:, FACW],
        query_sum[:, QFW],
        query_sum[:, :QHW],
        query_sum[:, QHW:QFW],
        key_sum[:, 2 * KDW : 2 * KDW + KHW],
        key_sum[:, :KDW],
        key_sum[:, 2 * KDW + KHW : FACW],
        key_sum[:, KDW : 2 * KDW],
        outproj_sum,
        gate_part,
        up_part,
        down_part,
    )


def solution(mesh):
    grid = Grid(mesh.shape["dp"], mesh.shape["tensor"])
    rows = P("dp", "tensor", None)
    placed = (rows, rows, P("dp", None), P("dp", None)) + (P(),) * 9
    halves = (P(None, "tensor"), P(None, "tensor"), P("tensor", None))
    return jax.shard_map(
        functools.partial(body, grid),
        mesh=mesh,
        in_specs=placed + halves,
        out_specs=(rows, rows) + (P(),) * 9 + halves,
        check_vma=False,
    )
```

```python
import functools
import math

import jax
import jax.numpy as jnp
from jax import lax
from jax.experimental import pallas as pl
from jax.experimental.pallas import tpu as pltpu

from jax.sharding import PartitionSpec as P

HEADS = 16
HEAD_DIM = 64
QRANK = 6
KRANK = 2
PAIRS = HEADS // 2
QHW = HEADS * QRANK
QDW = QRANK * HEAD_DIM
KDW = KRANK * HEAD_DIM
KHW = HEADS * KRANK
FACW = 2 * KDW + 2 * KHW
QFW = QHW + QDW
LOG2E = 1.4426950408889634
EPS = 1e-06
BF = jnp.bfloat16
F32 = jnp.float32


def mm(a, b, ca=1, cb=0):
    return lax.dot_general(a, b, (((ca,), (cb,)), ((), ())), preferred_element_type=F32)


def expand_pair(bk0, bk1, rows):
    first = rows[0] * bk0 + rows[1] * bk1
    second = rows[2] * bk0 + rows[3] * bk1
    return jnp.concatenate([first, second], axis=0) * (1.0 / KRANK)


def query_pair(qfac_ref, aq_s, pair):
    halves = []
    for h in range(2):
        acc = None
        for r in range(QRANK):
            row = aq_s[pl.ds(pair * (2 * QRANK) + h * QRANK + r, 1), :]
            term = row * qfac_ref[QHW + r * HEAD_DIM : QHW + (r + 1) * HEAD_DIM, :].astype(F32)
            acc = term if acc is None else acc + term
        halves.append(acc * (1.0 / QRANK))
    return jnp.concatenate(halves, axis=0).astype(BF)


def reverse_bits(r, size):
    total, bits = 0, size.bit_length() - 1
    for k in range(bits):
        total = total + (((r >> k) & 1) << (bits - 1 - k))
    return total


def fill_tables(scal_ref, qfac_ref, fac_refs, start_ref, fac_s, aq_s, kv_s, bias_s):
    length = qfac_ref.shape[1]
    me = scal_ref[1]
    across = len(fac_refs)
    aq_s[...] = qfac_ref[0:QHW, :].astype(F32)
    row = lax.broadcasted_iota(jnp.int32, (length, length), 0) + me * length
    column = lax.broadcasted_iota(jnp.int32, (length, length), 1)
    begin = start_ref[...]

    def fill(c, carry):
        for k, ref in enumerate(fac_refs):

            @pl.when(((c ^ me) % across) == k)
            def _(ref=ref):
                piece = ref[reverse_bits((c ^ me) // across, ref.shape[0])]
                fac_s[c] = piece[0 : 2 * KDW, :]
                kv_s[c] = piece[2 * KDW :, :].astype(F32)

        key = column + c * length
        keep = (key >= begin) & (key <= row)
        bias_s[c] = jnp.where(keep, 0.0, -1e30)
        return carry

    lax.fori_loop(scal_ref[0], me + 1, fill, 0)


def key_pair(fac_ref, kv_s, c, pair, which):
    base = which * KDW
    b0 = fac_ref[c, base : base + HEAD_DIM, :].astype(F32)
    b1 = fac_ref[c, base + HEAD_DIM : base + 2 * HEAD_DIM, :].astype(F32)
    rows = [kv_s[c, pl.ds(which * KHW + pair * 4 + j, 1), :] for j in range(4)]
    return expand_pair(b0, b1, rows), b0, b1, rows


def forward_kernel(across, scal_ref, qfac_ref, *refs):
    fac_refs, start_ref = refs[:across], refs[across]
    o_ref, lse_ref, fac_ref, aq_s, kv_s, bias_s, s_s = refs[across + 1 :]
    pair = pl.program_id(0)
    length = qfac_ref.shape[1]
    lo, me = scal_ref[0], scal_ref[1]

    @pl.when(pair == 0)
    def _():
        fill_tables(scal_ref, qfac_ref, fac_refs, start_ref, fac_ref, aq_s, kv_s, bias_s)

    query = jnp.transpose(query_pair(qfac_ref, aq_s, pair).astype(F32)) * (HEAD_DIM**-0.5)
    low_half = lax.broadcasted_iota(jnp.int32, (length, 2 * HEAD_DIM), 1) < HEAD_DIM
    queries = [
        jnp.where(low_half, query, 0.0).astype(BF),
        jnp.where(low_half, 0.0, query).astype(BF),
    ]
    lanes = 128
    pieces = length // lanes

    def score(c, tops):
        keys = key_pair(fac_ref, kv_s, c, pair, 0)[0].astype(BF)
        bias = bias_s[c]
        new = []
        for h in range(2):
            s = mm(queries[h], keys) * LOG2E + bias
            s_s[h, c] = s
            top = tops[h]
            for i in range(pieces):
                top = jnp.maximum(top, s[:, i * lanes : (i + 1) * lanes])
            new.append(top)
        return tuple(new)

    start = jnp.full((length, lanes), -1e30, F32)
    tops = lax.fori_loop(lo, me + 1, score, (start, start))
    tops = [jnp.max(top, axis=1, keepdims=True) for top in tops]

    def value(c, carry):
        values = key_pair(fac_ref, kv_s, c, pair, 1)[0].astype(BF)
        new = []
        for h in range(2):
            p = jnp.exp2(s_s[h, c] - tops[h])
            total = carry[2 * h]
            for i in range(pieces):
                total = total + p[:, i * lanes : (i + 1) * lanes]
            new += [total, carry[2 * h + 1] + mm(p.astype(BF), values, 1, 1)]
        return tuple(new)

    zero = jnp.zeros((length, lanes), F32)
    wide = jnp.zeros((length, 2 * HEAD_DIM), F32)
    done = lax.fori_loop(lo, me + 1, value, (zero, wide, zero, wide))
    outs = []
    for h in range(2):
        total = jnp.sum(done[2 * h], axis=1, keepdims=True)
        outs.append(done[2 * h + 1] / total)
        lse_ref[h] = jnp.broadcast_to(tops[h] + jnp.log2(total), (length, lanes))
    o_ref[...] = jnp.where(low_half, outs[0], outs[1]).astype(BF)


def full(shape):
    return pl.BlockSpec(shape, lambda p, s: (0,) * len(shape))


def attention_forward(scal, qfac, facs, start):
    length = qfac.shape[1]
    n = facs[0].shape[0] * len(facs)
    return pl.pallas_call(
        functools.partial(forward_kernel, len(facs)),
        out_shape=(
            jax.ShapeDtypeStruct((length, HEADS * HEAD_DIM), BF),
            jax.ShapeDtypeStruct((HEADS, length, 128), F32),
        ),
        grid_spec=pltpu.PrefetchScalarGridSpec(
            num_scalar_prefetch=1,
            grid=(PAIRS,),
            in_specs=[full(qfac.shape)] + [full(v.shape) for v in facs] + [full(start.shape)],
            out_specs=[
                pl.BlockSpec((length, 2 * HEAD_DIM), lambda p, s: (0, p)),
                pl.BlockSpec((2, length, 128), lambda p, s: (p, 0, 0)),
            ],
            scratch_shapes=[
                pltpu.VMEM((n, 2 * KDW, length), BF),
                pltpu.VMEM((QHW, length), F32),
                pltpu.VMEM((n, 2 * KHW, length), F32),
                pltpu.VMEM((n, length, length), F32),
                pltpu.VMEM((2, n, length, length), F32),
            ],
        ),
        compiler_params=pltpu.CompilerParams(
            dimension_semantics=("arbitrary",), vmem_limit_bytes=58 << 20
        ),
        cost_estimate=SMALL,
        name="attention_forward",
    )(scal, qfac, *facs, start)


def backward_kernel(across, scal_ref, qfac_ref, *refs):
    fac_refs = refs[:across]
    start_ref, o_ref, do_ref, lse_ref, cos_ref, sin_ref = refs[across : across + 6]
    terms_refs = refs[across + 6 : 2 * across + 6]
    dq_ref, fac_ref, aq_s, kv_s, bias_s, acc_s, heads_s, dbq_s, daq_s = refs[2 * across + 6 :]
    pair = pl.program_id(0)
    length = qfac_ref.shape[1]
    n = fac_ref.shape[0]
    lo, me = scal_ref[0], scal_ref[1]
    pieces = length // 128

    @pl.when(pair == 0)
    def _():
        fill_tables(scal_ref, qfac_ref, fac_refs, start_ref, fac_ref, aq_s, kv_s, bias_s)
        dbq_s[...] = jnp.zeros_like(dbq_s)

        def clear(c, carry):
            acc_s[c] = jnp.zeros((2 * KDW, length), F32)
            return carry

        lax.fori_loop(lo, me + 1, clear, 0)

    query_t = query_pair(qfac_ref, aq_s, pair).astype(F32) * (HEAD_DIM**-0.5)
    query = jnp.transpose(query_t)
    query_t = query_t.astype(BF)
    do = do_ref[...].astype(F32)
    do_t = jnp.transpose(do).astype(BF)
    low_half = lax.broadcasted_iota(jnp.int32, (length, 2 * HEAD_DIM), 1) < HEAD_DIM
    product = do * o_ref[...].astype(F32)
    queries, grads, deltas, stats = [], [], [], []
    for h in range(2):
        keep = low_half if h == 0 else jnp.logical_not(low_half)
        queries.append(jnp.where(keep, query, 0.0).astype(BF))
        grads.append(jnp.where(keep, do, 0.0).astype(BF))
        deltas.append(jnp.sum(jnp.where(keep, product, 0.0), axis=1, keepdims=True))
        stats.append(lse_ref[h])

    def step(c, dqs):
        keys, kb0, kb1, krows = key_pair(fac_ref, kv_s, c, pair, 0)
        values, vb0, vb1, vrows = key_pair(fac_ref, kv_s, c, pair, 1)
        keys, values = keys.astype(BF), values.astype(BF)
        bias = bias_s[c]
        new, sums, rows = [], [None] * 4, []
        for h in range(2):
            s = mm(queries[h], keys) * LOG2E + bias
            lse = jnp.concatenate([stats[h]] * pieces, axis=1)
            p = jnp.exp2(s - lse)
            dp = mm(grads[h], values)
            ds = (p * (dp - deltas[h])).astype(BF)
            pb = p.astype(BF)
            new.append(dqs[h] + mm(ds, keys, 1, 1))
            half = slice(h * HEAD_DIM, (h + 1) * HEAD_DIM)
            dk = mm(query_t[half, :], ds)
            dv = mm(do_t[half, :], pb)
            for which, d, b0, b1, a in ((0, dk, kb0, kb1, krows), (1, dv, vb0, vb1, vrows)):
                for r, b in ((0, b0), (1, b1)):
                    term = d * a[2 * h + r]
                    k = 2 * which + r
                    sums[k] = term if sums[k] is None else sums[k] + term
                    rows.append((which * 4 + 2 * h + r, jnp.sum(d * b, axis=0, keepdims=True)))
        for k in range(4):
            part = slice(k * HEAD_DIM, (k + 1) * HEAD_DIM)
            acc_s[c, part, :] = acc_s[c, part, :] + sums[k]
        for k, row in rows:
            where = (k // 4) * KHW + pair * 4 + k % 4
            heads_s[c, pl.ds(where, 1), :] = row
        return tuple(new)

    zero = jnp.zeros((length, 2 * HEAD_DIM), F32)
    dqs = lax.fori_loop(lo, me + 1, step, (zero, zero))
    dq_t = jnp.transpose(jnp.where(low_half, dqs[0], dqs[1])) * (HEAD_DIM**-0.5 / QRANK)
    for h in range(2):
        d = dq_t[h * HEAD_DIM : (h + 1) * HEAD_DIM, :]
        for r in range(QRANK):
            part = slice(r * HEAD_DIM, (r + 1) * HEAD_DIM)
            b = qfac_ref[QHW + r * HEAD_DIM : QHW + (r + 1) * HEAD_DIM, :].astype(F32)
            k = pl.ds(pair * (2 * QRANK) + h * QRANK + r, 1)
            daq_s[k, :] = jnp.sum(d * b, axis=0, keepdims=True)
            dbq_s[part, :] = dbq_s[part, :] + d * aq_s[k, :]

    @pl.when(pair == PAIRS - 1)
    def _():
        cosine, sine = cos_ref[...], sin_ref[...]
        half = HEAD_DIM // 2
        dq_ref[0:QHW, :] = daq_s[...].astype(BF)
        for r in range(QRANK):
            first = dbq_s[r * HEAD_DIM : r * HEAD_DIM + half, :]
            second = dbq_s[r * HEAD_DIM + half : (r + 1) * HEAD_DIM, :]
            turned = jnp.concatenate(
                [first * cosine + second * sine, second * cosine - first * sine], axis=0
            )
            dq_ref[QHW + r * HEAD_DIM : QHW + (r + 1) * HEAD_DIM, :] = turned.astype(BF)

        def flush(c, carry):
            inside = (c >= lo) & (c <= me)
            for k, ref in enumerate(terms_refs):

                @pl.when(inside & (((c ^ me) % across) == k))
                def _(ref=ref):
                    place = reverse_bits((c ^ me) // across, ref.shape[0])
                    ref[place, 0 : 2 * KDW, :] = (acc_s[c] * (1.0 / KRANK)).astype(BF)
                    ref[place, 2 * KDW :, :] = (heads_s[c] * (1.0 / KRANK)).astype(BF)

                @pl.when(jnp.logical_not(inside) & (((c ^ me) % across) == k))
                def _(ref=ref):
                    ref[reverse_bits((c ^ me) // across, ref.shape[0])] = jnp.zeros((FACW, length), BF)

            return carry

        lax.fori_loop(0, n, flush, 0)


def attention_backward(scal, qfac, facs, start, o, do, lse, cosine, sine):
    length = qfac.shape[1]
    across, along = len(facs), facs[0].shape[0]
    n = across * along
    return pl.pallas_call(
        functools.partial(backward_kernel, across),
        out_shape=(jax.ShapeDtypeStruct((along, FACW, length), BF),) * across
        + (jax.ShapeDtypeStruct((QFW, length), BF),),
        grid_spec=pltpu.PrefetchScalarGridSpec(
            num_scalar_prefetch=1,
            grid=(PAIRS,),
            in_specs=[
                full(qfac.shape),
            ]
            + [full(v.shape) for v in facs]
            + [
                full(start.shape),
                pl.BlockSpec((length, 2 * HEAD_DIM), lambda p, s: (0, p)),
                pl.BlockSpec((length, 2 * HEAD_DIM), lambda p, s: (0, p)),
                pl.BlockSpec((2, length, 128), lambda p, s: (p, 0, 0)),
                full(cosine.shape),
                full(sine.shape),
            ],
            out_specs=[full((along, FACW, length))] * across + [full((QFW, length))],
            scratch_shapes=[
                pltpu.VMEM((n, 2 * KDW, length), BF),
                pltpu.VMEM((QHW, length), F32),
                pltpu.VMEM((n, 2 * KHW, length), F32),
                pltpu.VMEM((n, length, length), F32),
                pltpu.VMEM((n, 2 * KDW, length), F32),
                pltpu.VMEM((n, 2 * KHW, length), F32),
                pltpu.VMEM((QDW, length), F32),
                pltpu.VMEM((QHW, length), F32),
            ],
        ),
        compiler_params=pltpu.CompilerParams(
            dimension_semantics=("arbitrary",), vmem_limit_bytes=58 << 20
        ),
        cost_estimate=SMALL,
        name="attention_backward",
    )(scal, qfac, *facs, start, o, do, lse, cosine, sine)


def norm_of(values):
    inverse = lax.rsqrt(jnp.mean(values * values, axis=-1, keepdims=True) + EPS)
    return values * inverse, inverse


def turn(values, cosine, sine, sign):
    half = HEAD_DIM // 2
    parts = []
    for r in range(values.shape[0] // HEAD_DIM):
        first = values[r * HEAD_DIM : r * HEAD_DIM + half, :]
        second = values[r * HEAD_DIM + half : (r + 1) * HEAD_DIM, :]
        parts.append(first * cosine - sign * second * sine)
        parts.append(second * cosine + sign * first * sine)
    return jnp.concatenate(parts, axis=0)


def enter_kernel(gain_ref, cos_ref, sin_ref, *refs):
    sources, (xa_ref, qfac_ref, fac_ref) = refs[:7], refs[7:10]
    x_ref, qh, qd, kh, kd, vh, vd, sem = refs[10:]
    copies = [
        pltpu.make_async_copy(source, target, sem.at[k])
        for k, (source, target) in enumerate(zip(sources, (x_ref, qh, qd, kh, kd, vh, vd)))
    ]
    for copy in copies:
        copy.start()
    for copy in copies:
        copy.wait()
    normed = norm_of(x_ref[...].astype(F32))[0]
    xa = (normed * gain_ref[...]).astype(BF)
    xa_ref[...] = xa
    cosine, sine = cos_ref[...], sin_ref[...]
    kdims = turn(jnp.transpose(mm(xa, kd[...])), cosine, sine, 1.0)
    fac_ref[0:KDW, :] = kdims.astype(BF)
    fac_ref[KDW : 2 * KDW, :] = jnp.transpose(mm(xa, vd[...])).astype(BF)
    fac_ref[2 * KDW : 2 * KDW + KHW, :] = mm(kh[...], xa, 1, 1).astype(BF)
    fac_ref[2 * KDW + KHW :, :] = mm(vh[...], xa, 1, 1).astype(BF)
    qfac_ref[0:QHW, :] = mm(qh[...], xa, 1, 1).astype(BF)
    qdims = turn(jnp.transpose(mm(xa, qd[...])), cosine, sine, 1.0)
    qfac_ref[QHW:, :] = qdims.astype(BF)


WHOLE = pl.BlockSpec(memory_space=pltpu.VMEM)
RAW = pl.BlockSpec(memory_space=pl.ANY)
SCALAR = pl.BlockSpec(memory_space=pltpu.SMEM)
SMALL = pl.CostEstimate(flops=1000, transcendentals=0, bytes_accessed=1000)


def enter(x, gain, weights, cosine, sine):
    length, width = x.shape
    moved = (x,) + tuple(weights)
    return pl.pallas_call(
        enter_kernel,
        out_shape=(
            jax.ShapeDtypeStruct((length, width), BF),
            jax.ShapeDtypeStruct((QFW, length), BF),
            jax.ShapeDtypeStruct((FACW, length), BF),
        ),
        in_specs=[WHOLE] * 3 + [RAW] * 7,
        out_specs=[WHOLE] * 3,
        scratch_shapes=[pltpu.VMEM(v.shape, BF) for v in moved] + [pltpu.SemaphoreType.DMA((7,))],
        compiler_params=pltpu.CompilerParams(vmem_limit_bytes=40 << 20),
        name="enter",
    )(gain, cosine, sine, *moved)


def block_place(ids_ref, sizes, index, rows):
    place, scale = 0, 1
    for k in reversed(range(len(sizes))):
        place = place + ((index % sizes[k]) ^ ids_ref[k]) * scale
        index, scale = index // sizes[k], scale * sizes[k]
    return pl.multiple_of(place * rows, rows)


def deal(ids_ref, sizes, t_s, outs):
    blocks, rows = outs[0].shape[:2]
    for side in range(2):

        def one(i, carry, side=side):
            place = block_place(ids_ref, sizes, side * blocks + i, rows)
            outs[side][i] = t_s[pl.ds(place, rows), :].astype(BF)
            return carry

        lax.fori_loop(0, blocks, one, 0)


def collect(ids_ref, sizes, sources, write):
    blocks, rows = sources[0].shape[:2]
    for side in range(2):

        def one(i, carry, side=side):
            place = block_place(ids_ref, sizes, side * blocks + i, rows)
            write(pl.ds(place, rows), sources[side][i].astype(F32))
            return carry

        lax.fori_loop(0, blocks, one, 0)


def leave_query_kernel(sizes, ids_ref, xa_ref, dq_ref, fgain_ref, o_ref, dhb_ref, kept_ref, sent_ref, t_s):
    xa_t = jnp.transpose(xa_ref[...])
    depth = o_ref.shape[1]
    t_s[:, 0:depth] = mm(jnp.transpose(o_ref[...]), dhb_ref[...])
    t_s[:, depth : depth + QHW] = mm(xa_t, dq_ref[0:QHW, :], 1, 1)
    t_s[:, depth + QHW : depth + QFW] = mm(xa_t, dq_ref[QHW:, :], 1, 1)
    gain = jnp.concatenate([fgain_ref[...]] * (512 - QFW), axis=0)
    t_s[:, depth + QFW :] = jnp.transpose(gain)
    deal(ids_ref, sizes, t_s, (kept_ref, sent_ref))


def leave_key_kernel(
    sizes, ids_ref, x_ref, xa_ref, gain_ref, dres_ref, dq_ref, kg_ref, cos_ref, sin_ref,
    qh, qd, kh, kd, vh, vd, tg_ref, kept_ref, sent_ref, out_ref
):
    normed, inverse = norm_of(x_ref[...].astype(F32))
    g = kg_ref[...]
    dkd = turn(g[0:KDW, :], cos_ref[...], sin_ref[...], -1.0)
    d_kd = jnp.transpose(dkd).astype(BF)
    d_vd = jnp.transpose(g[KDW : 2 * KDW, :]).astype(BF)
    d_kh = jnp.transpose(g[2 * KDW : 2 * KDW + KHW, :]).astype(BF)
    d_vh = jnp.transpose(g[2 * KDW + KHW :, :]).astype(BF)
    dq = dq_ref[...].astype(F32)
    d_qh = jnp.transpose(dq[0:QHW, :]).astype(BF)
    d_qd = jnp.transpose(dq[QHW:, :]).astype(BF)
    xa_t = jnp.transpose(xa_ref[...])
    out_ref[:, 0:KDW] = mm(xa_t, d_kd)
    out_ref[:, KDW : 2 * KDW] = mm(xa_t, d_vd)
    out_ref[:, 2 * KDW : 2 * KDW + KHW] = mm(xa_t, d_kh)
    out_ref[:, 2 * KDW + KHW : FACW] = mm(xa_t, d_vh)
    dxa = mm(d_qd, qd[...], 1, 1) + mm(d_qh, qh[...])
    dxa = dxa + mm(d_kd, kd[...], 1, 1) + mm(d_vd, vd[...], 1, 1)
    dxa = dxa + mm(d_kh, kh[...]) + mm(d_vh, vh[...])
    scaled = dxa * gain_ref[...]
    mean = jnp.mean(scaled * normed, axis=-1, keepdims=True)
    tg_ref[...] = (dres_ref[...] + inverse * (scaled - normed * mean)).astype(BF)
    gain_part = jnp.sum(dxa * normed, axis=0, keepdims=True)
    gain = jnp.concatenate([gain_part] * (384 - FACW), axis=0)
    out_ref[:, FACW:] = jnp.transpose(gain)
    deal(ids_ref, sizes, out_ref, (kept_ref, sent_ref))


def leave_query(sizes, ids, xa, dq, fgain, o, dhb):
    depth = xa.shape[1]
    blocks = math.prod(sizes) // 2
    columns = depth + 512
    return pl.pallas_call(
        functools.partial(leave_query_kernel, sizes),
        out_shape=(jax.ShapeDtypeStruct((blocks, depth // (2 * blocks), columns), BF),) * 2,
        in_specs=[SCALAR] + [WHOLE] * 5,
        out_specs=[WHOLE] * 2,
        scratch_shapes=[pltpu.VMEM((depth, columns), F32)],
        compiler_params=pltpu.CompilerParams(vmem_limit_bytes=40 << 20),
        cost_estimate=SMALL,
        name="leave_query",
    )(ids, xa, dq, fgain, o, dhb)


def leave_key(sizes, ids, x, xa, gain, dres, dq, kg, cosine, sine, weights):
    length, depth = x.shape
    blocks = math.prod(sizes) // 2
    return pl.pallas_call(
        functools.partial(leave_key_kernel, sizes),
        out_shape=(jax.ShapeDtypeStruct((length, depth), BF),)
        + (jax.ShapeDtypeStruct((blocks, depth // (2 * blocks), 384), BF),) * 2,
        in_specs=[SCALAR] + [WHOLE] * (8 + len(weights)),
        out_specs=[WHOLE] * 3,
        scratch_shapes=[pltpu.VMEM((depth, 384), F32)],
        compiler_params=pltpu.CompilerParams(vmem_limit_bytes=40 << 20),
        cost_estimate=SMALL,
        name="leave_key",
    )(ids, x, xa, gain, dres, dq, kg, cosine, sine, *weights)


def end_query_kernel(sizes, ids_ref, own_ref, got_ref, proj_ref, qh_ref, qd_ref, gain_ref, t_s):
    depth = proj_ref.shape[1]

    def write(rows, v):
        proj_ref[rows, :] = v[:, 0:depth]
        qd_ref[rows, :] = v[:, depth + QHW : depth + QFW]
        t_s[rows, 0:128] = v[:, depth : depth + 128]
        t_s[rows, 128:] = v[:, depth + 384 :]

    collect(ids_ref, sizes, (own_ref, got_ref), write)
    turned = jnp.transpose(t_s[...])
    qh_ref[...] = turned[0:QHW, :]
    gain_ref[...] = turned[128 + QFW - 384 : 128 + QFW - 384 + 1, :]


def end_query(sizes, ids, own, got):
    depth = own.shape[0] * own.shape[1] * 2
    return pl.pallas_call(
        functools.partial(end_query_kernel, sizes),
        out_shape=(
            jax.ShapeDtypeStruct((depth, depth), F32),
            jax.ShapeDtypeStruct((QHW, depth), F32),
            jax.ShapeDtypeStruct((depth, QDW), F32),
            jax.ShapeDtypeStruct((1, depth), F32),
        ),
        in_specs=[SCALAR] + [WHOLE] * 2,
        out_specs=[WHOLE] * 4,
        scratch_shapes=[pltpu.VMEM((depth, 256), F32)],
        compiler_params=pltpu.CompilerParams(vmem_limit_bytes=40 << 20),
        name="end_query",
    )(ids, own, got)


def end_key_kernel(sizes, ids_ref, own_ref, got_ref, kd_ref, vd_ref, kh_ref, vh_ref, gain_ref, t_s):
    def write(rows, v):
        kd_ref[rows, :] = v[:, 0:KDW]
        vd_ref[rows, :] = v[:, KDW : 2 * KDW]
        t_s[rows, :] = v[:, 2 * KDW :]

    collect(ids_ref, sizes, (own_ref, got_ref), write)
    turned = jnp.transpose(t_s[...])
    kh_ref[...] = turned[0:KHW, :]
    vh_ref[...] = turned[KHW : 2 * KHW, :]
    gain_ref[...] = turned[2 * KHW : 2 * KHW + 1, :]


def end_key(sizes, ids, own, got):
    depth = own.shape[0] * own.shape[1] * 2
    return pl.pallas_call(
        functools.partial(end_key_kernel, sizes),
        out_shape=(
            jax.ShapeDtypeStruct((depth, KDW), F32),
            jax.ShapeDtypeStruct((depth, KDW), F32),
            jax.ShapeDtypeStruct((KHW, depth), F32),
            jax.ShapeDtypeStruct((KHW, depth), F32),
            jax.ShapeDtypeStruct((1, depth), F32),
        ),
        in_specs=[SCALAR] + [WHOLE] * 2,
        out_specs=[WHOLE] * 5,
        scratch_shapes=[pltpu.VMEM((depth, 128), F32)],
        name="end_key",
    )(ids, own, got)


def after(v, *others):
    return lax.optimization_barrier((v,) + others)[0]


class Grid:
    def __init__(self, dp, tensor):
        self.c = 2
        self.y = dp // 2
        self.x = self.y if tensor % self.y == 0 else 1
        self.z = tensor // self.x
        self.dp, self.tensor = dp, tensor
        self.axes = {
            "c": ("dp", 1, self.c),
            "y": ("dp", self.c, self.y),
            "x": ("tensor", 1, self.x),
            "z": ("tensor", self.x, self.z),
        }

    def size(self, g):
        return self.axes[g][2]

    def place(self, g):
        axis, stride, size = self.axes[g]
        return ((lax.axis_index(axis) // stride) % size).astype(jnp.int32)

    def swap(self, v, g, r):
        axis, stride, size = self.axes[g]
        total = self.dp if axis == "dp" else self.tensor
        return lax.ppermute(v, axis, [(i, i ^ (r * stride)) for i in range(total)])

    def bits(self, g):
        return [1 << k for k in range(self.size(g).bit_length() - 1)]

    def rels(self, g):
        order = [0]
        for bit in reversed(self.bits(g)):
            order = order + [r ^ bit for r in order]
        return order

    def stack(self, v, g):
        v = v[None]
        for bit in reversed(self.bits(g)):
            v = jnp.concatenate([v, self.swap(v, g, bit)], axis=0)
        return v

    def unstack(self, v, g, last=BF):
        bits = self.bits(g)
        for k, bit in enumerate(bits):
            rows = v.shape[0] // 2
            got = self.swap(v[rows:].astype(BF), g, bit)
            v = v[:rows].astype(F32) + got.astype(F32)
        return v[0].astype(last)

    def direct(self, v, g):
        return [v] + [self.swap(v, g, r) for r in self.rels(g)[1:]]

    def swap_masks(self, v, dp_mask, tensor_mask):
        if not tensor_mask:
            return lax.ppermute(v, "dp", [(i, i ^ dp_mask) for i in range(self.dp)])
        if not dp_mask:
            return lax.ppermute(v, "tensor", [(i, i ^ tensor_mask) for i in range(self.tensor)])
        mask = dp_mask * self.tensor + tensor_mask
        pairs = [(i, i ^ mask) for i in range(self.dp * self.tensor)]
        return lax.ppermute(v, ("dp", "tensor"), pairs)

    def levels(self, plan):
        out = []
        for letters in plan:
            masks = [(0, 0)]
            for g in letters:
                axis, stride, size = self.axes[g]
                masks = [
                    (d + r * stride, t) if axis == "dp" else (d, t + r * stride)
                    for d, t in masks
                    for r in range(size)
                ]
            out.append(masks)
        return out

    def numbers(self, plan):
        out = []
        for letters in plan:
            number = jnp.int32(0)
            for g in letters:
                number = number * self.size(g) + self.place(g)
            out.append(number)
        return jnp.stack(out)

    def sum_all(self, kept, sent, plan, shared):
        levels = self.levels(plan)
        v = kept.astype(F32) + self.swap_masks(sent, *levels[0][1]).astype(F32)
        for masks in levels[1:]:
            low = v.astype(BF)
            total = v[0]
            for m in range(1, len(masks)):
                total = total + self.swap_masks(low[m], *masks[m]).astype(F32)
            v = total
        for masks in self.levels(shared):
            low = v.astype(BF)
            for m in masks[1:]:
                v = v + self.swap_masks(low, *m).astype(F32)
        v = v.astype(BF)
        for masks in reversed(levels[1:]):
            v = jnp.stack([v] + [self.swap_masks(v, *m) for m in masks[1:]])
        return v, self.swap_masks(v, *levels[0][1])


def ffn_kernel(parts, plan, shards, blend, scal_ref, xf_ref, dy_ref, *refs):
    own, arrays = plan
    count = (3 if own else 0) + len(arrays)
    sources, refs = refs[:count], refs[count:]
    if blend:
        mixed_in, dxf_in = refs[:2]
        refs = refs[2:]
    mixed_ref, dxf_ref, inner_ref, dgate_ref, dup_ref, w_s, sem = refs
    width = w_s.shape[2]
    rows = w_s.shape[3] // parts
    copies = []

    def move(source, target):
        copies.append(pltpu.make_async_copy(source, target, sem.at[len(copies)]))

    if own:
        for k in range(3):
            move(sources[k], w_s.at[k, 0])
    for (slots, q), source in zip(arrays, sources[3 if own else 0 :]):
        place = pl.multiple_of((scal_ref[0] ^ q) * rows, rows)
        for i, slot in enumerate(slots):
            move(source.at[i], w_s.at[:, slot, :, pl.ds(place, rows)])
    for copy in copies:
        copy.start()
    for copy in copies:
        copy.wait()
    xf, dy = xf_ref[...], dy_ref[...]
    units, unused, hidden = inner_ref.shape
    for s in range(units):
        wg, wu, wd = ((w_s[k] if units == 1 else w_s[k, s]).reshape(hidden, -1) for k in range(3))
        gate = mm(xf, wg, 1, 1)
        up = mm(xf, wu, 1, 1)
        d_inner = mm(dy, wd, 1, 1)
        sig = 1.0 / (1.0 + jnp.exp(-gate))
        act = gate * sig
        inner = (act * up).astype(BF)
        d_gate = (d_inner * up * sig * (1.0 + gate * (1.0 - sig))).astype(BF)
        d_up = (d_inner * act).astype(BF)
        inner_ref[s] = inner
        dgate_ref[s] = d_gate
        dup_ref[s] = d_up
        dxf = mm(d_gate, wg) + mm(d_up, wu)
        mixed = mm(inner, wd)
        if s == 0 and blend:
            dxf, mixed = dxf + dxf_in[...], mixed + mixed_in[...]
        if s > 0:
            dxf, mixed = dxf + total[0], mixed + total[1]
        total = (dxf, mixed)
    dxf_ref[...] = total[0].astype(dxf_ref.dtype)
    mixed_ref[...] = total[1].astype(mixed_ref.dtype)


def ffn(mine, xf, dy, own, arrays, parts, width, before, out_type, name):
    length, depth = xf.shape
    shards = (1 if own else 0) + sum(len(slots) for slots, q, v in arrays if q == 0)
    hidden = (1, length, shards * width) if width % 16 == 0 else (shards, length, width)
    plan = (bool(own), [(slots, q) for slots, q, v in arrays])
    sources = list(own) + [v for slots, q, v in arrays]
    moves = (3 if own else 0) + sum(len(slots) for slots, q, v in arrays)
    return pl.pallas_call(
        functools.partial(ffn_kernel, parts, plan, shards, bool(before)),
        out_shape=(jax.ShapeDtypeStruct((length, depth), out_type),) * 2
        + (jax.ShapeDtypeStruct(hidden, BF),) * 3,
        in_specs=[SCALAR, WHOLE, WHOLE] + [RAW] * len(sources) + [WHOLE] * len(before),
        out_specs=[WHOLE] * 5,
        scratch_shapes=[
            pltpu.VMEM((3, shards, width, depth), BF),
            pltpu.SemaphoreType.DMA((moves,)),
        ],
        compiler_params=pltpu.CompilerParams(vmem_limit_bytes=58 << 20),
        cost_estimate=SMALL,
        name=name,
    )(mine, xf, dy, *sources, *before)


def products(lefts, rights, width, write):
    slot = 0
    for group in range(len(lefts[0])):
        units, unused, hidden = lefts[0][group].shape
        for s in range(units):
            total = None
            for b in range(len(rights)):
                term = mm(jnp.transpose(lefts[b][group][s]), rights[b][...])
                total = term if total is None else total + term
            for i in range(hidden // width):
                write(slot, total[i * width : (i + 1) * width, :])
                slot += 1


def divide(refs, blocks):
    each = len(refs) // blocks
    return [refs[b * each : (b + 1) * each] for b in range(blocks)]


def store(outs, scal_ref, t_s, slot, first, value):
    rows, lanes = value.shape[0], outs[0].shape[3]
    t_s[0:rows, :] = value
    for q in range(2 * outs[0].shape[0]):
        place = pl.multiple_of((scal_ref[0] ^ q) * lanes, lanes)
        part = t_s[0:rows, pl.ds(place, lanes)]
        outs[q % 2][q // 2, slot, first : first + rows, :] = part.astype(BF)


def gate_up_kernel(blocks, scal_ref, *refs):
    xfs, outs, t_s = refs[:blocks], refs[-3:-1], refs[-1]
    rest = refs[blocks:-3]
    width = outs[0].shape[2] // 2
    for k in range(2):
        lefts = divide(rest[k * len(rest) // 2 : (k + 1) * len(rest) // 2], blocks)

        def write(slot, value, k=k):
            store(outs, scal_ref, t_s, slot, k * width, value)

        products(lefts, xfs, width, write)


def down_kernel(blocks, scal_ref, *refs):
    dys, outs, t_s = refs[:blocks], refs[-3:-1], refs[-1]
    width = outs[0].shape[2]

    def write(slot, value):
        store(outs, scal_ref, t_s, slot, 0, value)

    products(divide(refs[blocks:-3], blocks), dys, width, write)


def grads(kernel, mine, wholes, parts, zs, rows, depth, scratch, name):
    return pl.pallas_call(
        kernel,
        out_shape=(jax.ShapeDtypeStruct((parts // 2, zs, rows, depth // parts), BF),) * 2,
        in_specs=[SCALAR] + [WHOLE] * len(wholes),
        out_specs=[WHOLE] * 2,
        scratch_shapes=scratch,
        compiler_params=pltpu.CompilerParams(vmem_limit_bytes=58 << 20),
        cost_estimate=SMALL,
        name=name,
    )(mine, *wholes)


def unpack_kernel(scal_ref, first_ref, second_ref, gate_ref, up_ref, down_ref):
    width = gate_ref.shape[0]
    gate_ref[...] = first_ref[0, 0:width, :].astype(F32)
    up_ref[...] = first_ref[0, width:, :].astype(F32)
    down_ref[...] = second_ref[0].astype(F32)


def unpack(mine, first, second):
    parts, width, lanes = second.shape
    column = pl.BlockSpec((width, lanes), lambda q, s: (0, s[0] ^ q))
    return pl.pallas_call(
        unpack_kernel,
        out_shape=(jax.ShapeDtypeStruct((width, parts * lanes), F32),) * 3,
        grid_spec=pltpu.PrefetchScalarGridSpec(
            num_scalar_prefetch=1,
            grid=(parts,),
            in_specs=[
                pl.BlockSpec((1, 2 * width, lanes), lambda q, s: (q, 0, 0)),
                pl.BlockSpec((1, width, lanes), lambda q, s: (q, 0, 0)),
            ],
            out_specs=[column] * 3,
        ),
        compiler_params=pltpu.CompilerParams(dimension_semantics=("arbitrary",)),
        name="unpack",
    )(mine, first, second)


def spread_pieces(grid, got, tie):
    entries = []
    for k in range(grid.y):
        piece = got if k == 0 else grid.swap(got, "y", k)
        entries.append((2 * k, piece))
    return [
        pair
        for q, piece in entries
        for pair in ((q, piece), (q + 1, grid.swap(after(piece, tie), "c", 1)))
    ]


def reduce_core(grid, even, odd):
    held = even.astype(F32) + grid.swap(odd, "c", 1).astype(F32)
    return [held[0]] + [held[k].astype(BF) for k in range(1, grid.y)]


def reduce_part(grid, held):
    total = held[0]
    for k in range(1, grid.y):
        total = total + grid.swap(held[k], "y", k).astype(F32)
    return grid.unstack(total.astype(BF), "z")


def spread_part(grid, mine):
    column = [mine] + [grid.swap(mine, "y", k) for k in range(1, grid.y)]
    pieces = []
    for piece in column:
        pieces += [piece, grid.swap(piece, "c", 1)]
    return jnp.stack(pieces)


def contract(left, right, left_dim, right_dim):
    return lax.dot_general(
        left, right, (((left_dim,), (right_dim,)), ((), ())), preferred_element_type=jnp.float32
    )


def norm_back(grad_out, normed, inverse, gain):
    scaled = grad_out * gain
    gain_part = jnp.sum(grad_out * normed, axis=0)
    grad_in = inverse * (scaled - normed * jnp.mean(scaled * normed, axis=-1, keepdims=True))
    return (grad_in, gain_part)


def body(
    grid,
    tokens,
    cotangent,
    segments,
    positions,
    attngain,
    ffngain,
    queryheads,
    querydims,
    keyheads,
    keydims,
    valueheads,
    valuedims,
    outproj,
    gateproj,
    upproj,
    downproj,
):
    x = tokens[0]
    upstream = cotangent[0]
    length, depth = x.shape
    parts = grid.dp
    lanes = depth // parts
    me = lax.axis_index("tensor").astype(jnp.int32)
    spot = jnp.stack([lax.axis_index("dp").astype(jnp.int32), grid.place("z")])
    offset = me * length
    places = lax.dynamic_slice_in_dim(positions[0], offset, length)
    half = HEAD_DIM // 2
    freqs = 10000.0 ** (-jnp.arange(half, dtype=F32) * 2.0 / HEAD_DIM)
    angles = freqs[:, None] * places.astype(F32)[None, :]
    cosine, sine = jnp.cos(angles), jnp.sin(angles)
    start = (offset + jnp.arange(length, dtype=jnp.int32) - places)[:, None]
    scal = jnp.stack([jnp.maximum(offset - places[0], 0) // length, me]).astype(jnp.int32)
    weights = (queryheads.T, querydims, keyheads.T, keydims, valueheads.T, valuedims)

    own = (gateproj.T, upproj.T, downproj)
    width = downproj.shape[0]
    payload = jnp.stack(
        [lax.dynamic_slice_in_dim(v, spot[0] * lanes, lanes, 1) for v in own]
    )
    dys = [upstream] + [grid.swap(upstream, "x", r) for r in range(1, grid.x)]
    far = grid.bits("z")[::-1]
    held, rels = payload[None], [0]

    xa, qfac, fac = enter(x, attngain[None, :], weights, cosine, sine)
    near = jnp.stack(grid.direct(fac, "z"))
    held = after(held, near)
    arrived = [grid.swap(held, "z", far[0])] if far else []
    facs = [near] + [grid.swap(near, "x", r) for r in range(1, grid.x)]
    stages = []
    for k, bit in enumerate(far):
        got = arrived[k]
        new = [r ^ bit for r in rels]
        if k + 1 < len(far):
            held = jnp.concatenate([held, got], axis=0)
            arrived.append(grid.swap(held, "z", far[k + 1]))
        rels = rels + new
        stages.append((new, got))
    qfac = after(qfac, held, *dys[1:])
    attn_out, lse = attention_forward(scal, qfac, facs, start)
    stages = [
        [
            (new, q, v)
            for q, v in spread_pieces(
                grid, after(got, attn_out) if k == len(stages) - 1 else got, attn_out
            )
        ]
        for k, (new, got) in enumerate(stages)
    ]

    local = x.astype(F32)
    residual = local + jnp.dot(attn_out, outproj, preferred_element_type=jnp.float32)
    inverse_two = lax.rsqrt(jnp.mean(residual * residual, axis=-1, keepdims=True) + EPS)
    normed_two = residual * inverse_two
    input_two = (normed_two * ffngain).astype(jnp.bfloat16)
    xfs = [input_two] + [grid.swap(input_two, "x", r) for r in range(1, grid.x)]

    early, late, filled = [], [], 1
    for entries in stages[:-1]:
        for rels, q, v in entries:
            early.append(([filled + i for i in range(len(rels))], q, v))
        filled += len(entries[0][0])
    for rels, q, v in stages[-1] if stages else []:
        late.append((list(range(len(rels))), q, v))


    results = [None] * grid.x
    firsts = []
    for k in range(grid.x):
        kind = BF if k and not late else F32
        if k:
            xfs[k] = after(xfs[k], firsts[0][0])
        firsts.append(
            ffn(spot, xfs[k], dys[k], own, early, parts, width, (), kind, "ffn_early")
        )
    for k in reversed(range(grid.x)):
        first = firsts[k]
        if late:
            second = ffn(
                spot, xfs[k], dys[k], (), late, parts, width, first[:2], BF if k else F32, "ffn_late"
            )
            results[k] = (second[0], second[1]) + tuple(
                [first[i], second[i]] for i in range(2, 5)
            )
        else:
            results[k] = (first[0], first[1]) + tuple([first[i]] for i in range(2, 5))
    d_norm_two, ffn_out = results[0][1], results[0][0]
    inners, dgates, dups = (
        [v for k in range(grid.x) for v in results[k][i]] for i in range(2, 5)
    )
    first_parts = grads(
        functools.partial(gate_up_kernel, grid.x),
        spot, xfs + dgates + dups, parts, grid.z, 2 * width, depth,
        [pltpu.VMEM((width, depth), F32)], "gate_up_grads",
    )
    second_parts = grads(
        functools.partial(down_kernel, grid.x),
        spot, dys + inners, parts, grid.z, width, depth,
        [pltpu.VMEM((width, depth), F32)], "down_grads",
    )
    first_held = reduce_core(grid, *first_parts)
    for r in range(1, grid.x):
        got = grid.swap(results[r][1], "x", r)
        d_norm_two = d_norm_two + after(got, second_parts[0], first_held[0]).astype(F32)
    grad_through, ffngain_part = norm_back(d_norm_two, normed_two, inverse_two, ffngain)
    d_residual = upstream.astype(jnp.float32) + grad_through
    d_res_low = d_residual.astype(jnp.bfloat16)
    d_attended = contract(d_res_low, outproj, 1, 1).astype(jnp.bfloat16)
    d_attended = after(d_attended, first_held[-1])
    back = attention_backward(
        scal, qfac, facs, start, attn_out, d_attended, lse, cosine, sine
    )
    terms, dq = back[:-1], back[-1]
    near = terms[0].astype(F32)
    for r in range(1, grid.x):
        near = near + grid.swap(terms[r], "x", r).astype(F32)
    low = near.astype(BF)
    key_grads = near[0]
    for k, r in enumerate(grid.rels("z")):
        if k:
            key_grads = key_grads + grid.swap(low[k], "z", r).astype(F32)

    for r in range(1, grid.x):
        ffn_out = ffn_out + grid.swap(after(results[r][0], d_res_low), "x", r).astype(F32)
    mixed = (residual + ffn_out).astype(jnp.bfloat16)

    first_mine = reduce_part(grid, first_held)
    second_mine = reduce_part(grid, reduce_core(grid, *second_parts))
    gate_part, up_part, down_part = unpack(
        spot, spread_part(grid, first_mine), spread_part(grid, second_mine)
    )

    plan, shared = ("c", "xy", "z"), ()
    if depth // (parts * grid.tensor) < 16:
        plan, shared = ("c", "xy"), ("z",)
    sizes = tuple(len(masks) for masks in grid.levels(plan))
    ids = grid.numbers(plan)
    shape = sizes[1:] + (depth // math.prod(sizes), -1)
    tokens_grad, kept, sent = leave_key(
        sizes, ids, x, xa, attngain[None, :], d_residual, dq, key_grads, cosine, sine, weights
    )
    sums = grid.sum_all(kept.reshape(shape), sent.reshape(shape), plan, shared)
    flat = [v.reshape(kept.shape) for v in sums]
    kd_grad, vd_grad, kh_grad, vh_grad, again_grad = end_key(sizes, ids, *flat)
    kept, sent = leave_query(sizes, ids, xa, dq, ffngain_part[None, :], attn_out, d_res_low)
    sums = grid.sum_all(kept.reshape(shape), sent.reshape(shape), plan, shared)
    flat = [v.reshape(kept.shape) for v in sums]
    out_part, qh_grad, qd_grad, fgain_grad = end_query(sizes, ids, *flat)
    return (
        mixed[None],
        tokens_grad[None],
        again_grad[0],
        fgain_grad[0],
        qh_grad.T,
        qd_grad,
        kh_grad.T,
        kd_grad,
        vh_grad.T,
        vd_grad,
        out_part,
        gate_part.T,
        up_part.T,
        down_part,
    )


def solution(mesh):
    grid = Grid(mesh.shape["dp"], mesh.shape["tensor"])
    rows = P("dp", "tensor", None)
    placed = (rows, rows, P("dp", None), P("dp", None)) + (P(),) * 9
    halves = (P(None, "tensor"), P(None, "tensor"), P("tensor", None))
    return jax.shard_map(
        functools.partial(body, grid),
        mesh=mesh,
        in_specs=placed + halves,
        out_specs=(rows, rows) + (P(),) * 9 + halves,
        check_vma=False,
    )
```

```python
import functools
import math

import jax
import jax.numpy as jnp
from jax import lax
from jax.experimental import pallas as pl
from jax.experimental.pallas import tpu as pltpu

from jax.sharding import PartitionSpec as P

HEADS = 16
HEAD_DIM = 64
QRANK = 6
KRANK = 2
PAIRS = HEADS // 2
QHW = HEADS * QRANK
QDW = QRANK * HEAD_DIM
KDW = KRANK * HEAD_DIM
KHW = HEADS * KRANK
FACW = 2 * KDW + 2 * KHW
QFW = QHW + QDW
LOG2E = 1.4426950408889634
EPS = 1e-06
BF = jnp.bfloat16
F32 = jnp.float32


def mm(a, b, ca=1, cb=0):
    return lax.dot_general(a, b, (((ca,), (cb,)), ((), ())), preferred_element_type=F32)


def expand_pair(bk0, bk1, rows):
    first = rows[0] * bk0 + rows[1] * bk1
    second = rows[2] * bk0 + rows[3] * bk1
    return jnp.concatenate([first, second], axis=0) * (1.0 / KRANK)


def query_pair(qfac_ref, aq_s, pair):
    halves = []
    for h in range(2):
        acc = None
        for r in range(QRANK):
            row = aq_s[pl.ds(pair * (2 * QRANK) + h * QRANK + r, 1), :]
            term = row * qfac_ref[QHW + r * HEAD_DIM : QHW + (r + 1) * HEAD_DIM, :].astype(F32)
            acc = term if acc is None else acc + term
        halves.append(acc * (1.0 / QRANK))
    return jnp.concatenate(halves, axis=0).astype(BF)


def reverse_bits(r, size):
    total, bits = 0, size.bit_length() - 1
    for k in range(bits):
        total = total + (((r >> k) & 1) << (bits - 1 - k))
    return total


def fill_tables(scal_ref, qfac_ref, fac_refs, start_ref, fac_s, aq_s, kv_s, bias_s):
    length = qfac_ref.shape[1]
    me = scal_ref[1]
    across = len(fac_refs)
    aq_s[...] = qfac_ref[0:QHW, :].astype(F32)
    row = lax.broadcasted_iota(jnp.int32, (length, length), 0) + me * length
    column = lax.broadcasted_iota(jnp.int32, (length, length), 1)
    begin = start_ref[...]

    def fill(c, carry):
        for k, ref in enumerate(fac_refs):

            @pl.when(((c ^ me) % across) == k)
            def _(ref=ref):
                piece = ref[reverse_bits((c ^ me) // across, ref.shape[0])]
                fac_s[c] = piece[0 : 2 * KDW, :]
                kv_s[c] = piece[2 * KDW :, :].astype(F32)

        key = column + c * length
        keep = (key >= begin) & (key <= row)
        bias_s[c] = jnp.where(keep, 0.0, -1e30)
        return carry

    lax.fori_loop(scal_ref[0], me + 1, fill, 0)


def key_pair(fac_ref, kv_s, c, pair, which):
    base = which * KDW
    b0 = fac_ref[c, base : base + HEAD_DIM, :].astype(F32)
    b1 = fac_ref[c, base + HEAD_DIM : base + 2 * HEAD_DIM, :].astype(F32)
    rows = [kv_s[c, pl.ds(which * KHW + pair * 4 + j, 1), :] for j in range(4)]
    return expand_pair(b0, b1, rows), b0, b1, rows


def forward_kernel(across, scal_ref, qfac_ref, *refs):
    fac_refs, start_ref = refs[:across], refs[across]
    o_ref, lse_ref, fac_ref, aq_s, kv_s, bias_s, s_s = refs[across + 1 :]
    pair = pl.program_id(0)
    length = qfac_ref.shape[1]
    lo, me = scal_ref[0], scal_ref[1]

    @pl.when(pair == 0)
    def _():
        fill_tables(scal_ref, qfac_ref, fac_refs, start_ref, fac_ref, aq_s, kv_s, bias_s)

    query = jnp.transpose(query_pair(qfac_ref, aq_s, pair).astype(F32)) * (HEAD_DIM**-0.5)
    low_half = lax.broadcasted_iota(jnp.int32, (length, 2 * HEAD_DIM), 1) < HEAD_DIM
    queries = [
        jnp.where(low_half, query, 0.0).astype(BF),
        jnp.where(low_half, 0.0, query).astype(BF),
    ]
    lanes = 128
    pieces = length // lanes

    def score(c, tops):
        keys = key_pair(fac_ref, kv_s, c, pair, 0)[0].astype(BF)
        bias = bias_s[c]
        new = []
        for h in range(2):
            s = mm(queries[h], keys) * LOG2E + bias
            s_s[h, c] = s
            top = tops[h]
            for i in range(pieces):
                top = jnp.maximum(top, s[:, i * lanes : (i + 1) * lanes])
            new.append(top)
        return tuple(new)

    start = jnp.full((length, lanes), -1e30, F32)
    tops = lax.fori_loop(lo, me + 1, score, (start, start))
    tops = [jnp.max(top, axis=1, keepdims=True) for top in tops]

    def value(c, carry):
        values = key_pair(fac_ref, kv_s, c, pair, 1)[0].astype(BF)
        new = []
        for h in range(2):
            p = jnp.exp2(s_s[h, c] - tops[h])
            total = carry[2 * h]
            for i in range(pieces):
                total = total + p[:, i * lanes : (i + 1) * lanes]
            new += [total, carry[2 * h + 1] + mm(p.astype(BF), values, 1, 1)]
        return tuple(new)

    zero = jnp.zeros((length, lanes), F32)
    wide = jnp.zeros((length, 2 * HEAD_DIM), F32)
    done = lax.fori_loop(lo, me + 1, value, (zero, wide, zero, wide))
    outs = []
    for h in range(2):
        total = jnp.sum(done[2 * h], axis=1, keepdims=True)
        outs.append(done[2 * h + 1] / total)
        lse_ref[h] = jnp.broadcast_to(tops[h] + jnp.log2(total), (length, lanes))
    o_ref[...] = jnp.where(low_half, outs[0], outs[1]).astype(BF)


def full(shape):
    return pl.BlockSpec(shape, lambda p, s: (0,) * len(shape))


def attention_forward(scal, qfac, facs, start):
    length = qfac.shape[1]
    n = facs[0].shape[0] * len(facs)
    return pl.pallas_call(
        functools.partial(forward_kernel, len(facs)),
        out_shape=(
            jax.ShapeDtypeStruct((length, HEADS * HEAD_DIM), BF),
            jax.ShapeDtypeStruct((HEADS, length, 128), F32),
        ),
        grid_spec=pltpu.PrefetchScalarGridSpec(
            num_scalar_prefetch=1,
            grid=(PAIRS,),
            in_specs=[full(qfac.shape)] + [full(v.shape) for v in facs] + [full(start.shape)],
            out_specs=[
                pl.BlockSpec((length, 2 * HEAD_DIM), lambda p, s: (0, p)),
                pl.BlockSpec((2, length, 128), lambda p, s: (p, 0, 0)),
            ],
            scratch_shapes=[
                pltpu.VMEM((n, 2 * KDW, length), BF),
                pltpu.VMEM((QHW, length), F32),
                pltpu.VMEM((n, 2 * KHW, length), F32),
                pltpu.VMEM((n, length, length), F32),
                pltpu.VMEM((2, n, length, length), F32),
            ],
        ),
        compiler_params=pltpu.CompilerParams(
            dimension_semantics=("arbitrary",), vmem_limit_bytes=58 << 20
        ),
        cost_estimate=SMALL,
        name="attention_forward",
    )(scal, qfac, *facs, start)


def backward_kernel(across, scal_ref, qfac_ref, *refs):
    fac_refs = refs[:across]
    start_ref, o_ref, do_ref, lse_ref, cos_ref, sin_ref = refs[across : across + 6]
    terms_refs = refs[across + 6 : 2 * across + 6]
    dq_ref, fac_ref, aq_s, kv_s, bias_s, acc_s, heads_s, dbq_s, daq_s = refs[2 * across + 6 :]
    pair = pl.program_id(0)
    length = qfac_ref.shape[1]
    n = fac_ref.shape[0]
    lo, me = scal_ref[0], scal_ref[1]
    pieces = length // 128

    @pl.when(pair == 0)
    def _():
        fill_tables(scal_ref, qfac_ref, fac_refs, start_ref, fac_ref, aq_s, kv_s, bias_s)
        dbq_s[...] = jnp.zeros_like(dbq_s)

        def clear(c, carry):
            acc_s[c] = jnp.zeros((2 * KDW, length), F32)
            return carry

        lax.fori_loop(lo, me + 1, clear, 0)

    query_t = query_pair(qfac_ref, aq_s, pair).astype(F32) * (HEAD_DIM**-0.5)
    query = jnp.transpose(query_t)
    query_t = query_t.astype(BF)
    do = do_ref[...].astype(F32)
    do_t = jnp.transpose(do).astype(BF)
    low_half = lax.broadcasted_iota(jnp.int32, (length, 2 * HEAD_DIM), 1) < HEAD_DIM
    product = do * o_ref[...].astype(F32)
    queries, grads, deltas, stats = [], [], [], []
    for h in range(2):
        keep = low_half if h == 0 else jnp.logical_not(low_half)
        queries.append(jnp.where(keep, query, 0.0).astype(BF))
        grads.append(jnp.where(keep, do, 0.0).astype(BF))
        deltas.append(jnp.sum(jnp.where(keep, product, 0.0), axis=1, keepdims=True))
        stats.append(lse_ref[h])

    def step(c, dqs):
        keys, kb0, kb1, krows = key_pair(fac_ref, kv_s, c, pair, 0)
        values, vb0, vb1, vrows = key_pair(fac_ref, kv_s, c, pair, 1)
        keys, values = keys.astype(BF), values.astype(BF)
        bias = bias_s[c]
        new, sums, rows = [], [None] * 4, []
        for h in range(2):
            s = mm(queries[h], keys) * LOG2E + bias
            lse = jnp.concatenate([stats[h]] * pieces, axis=1)
            p = jnp.exp2(s - lse)
            dp = mm(grads[h], values)
            ds = (p * (dp - deltas[h])).astype(BF)
            pb = p.astype(BF)
            new.append(dqs[h] + mm(ds, keys, 1, 1))
            half = slice(h * HEAD_DIM, (h + 1) * HEAD_DIM)
            dk = mm(query_t[half, :], ds)
            dv = mm(do_t[half, :], pb)
            for which, d, b0, b1, a in ((0, dk, kb0, kb1, krows), (1, dv, vb0, vb1, vrows)):
                for r, b in ((0, b0), (1, b1)):
                    term = d * a[2 * h + r]
                    k = 2 * which + r
                    sums[k] = term if sums[k] is None else sums[k] + term
                    rows.append((which * 4 + 2 * h + r, jnp.sum(d * b, axis=0, keepdims=True)))
        for k in range(4):
            part = slice(k * HEAD_DIM, (k + 1) * HEAD_DIM)
            acc_s[c, part, :] = acc_s[c, part, :] + sums[k]
        for k, row in rows:
            where = (k // 4) * KHW + pair * 4 + k % 4
            heads_s[c, pl.ds(where, 1), :] = row
        return tuple(new)

    zero = jnp.zeros((length, 2 * HEAD_DIM), F32)
    dqs = lax.fori_loop(lo, me + 1, step, (zero, zero))
    dq_t = jnp.transpose(jnp.where(low_half, dqs[0], dqs[1])) * (HEAD_DIM**-0.5 / QRANK)
    for h in range(2):
        d = dq_t[h * HEAD_DIM : (h + 1) * HEAD_DIM, :]
        for r in range(QRANK):
            part = slice(r * HEAD_DIM, (r + 1) * HEAD_DIM)
            b = qfac_ref[QHW + r * HEAD_DIM : QHW + (r + 1) * HEAD_DIM, :].astype(F32)
            k = pl.ds(pair * (2 * QRANK) + h * QRANK + r, 1)
            daq_s[k, :] = jnp.sum(d * b, axis=0, keepdims=True)
            dbq_s[part, :] = dbq_s[part, :] + d * aq_s[k, :]

    @pl.when(pair == PAIRS - 1)
    def _():
        cosine, sine = cos_ref[...], sin_ref[...]
        half = HEAD_DIM // 2
        dq_ref[0:QHW, :] = daq_s[...].astype(BF)
        for r in range(QRANK):
            first = dbq_s[r * HEAD_DIM : r * HEAD_DIM + half, :]
            second = dbq_s[r * HEAD_DIM + half : (r + 1) * HEAD_DIM, :]
            turned = jnp.concatenate(
                [first * cosine + second * sine, second * cosine - first * sine], axis=0
            )
            dq_ref[QHW + r * HEAD_DIM : QHW + (r + 1) * HEAD_DIM, :] = turned.astype(BF)

        def flush(c, carry):
            inside = (c >= lo) & (c <= me)
            for k, ref in enumerate(terms_refs):

                @pl.when(inside & (((c ^ me) % across) == k))
                def _(ref=ref):
                    place = reverse_bits((c ^ me) // across, ref.shape[0])
                    ref[place, 0 : 2 * KDW, :] = (acc_s[c] * (1.0 / KRANK)).astype(BF)
                    ref[place, 2 * KDW :, :] = (heads_s[c] * (1.0 / KRANK)).astype(BF)

                @pl.when(jnp.logical_not(inside) & (((c ^ me) % across) == k))
                def _(ref=ref):
                    ref[reverse_bits((c ^ me) // across, ref.shape[0])] = jnp.zeros((FACW, length), BF)

            return carry

        lax.fori_loop(0, n, flush, 0)


def attention_backward(scal, qfac, facs, start, o, do, lse, cosine, sine):
    length = qfac.shape[1]
    across, along = len(facs), facs[0].shape[0]
    n = across * along
    return pl.pallas_call(
        functools.partial(backward_kernel, across),
        out_shape=(jax.ShapeDtypeStruct((along, FACW, length), BF),) * across
        + (jax.ShapeDtypeStruct((QFW, length), BF),),
        grid_spec=pltpu.PrefetchScalarGridSpec(
            num_scalar_prefetch=1,
            grid=(PAIRS,),
            in_specs=[
                full(qfac.shape),
            ]
            + [full(v.shape) for v in facs]
            + [
                full(start.shape),
                pl.BlockSpec((length, 2 * HEAD_DIM), lambda p, s: (0, p)),
                pl.BlockSpec((length, 2 * HEAD_DIM), lambda p, s: (0, p)),
                pl.BlockSpec((2, length, 128), lambda p, s: (p, 0, 0)),
                full(cosine.shape),
                full(sine.shape),
            ],
            out_specs=[full((along, FACW, length))] * across + [full((QFW, length))],
            scratch_shapes=[
                pltpu.VMEM((n, 2 * KDW, length), BF),
                pltpu.VMEM((QHW, length), F32),
                pltpu.VMEM((n, 2 * KHW, length), F32),
                pltpu.VMEM((n, length, length), F32),
                pltpu.VMEM((n, 2 * KDW, length), F32),
                pltpu.VMEM((n, 2 * KHW, length), F32),
                pltpu.VMEM((QDW, length), F32),
                pltpu.VMEM((QHW, length), F32),
            ],
        ),
        compiler_params=pltpu.CompilerParams(
            dimension_semantics=("arbitrary",), vmem_limit_bytes=58 << 20
        ),
        cost_estimate=SMALL,
        name="attention_backward",
    )(scal, qfac, *facs, start, o, do, lse, cosine, sine)


def norm_of(values):
    inverse = lax.rsqrt(jnp.mean(values * values, axis=-1, keepdims=True) + EPS)
    return values * inverse, inverse


def turn(values, cosine, sine, sign):
    half = HEAD_DIM // 2
    parts = []
    for r in range(values.shape[0] // HEAD_DIM):
        first = values[r * HEAD_DIM : r * HEAD_DIM + half, :]
        second = values[r * HEAD_DIM + half : (r + 1) * HEAD_DIM, :]
        parts.append(first * cosine - sign * second * sine)
        parts.append(second * cosine + sign * first * sine)
    return jnp.concatenate(parts, axis=0)


def enter_kernel(gain_ref, cos_ref, sin_ref, *refs):
    sources, (xa_ref, qfac_ref, fac_ref) = refs[:7], refs[7:10]
    x_ref, qh, qd, kh, kd, vh, vd, sem = refs[10:]
    copies = [
        pltpu.make_async_copy(source, target, sem.at[k])
        for k, (source, target) in enumerate(zip(sources, (x_ref, qh, qd, kh, kd, vh, vd)))
    ]
    for copy in copies:
        copy.start()
    for copy in copies:
        copy.wait()
    normed = norm_of(x_ref[...].astype(F32))[0]
    xa = (normed * gain_ref[...]).astype(BF)
    xa_ref[...] = xa
    cosine, sine = cos_ref[...], sin_ref[...]
    kdims = turn(jnp.transpose(mm(xa, kd[...])), cosine, sine, 1.0)
    fac_ref[0:KDW, :] = kdims.astype(BF)
    fac_ref[KDW : 2 * KDW, :] = jnp.transpose(mm(xa, vd[...])).astype(BF)
    fac_ref[2 * KDW : 2 * KDW + KHW, :] = mm(kh[...], xa, 1, 1).astype(BF)
    fac_ref[2 * KDW + KHW :, :] = mm(vh[...], xa, 1, 1).astype(BF)
    qfac_ref[0:QHW, :] = mm(qh[...], xa, 1, 1).astype(BF)
    qdims = turn(jnp.transpose(mm(xa, qd[...])), cosine, sine, 1.0)
    qfac_ref[QHW:, :] = qdims.astype(BF)


WHOLE = pl.BlockSpec(memory_space=pltpu.VMEM)
RAW = pl.BlockSpec(memory_space=pl.ANY)
SCALAR = pl.BlockSpec(memory_space=pltpu.SMEM)
SMALL = pl.CostEstimate(flops=1000, transcendentals=0, bytes_accessed=1000)


def enter(x, gain, weights, cosine, sine):
    length, width = x.shape
    moved = (x,) + tuple(weights)
    return pl.pallas_call(
        enter_kernel,
        out_shape=(
            jax.ShapeDtypeStruct((length, width), BF),
            jax.ShapeDtypeStruct((QFW, length), BF),
            jax.ShapeDtypeStruct((FACW, length), BF),
        ),
        in_specs=[WHOLE] * 3 + [RAW] * 7,
        out_specs=[WHOLE] * 3,
        scratch_shapes=[pltpu.VMEM(v.shape, BF) for v in moved] + [pltpu.SemaphoreType.DMA((7,))],
        compiler_params=pltpu.CompilerParams(vmem_limit_bytes=40 << 20),
        name="enter",
    )(gain, cosine, sine, *moved)


def block_place(ids_ref, sizes, index, rows):
    place, scale = 0, 1
    for k in reversed(range(len(sizes))):
        place = place + ((index % sizes[k]) ^ ids_ref[k]) * scale
        index, scale = index // sizes[k], scale * sizes[k]
    return pl.multiple_of(place * rows, rows)


def deal(ids_ref, sizes, t_s, outs):
    blocks, rows = outs[0].shape[:2]
    for side in range(2):

        def one(i, carry, side=side):
            place = block_place(ids_ref, sizes, side * blocks + i, rows)
            outs[side][i] = t_s[pl.ds(place, rows), :].astype(BF)
            return carry

        lax.fori_loop(0, blocks, one, 0)


def collect(ids_ref, sizes, sources, write):
    blocks, rows = sources[0].shape[:2]
    for side in range(2):

        def one(i, carry, side=side):
            place = block_place(ids_ref, sizes, side * blocks + i, rows)
            write(pl.ds(place, rows), sources[side][i].astype(F32))
            return carry

        lax.fori_loop(0, blocks, one, 0)


def leave_out_kernel(sizes, ids_ref, o_ref, dhb_ref, kept_ref, sent_ref, t_s):
    t_s[...] = mm(jnp.transpose(o_ref[...]), dhb_ref[...])
    deal(ids_ref, sizes, t_s, (kept_ref, sent_ref))


SMALLS = 256
RESTW = 2 * KDW + QDW + SMALLS
GAINS = QHW + 2 * KHW
GAIN_COPIES = (SMALLS - GAINS) // 2


def leave_rest_kernel(
    sizes, ids_ref, x_ref, xa_ref, gain_ref, dres_ref, dq_ref, kg_ref, fgain_ref, cos_ref, sin_ref,
    qh, qd, kh, kd, vh, vd, tg_ref, kept_ref, sent_ref, out_ref
):
    normed, inverse = norm_of(x_ref[...].astype(F32))
    xa = xa_ref[...]
    g = kg_ref[...]
    dkd = turn(g[0:KDW, :], cos_ref[...], sin_ref[...], -1.0)
    d_kd = jnp.transpose(dkd).astype(BF)
    d_vd = jnp.transpose(g[KDW : 2 * KDW, :]).astype(BF)
    d_kh = jnp.transpose(g[2 * KDW : 2 * KDW + KHW, :]).astype(BF)
    d_vh = jnp.transpose(g[2 * KDW + KHW :, :]).astype(BF)
    dq = dq_ref[...].astype(F32)
    d_qh = jnp.transpose(dq[0:QHW, :]).astype(BF)
    d_qd = jnp.transpose(dq[QHW:, :]).astype(BF)
    xa_t = jnp.transpose(xa)
    out_ref[:, 0:KDW] = mm(xa_t, d_kd)
    out_ref[:, KDW : 2 * KDW] = mm(xa_t, d_vd)
    out_ref[:, 2 * KDW : 2 * KDW + QDW] = mm(xa_t, d_qd)
    dxa = mm(d_qd, qd[...], 1, 1) + mm(d_qh, qh[...])
    dxa = dxa + mm(d_kd, kd[...], 1, 1) + mm(d_vd, vd[...], 1, 1)
    dxa = dxa + mm(d_kh, kh[...]) + mm(d_vh, vh[...])
    scaled = dxa * gain_ref[...]
    mean = jnp.mean(scaled * normed, axis=-1, keepdims=True)
    tg_ref[...] = (dres_ref[...] + inverse * (scaled - normed * mean)).astype(BF)
    gain_part = jnp.sum(dxa * normed, axis=0, keepdims=True)
    low = g[2 * KDW :, :].astype(BF)
    small = [mm(dq_ref[0:QHW, :], xa), mm(low[0:KHW, :], xa), mm(low[KHW:, :], xa)]
    small += [gain_part] * GAIN_COPIES + [fgain_ref[...]] * GAIN_COPIES
    out_ref[:, 2 * KDW + QDW :] = jnp.transpose(jnp.concatenate(small, axis=0))
    deal(ids_ref, sizes, out_ref, (kept_ref, sent_ref))


def leave_out(sizes, ids, o, dhb):
    depth = o.shape[1]
    blocks = math.prod(sizes) // 2
    return pl.pallas_call(
        functools.partial(leave_out_kernel, sizes),
        out_shape=(jax.ShapeDtypeStruct((blocks, depth // (2 * blocks), depth), BF),) * 2,
        in_specs=[SCALAR] + [WHOLE] * 2,
        out_specs=[WHOLE] * 2,
        scratch_shapes=[pltpu.VMEM((depth, depth), F32)],
        compiler_params=pltpu.CompilerParams(vmem_limit_bytes=40 << 20),
        cost_estimate=SMALL,
        name="leave_out",
    )(ids, o, dhb)


def leave_rest(sizes, ids, x, xa, gain, dres, dq, kg, fgain, cosine, sine, weights):
    length, depth = x.shape
    blocks = math.prod(sizes) // 2
    return pl.pallas_call(
        functools.partial(leave_rest_kernel, sizes),
        out_shape=(jax.ShapeDtypeStruct((length, depth), BF),)
        + (jax.ShapeDtypeStruct((blocks, depth // (2 * blocks), RESTW), BF),) * 2,
        in_specs=[SCALAR] + [WHOLE] * (9 + len(weights)),
        out_specs=[WHOLE] * 3,
        scratch_shapes=[pltpu.VMEM((depth, RESTW), F32)],
        compiler_params=pltpu.CompilerParams(vmem_limit_bytes=40 << 20),
        cost_estimate=SMALL,
        name="leave_rest",
    )(ids, x, xa, gain, dres, dq, kg, fgain, cosine, sine, *weights)


def end_out_kernel(sizes, ids_ref, own_ref, got_ref, proj_ref):
    def write(rows, v):
        proj_ref[rows, :] = v

    collect(ids_ref, sizes, (own_ref, got_ref), write)


def end_out(sizes, ids, own, got):
    depth = own.shape[0] * own.shape[1] * 2
    return pl.pallas_call(
        functools.partial(end_out_kernel, sizes),
        out_shape=jax.ShapeDtypeStruct((depth, depth), F32),
        in_specs=[SCALAR] + [WHOLE] * 2,
        out_specs=WHOLE,
        compiler_params=pltpu.CompilerParams(vmem_limit_bytes=40 << 20),
        cost_estimate=SMALL,
        name="end_out",
    )(ids, own, got)


def end_rest_kernel(
    sizes, ids_ref, own_ref, got_ref, kd_ref, vd_ref, qd_ref, qh_ref, kh_ref, vh_ref, a_ref, f_ref, t_s
):
    def write(rows, v):
        kd_ref[rows, :] = v[:, 0:KDW]
        vd_ref[rows, :] = v[:, KDW : 2 * KDW]
        qd_ref[rows, :] = v[:, 2 * KDW : 2 * KDW + QDW]
        t_s[rows, :] = v[:, 2 * KDW + QDW :]

    collect(ids_ref, sizes, (own_ref, got_ref), write)
    turned = jnp.transpose(t_s[...])
    qh_ref[...] = turned[0:QHW, :]
    kh_ref[...] = turned[QHW : QHW + KHW, :]
    vh_ref[...] = turned[QHW + KHW : GAINS, :]
    a_ref[...] = turned[GAINS : GAINS + 1, :]
    f_ref[...] = turned[GAINS + GAIN_COPIES : GAINS + GAIN_COPIES + 1, :]


def end_rest(sizes, ids, own, got):
    depth = own.shape[0] * own.shape[1] * 2
    shapes = [(depth, KDW), (depth, KDW), (depth, QDW), (QHW, depth), (KHW, depth), (KHW, depth)]
    shapes += [(1, depth), (1, depth)]
    return pl.pallas_call(
        functools.partial(end_rest_kernel, sizes),
        out_shape=tuple(jax.ShapeDtypeStruct(v, F32) for v in shapes),
        in_specs=[SCALAR] + [WHOLE] * 2,
        out_specs=[WHOLE] * 8,
        scratch_shapes=[pltpu.VMEM((depth, SMALLS), F32)],
        compiler_params=pltpu.CompilerParams(vmem_limit_bytes=40 << 20),
        name="end_rest",
    )(ids, own, got)


def after(v, *others):
    return lax.optimization_barrier((v,) + others)[0]


class Grid:
    def __init__(self, dp, tensor):
        self.c = 2
        self.y = dp // 2
        self.x = self.y if tensor % self.y == 0 else 1
        self.z = tensor // self.x
        self.dp, self.tensor = dp, tensor
        self.axes = {
            "c": ("dp", 1, self.c),
            "y": ("dp", self.c, self.y),
            "x": ("tensor", 1, self.x),
            "z": ("tensor", self.x, self.z),
        }

    def size(self, g):
        return self.axes[g][2]

    def place(self, g):
        axis, stride, size = self.axes[g]
        return ((lax.axis_index(axis) // stride) % size).astype(jnp.int32)

    def swap(self, v, g, r):
        axis, stride, size = self.axes[g]
        total = self.dp if axis == "dp" else self.tensor
        return lax.ppermute(v, axis, [(i, i ^ (r * stride)) for i in range(total)])

    def bits(self, g):
        return [1 << k for k in range(self.size(g).bit_length() - 1)]

    def rels(self, g):
        order = [0]
        for bit in reversed(self.bits(g)):
            order = order + [r ^ bit for r in order]
        return order

    def stack(self, v, g):
        v = v[None]
        for bit in reversed(self.bits(g)):
            v = jnp.concatenate([v, self.swap(v, g, bit)], axis=0)
        return v

    def unstack(self, v, g, last=BF):
        bits = self.bits(g)
        for k, bit in enumerate(bits):
            rows = v.shape[0] // 2
            got = self.swap(v[rows:].astype(BF), g, bit)
            v = v[:rows].astype(F32) + got.astype(F32)
        return v[0].astype(last)

    def direct(self, v, g):
        return [v] + [self.swap(v, g, r) for r in self.rels(g)[1:]]

    def swap_masks(self, v, dp_mask, tensor_mask):
        if not tensor_mask:
            return lax.ppermute(v, "dp", [(i, i ^ dp_mask) for i in range(self.dp)])
        if not dp_mask:
            return lax.ppermute(v, "tensor", [(i, i ^ tensor_mask) for i in range(self.tensor)])
        mask = dp_mask * self.tensor + tensor_mask
        pairs = [(i, i ^ mask) for i in range(self.dp * self.tensor)]
        return lax.ppermute(v, ("dp", "tensor"), pairs)

    def levels(self, plan):
        out = []
        for letters in plan:
            masks = [(0, 0)]
            for g in letters:
                axis, stride, size = self.axes[g]
                masks = [
                    (d + r * stride, t) if axis == "dp" else (d, t + r * stride)
                    for d, t in masks
                    for r in range(size)
                ]
            out.append(masks)
        return out

    def numbers(self, plan):
        out = []
        for letters in plan:
            number = jnp.int32(0)
            for g in letters:
                number = number * self.size(g) + self.place(g)
            out.append(number)
        return jnp.stack(out)

    def swaps(self, low, masks):
        return [self.swap_masks(low[m], *masks[m]) for m in range(1, len(masks))]

    def swaps_whole(self, low, masks):
        return [self.swap_masks(low, *m) for m in masks[1:]]


def ffn_kernel(parts, plan, shards, blend, scal_ref, xf_ref, dy_ref, *refs):
    own, arrays = plan
    count = (3 if own else 0) + len(arrays)
    sources, refs = refs[:count], refs[count:]
    if blend:
        mixed_in, dxf_in = refs[:2]
        refs = refs[2:]
    mixed_ref, dxf_ref, inner_ref, dgate_ref, dup_ref, w_s, sem = refs
    width = w_s.shape[2]
    rows = w_s.shape[3] // parts
    copies = []

    def move(source, target):
        copies.append(pltpu.make_async_copy(source, target, sem.at[len(copies)]))

    if own:
        for k in range(3):
            move(sources[k], w_s.at[k, 0])
    for (slots, q), source in zip(arrays, sources[3 if own else 0 :]):
        place = pl.multiple_of((scal_ref[0] ^ q) * rows, rows)
        for i, slot in enumerate(slots):
            move(source.at[i], w_s.at[:, slot, :, pl.ds(place, rows)])
    for copy in copies:
        copy.start()
    for copy in copies:
        copy.wait()
    xf, dy = xf_ref[...], dy_ref[...]
    units, unused, hidden = inner_ref.shape
    for s in range(units):
        wg, wu, wd = ((w_s[k] if units == 1 else w_s[k, s]).reshape(hidden, -1) for k in range(3))
        gate = mm(xf, wg, 1, 1)
        up = mm(xf, wu, 1, 1)
        d_inner = mm(dy, wd, 1, 1)
        sig = 1.0 / (1.0 + jnp.exp(-gate))
        act = gate * sig
        inner = (act * up).astype(BF)
        d_gate = (d_inner * up * sig * (1.0 + gate * (1.0 - sig))).astype(BF)
        d_up = (d_inner * act).astype(BF)
        inner_ref[s] = inner
        dgate_ref[s] = d_gate
        dup_ref[s] = d_up
        dxf = mm(d_gate, wg) + mm(d_up, wu)
        mixed = mm(inner, wd)
        if s == 0 and blend:
            dxf, mixed = dxf + dxf_in[...], mixed + mixed_in[...]
        if s > 0:
            dxf, mixed = dxf + total[0], mixed + total[1]
        total = (dxf, mixed)
    dxf_ref[...] = total[0].astype(dxf_ref.dtype)
    mixed_ref[...] = total[1].astype(mixed_ref.dtype)


def ffn(mine, xf, dy, own, arrays, parts, width, before, out_type, name):
    length, depth = xf.shape
    shards = (1 if own else 0) + sum(len(slots) for slots, q, v in arrays if q == 0)
    hidden = (1, length, shards * width) if width % 16 == 0 else (shards, length, width)
    plan = (bool(own), [(slots, q) for slots, q, v in arrays])
    sources = list(own) + [v for slots, q, v in arrays]
    moves = (3 if own else 0) + sum(len(slots) for slots, q, v in arrays)
    return pl.pallas_call(
        functools.partial(ffn_kernel, parts, plan, shards, bool(before)),
        out_shape=(jax.ShapeDtypeStruct((length, depth), out_type),) * 2
        + (jax.ShapeDtypeStruct(hidden, BF),) * 3,
        in_specs=[SCALAR, WHOLE, WHOLE] + [RAW] * len(sources) + [WHOLE] * len(before),
        out_specs=[WHOLE] * 5,
        scratch_shapes=[
            pltpu.VMEM((3, shards, width, depth), BF),
            pltpu.SemaphoreType.DMA((moves,)),
        ],
        compiler_params=pltpu.CompilerParams(vmem_limit_bytes=58 << 20),
        cost_estimate=SMALL,
        name=name,
    )(mine, xf, dy, *sources, *before)


def products(lefts, rights, width, write):
    slot = 0
    for group in range(len(lefts[0])):
        units, unused, hidden = lefts[0][group].shape
        for s in range(units):
            total = None
            for b in range(len(rights)):
                term = mm(jnp.transpose(lefts[b][group][s]), rights[b][...])
                total = term if total is None else total + term
            for i in range(hidden // width):
                write(slot, total[i * width : (i + 1) * width, :])
                slot += 1


def divide(refs, blocks):
    each = len(refs) // blocks
    return [refs[b * each : (b + 1) * each] for b in range(blocks)]


def store(outs, scal_ref, t_s, slot, first, value):
    rows, lanes = value.shape[0], outs[0].shape[3]
    t_s[0:rows, :] = value
    for q in range(2 * outs[0].shape[0]):
        place = pl.multiple_of((scal_ref[0] ^ q) * lanes, lanes)
        part = t_s[0:rows, pl.ds(place, lanes)]
        outs[q % 2][q // 2, slot, first : first + rows, :] = part.astype(BF)


def gate_up_kernel(blocks, scal_ref, *refs):
    xfs, outs, t_s = refs[:blocks], refs[-3:-1], refs[-1]
    rest = refs[blocks:-3]
    width = outs[0].shape[2] // 2
    for k in range(2):
        lefts = divide(rest[k * len(rest) // 2 : (k + 1) * len(rest) // 2], blocks)

        def write(slot, value, k=k):
            store(outs, scal_ref, t_s, slot, k * width, value)

        products(lefts, xfs, width, write)


def down_kernel(blocks, scal_ref, *refs):
    dys, outs, t_s = refs[:blocks], refs[-3:-1], refs[-1]
    width = outs[0].shape[2]

    def write(slot, value):
        store(outs, scal_ref, t_s, slot, 0, value)

    products(divide(refs[blocks:-3], blocks), dys, width, write)


def grads(kernel, mine, wholes, parts, zs, rows, depth, scratch, name):
    return pl.pallas_call(
        kernel,
        out_shape=(jax.ShapeDtypeStruct((parts // 2, zs, rows, depth // parts), BF),) * 2,
        in_specs=[SCALAR] + [WHOLE] * len(wholes),
        out_specs=[WHOLE] * 2,
        scratch_shapes=scratch,
        compiler_params=pltpu.CompilerParams(vmem_limit_bytes=58 << 20),
        cost_estimate=SMALL,
        name=name,
    )(mine, *wholes)


def unpack_kernel(scal_ref, own_ref, got_ref, gate_ref, up_ref, down_ref):
    width = gate_ref.shape[0]
    for side, ref in enumerate((own_ref, got_ref)):

        @pl.when(pl.program_id(0) % 2 == side)
        def _(ref=ref):
            gate_ref[...] = ref[0, 0:width, :].astype(F32)
            up_ref[...] = ref[0, width : 2 * width, :].astype(F32)
            down_ref[...] = ref[0, 2 * width :, :].astype(F32)


def unpack(mine, own, got):
    half, rows, lanes = own.shape
    width, parts = rows // 3, 2 * half
    column = pl.BlockSpec((width, lanes), lambda q, s: (0, s[0] ^ q))
    return pl.pallas_call(
        unpack_kernel,
        out_shape=(jax.ShapeDtypeStruct((width, parts * lanes), F32),) * 3,
        grid_spec=pltpu.PrefetchScalarGridSpec(
            num_scalar_prefetch=1,
            grid=(parts,),
            in_specs=[pl.BlockSpec((1, rows, lanes), lambda q, s: (q // 2, 0, 0))] * 2,
            out_specs=[column] * 3,
        ),
        compiler_params=pltpu.CompilerParams(dimension_semantics=("arbitrary",)),
        cost_estimate=SMALL,
        name="unpack",
    )(mine, own, got)


def spread_pieces(grid, got, tie):
    entries = []
    for k in range(grid.y):
        piece = got if k == 0 else grid.swap(got, "y", k)
        entries.append((2 * k, piece))
    return [
        pair
        for q, piece in entries
        for pair in ((q, piece), (q + 1, grid.swap(after(piece, tie), "c", 1)))
    ]


def reduce_core(grid, even, odd):
    got = grid.swap(odd, "c", 1)
    goes = [
        (even[k].astype(F32) + got[k].astype(F32)).astype(BF) for k in range(1, grid.y)
    ]
    return (even[0], got[0]), goes


def total_of(*terms):
    total = terms[0].astype(F32)
    for term in terms[1:]:
        total = total + term.astype(F32)
    return total


def contract(left, right, left_dim, right_dim):
    return lax.dot_general(
        left, right, (((left_dim,), (right_dim,)), ((), ())), preferred_element_type=jnp.float32
    )


def norm_back(grad_out, normed, inverse, gain):
    scaled = grad_out * gain
    gain_part = jnp.sum(grad_out * normed, axis=0)
    grad_in = inverse * (scaled - normed * jnp.mean(scaled * normed, axis=-1, keepdims=True))
    return (grad_in, gain_part)


def body(
    grid,
    tokens,
    cotangent,
    segments,
    positions,
    attngain,
    ffngain,
    queryheads,
    querydims,
    keyheads,
    keydims,
    valueheads,
    valuedims,
    outproj,
    gateproj,
    upproj,
    downproj,
):
    x = tokens[0]
    upstream = cotangent[0]
    length, depth = x.shape
    parts = grid.dp
    lanes = depth // parts
    me = lax.axis_index("tensor").astype(jnp.int32)
    spot = jnp.stack([lax.axis_index("dp").astype(jnp.int32), grid.place("z")])
    offset = me * length
    places = lax.dynamic_slice_in_dim(positions[0], offset, length)
    half = HEAD_DIM // 2
    freqs = 10000.0 ** (-jnp.arange(half, dtype=F32) * 2.0 / HEAD_DIM)
    angles = freqs[:, None] * places.astype(F32)[None, :]
    cosine, sine = jnp.cos(angles), jnp.sin(angles)
    start = (offset + jnp.arange(length, dtype=jnp.int32) - places)[:, None]
    scal = jnp.stack([jnp.maximum(offset - places[0], 0) // length, me]).astype(jnp.int32)
    weights = (queryheads.T, querydims, keyheads.T, keydims, valueheads.T, valuedims)

    own = (gateproj.T, upproj.T, downproj)
    width = downproj.shape[0]
    payload = jnp.stack(
        [lax.dynamic_slice_in_dim(v, spot[0] * lanes, lanes, 1) for v in own]
    )
    dys = [upstream] + [grid.swap(upstream, "x", r) for r in range(1, grid.x)]
    far = grid.bits("z")[::-1]
    held, rels = payload[None], [0]

    xa, qfac, fac = enter(x, attngain[None, :], weights, cosine, sine)
    near = jnp.stack(grid.direct(fac, "z"))
    held = after(held, near)
    arrived = [grid.swap(held, "z", far[0])] if far else []
    facs = [near] + [grid.swap(near, "x", r) for r in range(1, grid.x)]
    stages = []
    for k, bit in enumerate(far):
        got = arrived[k]
        new = [r ^ bit for r in rels]
        if k + 1 < len(far):
            held = jnp.concatenate([held, got], axis=0)
            arrived.append(grid.swap(held, "z", far[k + 1]))
        rels = rels + new
        stages.append((new, got))
    qfac = after(qfac, held, *dys[1:])
    attn_out, lse = attention_forward(scal, qfac, facs, start)
    stages = [
        [
            (new, q, v)
            for q, v in spread_pieces(
                grid, after(got, attn_out) if k == len(stages) - 1 else got, attn_out
            )
        ]
        for k, (new, got) in enumerate(stages)
    ]

    local = x.astype(F32)
    residual = local + jnp.dot(attn_out, outproj, preferred_element_type=jnp.float32)
    inverse_two = lax.rsqrt(jnp.mean(residual * residual, axis=-1, keepdims=True) + EPS)
    normed_two = residual * inverse_two
    input_two = (normed_two * ffngain).astype(jnp.bfloat16)
    xfs = [input_two] + [grid.swap(input_two, "x", r) for r in range(1, grid.x)]

    early, late, filled = [], [], 1
    for entries in stages[:-1]:
        for rels, q, v in entries:
            early.append(([filled + i for i in range(len(rels))], q, v))
        filled += len(entries[0][0])
    for rels, q, v in stages[-1] if stages else []:
        late.append((list(range(len(rels))), q, v))


    results = [None] * grid.x
    firsts = []
    for k in range(grid.x):
        kind = BF if k and not late else F32
        if k:
            xfs[k] = after(xfs[k], firsts[0][0])
        firsts.append(
            ffn(spot, xfs[k], dys[k], own, early, parts, width, (), kind, "ffn_early")
        )
    for k in reversed(range(grid.x)):
        first = firsts[k]
        if late:
            second = ffn(
                spot, xfs[k], dys[k], (), late, parts, width, first[:2], BF if k else F32, "ffn_late"
            )
            results[k] = (second[0], second[1]) + tuple(
                [first[i], second[i]] for i in range(2, 5)
            )
        else:
            results[k] = (first[0], first[1]) + tuple([first[i]] for i in range(2, 5))
    d_norm_two, ffn_out = results[0][1], results[0][0]
    inners, dgates, dups = (
        [v for k in range(grid.x) for v in results[k][i]] for i in range(2, 5)
    )
    first_parts = grads(
        functools.partial(gate_up_kernel, grid.x),
        spot, xfs + dgates + dups, parts, grid.z, 2 * width, depth,
        [pltpu.VMEM((width, depth), F32)], "gate_up_grads",
    )
    second_parts = grads(
        functools.partial(down_kernel, grid.x),
        spot, dys + inners, parts, grid.z, width, depth,
        [pltpu.VMEM((width, depth), F32)], "down_grads",
    )
    first_kept, first_goes = reduce_core(grid, *first_parts)
    for r in range(1, grid.x):
        got = grid.swap(results[r][1], "x", r)
        d_norm_two = d_norm_two + after(got, second_parts[0], first_goes[0]).astype(F32)
    grad_through, ffngain_part = norm_back(d_norm_two, normed_two, inverse_two, ffngain)
    d_residual = upstream.astype(jnp.float32) + grad_through
    d_res_low = d_residual.astype(jnp.bfloat16)
    d_attended = contract(d_res_low, outproj, 1, 1).astype(jnp.bfloat16)

    plan, z_masks = ("c", "xy", "z"), grid.levels(("z",))[0]
    split_z = depth // (parts * grid.tensor) >= 16
    if not split_z:
        plan = ("c", "xy")
    levels = grid.levels(plan)
    core_masks, xy_masks = levels[0], levels[1]
    sizes = tuple(len(masks) for masks in levels)
    ids = grid.numbers(plan)
    shape = sizes[1:] + (depth // math.prod(sizes), -1)

    def along_z(v):
        low = v.astype(BF)
        if split_z:
            return total_of(v[0], *grid.swaps(low, z_masks)).astype(BF)
        return total_of(v, *grid.swaps_whole(low, z_masks)).astype(BF)

    def share_z(v):
        return jnp.stack([v] + grid.swaps_whole(v, z_masks)) if split_z else v

    second_kept, second_goes = reduce_core(grid, *second_parts)
    kept, sent = leave_out(sizes, ids, attn_out, d_res_low)
    out_sum = total_of(
        kept.reshape(shape), grid.swap_masks(sent.reshape(shape), *core_masks[1])
    )
    out_low = out_sum.astype(BF)
    d_attended = after(d_attended, first_goes[-1], second_goes[-1], out_low)
    back = attention_backward(
        scal, qfac, facs, start, attn_out, d_attended, lse, cosine, sine
    )
    terms, dq = list(back[:-1]), back[-1]

    first_got = [grid.swap(v, "y", k + 1) for k, v in enumerate(first_goes)]
    second_got = [grid.swap(v, "y", k + 1) for k, v in enumerate(second_goes)]
    out_got = grid.swaps(out_low, xy_masks)
    out_first = after(out_sum[0], dq)
    first_kept = (after(first_kept[0], dq), first_kept[1])
    second_kept = (after(second_kept[0], dq), second_kept[1])
    terms[1:] = [after(v, *second_got) for v in terms[1:]]
    out_mine = along_z(total_of(out_first, *out_got))
    out_mine = share_z(out_mine)
    near = terms[0].astype(F32)
    for r in range(1, grid.x):
        near = near + grid.swap(terms[r], "x", r).astype(F32)
    ffn_sum = jnp.concatenate(
        [total_of(*first_kept, *first_got), total_of(*second_kept, *second_got)], axis=1
    )
    low = after(near.astype(BF), out_mine, *first_got)
    key_grads = near[0]
    for i, r in enumerate(grid.rels("z")):
        if i:
            key_grads = key_grads + grid.swap(low[i], "z", r).astype(F32)
    for k, bit in enumerate(grid.bits("z")):
        rows = ffn_sum.shape[0] // 2
        goes = ffn_sum[rows:].astype(BF)
        if k == 0:
            goes = after(goes, key_grads)
        got = grid.swap(goes, "z", bit)
        if k == 0:
            first_z = got
        ffn_sum = ffn_sum[:rows] + got.astype(F32)
    out_mine = after(out_mine, key_grads)
    out_others = grid.swaps_whole(out_mine, xy_masks)
    out_own = jnp.stack([out_mine] + out_others)
    out_other = grid.swap_masks(out_own, *core_masks[1])

    def flat(v):
        return v.reshape(math.prod(sizes) // 2, -1, v.shape[-1])

    out_part = end_out(sizes, ids, flat(out_own), flat(out_other))
    tokens_grad, kept, sent = leave_rest(
        sizes, ids, x, xa, attngain[None, :], d_residual, dq, key_grads, ffngain_part[None, :],
        cosine, sine, weights,
    )
    rest = total_of(kept.reshape(shape), grid.swap_masks(sent.reshape(shape), *core_masks[1]))
    low = after(rest.astype(BF), *out_others)
    rest = total_of(rest[0], *grid.swaps(low, xy_masks))
    rest = after(rest, first_z)

    ffn_got = [grid.swap(after(results[r][0], rest), "x", r) for r in range(1, grid.x)]
    mixed = (residual + total_of(ffn_out, *ffn_got)).astype(jnp.bfloat16)

    rest = along_z(rest)
    mine = after(ffn_sum[0].astype(BF), rest)
    rest = after(share_z(rest), *ffn_got)
    rest = jnp.stack([rest] + grid.swaps_whole(rest, xy_masks))
    rest = after(rest, out_part)
    others = grid.swap_masks(rest, *core_masks[1])
    mine = jnp.stack([mine] + [grid.swap(mine, "y", k) for k in range(1, grid.y)])
    gate_part, up_part, down_part = unpack(spot, mine, grid.swap(mine, "c", 1))

    kd_grad, vd_grad, qd_grad, qh_grad, kh_grad, vh_grad, again_grad, fgain_grad = end_rest(
        sizes, ids, after(flat(rest), down_part), flat(others)
    )
    return (
        mixed[None],
        tokens_grad[None],
        again_grad[0],
        fgain_grad[0],
        qh_grad.T,
        qd_grad,
        kh_grad.T,
        kd_grad,
        vh_grad.T,
        vd_grad,
        out_part,
        gate_part.T,
        up_part.T,
        down_part,
    )


def solution(mesh):
    grid = Grid(mesh.shape["dp"], mesh.shape["tensor"])
    rows = P("dp", "tensor", None)
    placed = (rows, rows, P("dp", None), P("dp", None)) + (P(),) * 9
    halves = (P(None, "tensor"), P(None, "tensor"), P("tensor", None))
    return jax.shard_map(
        functools.partial(body, grid),
        mesh=mesh,
        in_specs=placed + halves,
        out_specs=(rows, rows) + (P(),) * 9 + halves,
        check_vma=False,
    )
```

```python
import functools
import math

import jax
import jax.numpy as jnp
from jax import lax
from jax.experimental import pallas as pl
from jax.experimental.pallas import tpu as pltpu

from jax.sharding import PartitionSpec as P

HEADS = 16
HEAD_DIM = 64
QRANK = 6
KRANK = 2
PAIRS = HEADS // 2
QHW = HEADS * QRANK
QDW = QRANK * HEAD_DIM
KDW = KRANK * HEAD_DIM
KHW = HEADS * KRANK
FACW = 2 * KDW + 2 * KHW
QFW = QHW + QDW
LOG2E = 1.4426950408889634
EPS = 1e-06
BF = jnp.bfloat16
F32 = jnp.float32


def mm(a, b, ca=1, cb=0):
    return lax.dot_general(a, b, (((ca,), (cb,)), ((), ())), preferred_element_type=F32)


def expand_pair(bk0, bk1, rows):
    first = rows[0] * bk0 + rows[1] * bk1
    second = rows[2] * bk0 + rows[3] * bk1
    return jnp.concatenate([first, second], axis=0) * (1.0 / KRANK)


def query_pair(qfac_ref, aq_s, pair):
    halves = []
    for h in range(2):
        acc = None
        for r in range(QRANK):
            row = aq_s[pl.ds(pair * (2 * QRANK) + h * QRANK + r, 1), :]
            term = row * qfac_ref[QHW + r * HEAD_DIM : QHW + (r + 1) * HEAD_DIM, :].astype(F32)
            acc = term if acc is None else acc + term
        halves.append(acc * (1.0 / QRANK))
    return jnp.concatenate(halves, axis=0).astype(BF)


def reverse_bits(r, size):
    total, bits = 0, size.bit_length() - 1
    for k in range(bits):
        total = total + (((r >> k) & 1) << (bits - 1 - k))
    return total


def fill_tables(scal_ref, qfac_ref, fac_refs, start_ref, fac_s, aq_s, kv_s, bias_s):
    length = qfac_ref.shape[1]
    me = scal_ref[1]
    across = len(fac_refs)
    aq_s[...] = qfac_ref[0:QHW, :].astype(F32)
    row = lax.broadcasted_iota(jnp.int32, (length, length), 0) + me * length
    column = lax.broadcasted_iota(jnp.int32, (length, length), 1)
    begin = start_ref[...]

    def fill(c, carry):
        for k, ref in enumerate(fac_refs):

            @pl.when(((c ^ me) % across) == k)
            def _(ref=ref):
                piece = ref[reverse_bits((c ^ me) // across, ref.shape[0])]
                fac_s[c] = piece[0 : 2 * KDW, :]
                kv_s[c] = piece[2 * KDW :, :].astype(F32)

        key = column + c * length
        keep = (key >= begin) & (key <= row)
        bias_s[c] = jnp.where(keep, 0.0, -1e30)
        return carry

    lax.fori_loop(scal_ref[0], me + 1, fill, 0)


def key_pair(fac_ref, kv_s, c, pair, which):
    base = which * KDW
    b0 = fac_ref[c, base : base + HEAD_DIM, :].astype(F32)
    b1 = fac_ref[c, base + HEAD_DIM : base + 2 * HEAD_DIM, :].astype(F32)
    rows = [kv_s[c, pl.ds(which * KHW + pair * 4 + j, 1), :] for j in range(4)]
    return expand_pair(b0, b1, rows), b0, b1, rows


def forward_kernel(across, scal_ref, qfac_ref, *refs):
    fac_refs, start_ref = refs[:across], refs[across]
    o_ref, lse_ref, fac_ref, aq_s, kv_s, bias_s, s_s = refs[across + 1 :]
    pair = pl.program_id(0)
    length = qfac_ref.shape[1]
    lo, me = scal_ref[0], scal_ref[1]

    @pl.when(pair == 0)
    def _():
        fill_tables(scal_ref, qfac_ref, fac_refs, start_ref, fac_ref, aq_s, kv_s, bias_s)

    query = jnp.transpose(query_pair(qfac_ref, aq_s, pair).astype(F32)) * (HEAD_DIM**-0.5)
    low_half = lax.broadcasted_iota(jnp.int32, (length, 2 * HEAD_DIM), 1) < HEAD_DIM
    queries = [
        jnp.where(low_half, query, 0.0).astype(BF),
        jnp.where(low_half, 0.0, query).astype(BF),
    ]
    lanes = 128
    pieces = length // lanes

    def score(c, tops):
        keys = key_pair(fac_ref, kv_s, c, pair, 0)[0].astype(BF)
        bias = bias_s[c]
        new = []
        for h in range(2):
            s = mm(queries[h], keys) * LOG2E + bias
            s_s[h, c] = s
            top = tops[h]
            for i in range(pieces):
                top = jnp.maximum(top, s[:, i * lanes : (i + 1) * lanes])
            new.append(top)
        return tuple(new)

    start = jnp.full((length, lanes), -1e30, F32)
    tops = lax.fori_loop(lo, me + 1, score, (start, start))
    tops = [jnp.max(top, axis=1, keepdims=True) for top in tops]

    def value(c, carry):
        values = key_pair(fac_ref, kv_s, c, pair, 1)[0].astype(BF)
        new = []
        for h in range(2):
            p = jnp.exp2(s_s[h, c] - tops[h])
            total = carry[2 * h]
            for i in range(pieces):
                total = total + p[:, i * lanes : (i + 1) * lanes]
            new += [total, carry[2 * h + 1] + mm(p.astype(BF), values, 1, 1)]
        return tuple(new)

    zero = jnp.zeros((length, lanes), F32)
    wide = jnp.zeros((length, 2 * HEAD_DIM), F32)
    done = lax.fori_loop(lo, me + 1, value, (zero, wide, zero, wide))
    outs = []
    for h in range(2):
        total = jnp.sum(done[2 * h], axis=1, keepdims=True)
        outs.append(done[2 * h + 1] / total)
        lse_ref[h] = jnp.broadcast_to(tops[h] + jnp.log2(total), (length, lanes))
    o_ref[...] = jnp.where(low_half, outs[0], outs[1]).astype(BF)


def full(shape):
    return pl.BlockSpec(shape, lambda p, s: (0,) * len(shape))


def attention_forward(scal, qfac, facs, start):
    length = qfac.shape[1]
    n = facs[0].shape[0] * len(facs)
    return pl.pallas_call(
        functools.partial(forward_kernel, len(facs)),
        out_shape=(
            jax.ShapeDtypeStruct((length, HEADS * HEAD_DIM), BF),
            jax.ShapeDtypeStruct((HEADS, length, 128), F32),
        ),
        grid_spec=pltpu.PrefetchScalarGridSpec(
            num_scalar_prefetch=1,
            grid=(PAIRS,),
            in_specs=[full(qfac.shape)] + [full(v.shape) for v in facs] + [full(start.shape)],
            out_specs=[
                pl.BlockSpec((length, 2 * HEAD_DIM), lambda p, s: (0, p)),
                pl.BlockSpec((2, length, 128), lambda p, s: (p, 0, 0)),
            ],
            scratch_shapes=[
                pltpu.VMEM((n, 2 * KDW, length), BF),
                pltpu.VMEM((QHW, length), F32),
                pltpu.VMEM((n, 2 * KHW, length), F32),
                pltpu.VMEM((n, length, length), F32),
                pltpu.VMEM((2, n, length, length), F32),
            ],
        ),
        compiler_params=pltpu.CompilerParams(
            dimension_semantics=("arbitrary",), vmem_limit_bytes=58 << 20
        ),
        cost_estimate=SMALL,
        name="attention_forward",
    )(scal, qfac, *facs, start)


def backward_kernel(across, scal_ref, qfac_ref, *refs):
    fac_refs = refs[:across]
    start_ref, o_ref, do_ref, lse_ref, cos_ref, sin_ref = refs[across : across + 6]
    terms_refs = refs[across + 6 : 2 * across + 6]
    dq_ref, fac_ref, aq_s, kv_s, bias_s, acc_s, heads_s, dbq_s, daq_s = refs[2 * across + 6 :]
    pair = pl.program_id(0)
    length = qfac_ref.shape[1]
    n = fac_ref.shape[0]
    lo, me = scal_ref[0], scal_ref[1]
    pieces = length // 128

    @pl.when(pair == 0)
    def _():
        fill_tables(scal_ref, qfac_ref, fac_refs, start_ref, fac_ref, aq_s, kv_s, bias_s)
        dbq_s[...] = jnp.zeros_like(dbq_s)

        def clear(c, carry):
            acc_s[c] = jnp.zeros((2 * KDW, length), F32)
            return carry

        lax.fori_loop(lo, me + 1, clear, 0)

    query_t = query_pair(qfac_ref, aq_s, pair).astype(F32) * (HEAD_DIM**-0.5)
    query = jnp.transpose(query_t)
    query_t = query_t.astype(BF)
    do = do_ref[...].astype(F32)
    do_t = jnp.transpose(do).astype(BF)
    low_half = lax.broadcasted_iota(jnp.int32, (length, 2 * HEAD_DIM), 1) < HEAD_DIM
    product = do * o_ref[...].astype(F32)
    queries, grads, deltas, stats = [], [], [], []
    for h in range(2):
        keep = low_half if h == 0 else jnp.logical_not(low_half)
        queries.append(jnp.where(keep, query, 0.0).astype(BF))
        grads.append(jnp.where(keep, do, 0.0).astype(BF))
        deltas.append(jnp.sum(jnp.where(keep, product, 0.0), axis=1, keepdims=True))
        stats.append(lse_ref[h])

    def step(c, dqs):
        keys, kb0, kb1, krows = key_pair(fac_ref, kv_s, c, pair, 0)
        values, vb0, vb1, vrows = key_pair(fac_ref, kv_s, c, pair, 1)
        keys, values = keys.astype(BF), values.astype(BF)
        bias = bias_s[c]
        new, sums, rows = [], [None] * 4, []
        for h in range(2):
            s = mm(queries[h], keys) * LOG2E + bias
            lse = jnp.concatenate([stats[h]] * pieces, axis=1)
            p = jnp.exp2(s - lse)
            dp = mm(grads[h], values)
            ds = (p * (dp - deltas[h])).astype(BF)
            pb = p.astype(BF)
            new.append(dqs[h] + mm(ds, keys, 1, 1))
            half = slice(h * HEAD_DIM, (h + 1) * HEAD_DIM)
            dk = mm(query_t[half, :], ds)
            dv = mm(do_t[half, :], pb)
            for which, d, b0, b1, a in ((0, dk, kb0, kb1, krows), (1, dv, vb0, vb1, vrows)):
                for r, b in ((0, b0), (1, b1)):
                    term = d * a[2 * h + r]
                    k = 2 * which + r
                    sums[k] = term if sums[k] is None else sums[k] + term
                    rows.append((which * 4 + 2 * h + r, jnp.sum(d * b, axis=0, keepdims=True)))
        for k in range(4):
            part = slice(k * HEAD_DIM, (k + 1) * HEAD_DIM)
            acc_s[c, part, :] = acc_s[c, part, :] + sums[k]
        for k, row in rows:
            where = (k // 4) * KHW + pair * 4 + k % 4
            heads_s[c, pl.ds(where, 1), :] = row
        return tuple(new)

    zero = jnp.zeros((length, 2 * HEAD_DIM), F32)
    dqs = lax.fori_loop(lo, me + 1, step, (zero, zero))
    dq_t = jnp.transpose(jnp.where(low_half, dqs[0], dqs[1])) * (HEAD_DIM**-0.5 / QRANK)
    for h in range(2):
        d = dq_t[h * HEAD_DIM : (h + 1) * HEAD_DIM, :]
        for r in range(QRANK):
            part = slice(r * HEAD_DIM, (r + 1) * HEAD_DIM)
            b = qfac_ref[QHW + r * HEAD_DIM : QHW + (r + 1) * HEAD_DIM, :].astype(F32)
            k = pl.ds(pair * (2 * QRANK) + h * QRANK + r, 1)
            daq_s[k, :] = jnp.sum(d * b, axis=0, keepdims=True)
            dbq_s[part, :] = dbq_s[part, :] + d * aq_s[k, :]

    @pl.when(pair == PAIRS - 1)
    def _():
        cosine, sine = cos_ref[...], sin_ref[...]
        half = HEAD_DIM // 2
        dq_ref[0:QHW, :] = daq_s[...].astype(BF)
        for r in range(QRANK):
            first = dbq_s[r * HEAD_DIM : r * HEAD_DIM + half, :]
            second = dbq_s[r * HEAD_DIM + half : (r + 1) * HEAD_DIM, :]
            turned = jnp.concatenate(
                [first * cosine + second * sine, second * cosine - first * sine], axis=0
            )
            dq_ref[QHW + r * HEAD_DIM : QHW + (r + 1) * HEAD_DIM, :] = turned.astype(BF)

        def flush(c, carry):
            inside = (c >= lo) & (c <= me)
            for k, ref in enumerate(terms_refs):

                @pl.when(inside & (((c ^ me) % across) == k))
                def _(ref=ref):
                    place = reverse_bits((c ^ me) // across, ref.shape[0])
                    ref[place, 0 : 2 * KDW, :] = (acc_s[c] * (1.0 / KRANK)).astype(BF)
                    ref[place, 2 * KDW :, :] = (heads_s[c] * (1.0 / KRANK)).astype(BF)

                @pl.when(jnp.logical_not(inside) & (((c ^ me) % across) == k))
                def _(ref=ref):
                    ref[reverse_bits((c ^ me) // across, ref.shape[0])] = jnp.zeros((FACW, length), BF)

            return carry

        lax.fori_loop(0, n, flush, 0)


def attention_backward(scal, qfac, facs, start, o, do, lse, cosine, sine):
    length = qfac.shape[1]
    across, along = len(facs), facs[0].shape[0]
    n = across * along
    return pl.pallas_call(
        functools.partial(backward_kernel, across),
        out_shape=(jax.ShapeDtypeStruct((along, FACW, length), BF),) * across
        + (jax.ShapeDtypeStruct((QFW, length), BF),),
        grid_spec=pltpu.PrefetchScalarGridSpec(
            num_scalar_prefetch=1,
            grid=(PAIRS,),
            in_specs=[
                full(qfac.shape),
            ]
            + [full(v.shape) for v in facs]
            + [
                full(start.shape),
                pl.BlockSpec((length, 2 * HEAD_DIM), lambda p, s: (0, p)),
                pl.BlockSpec((length, 2 * HEAD_DIM), lambda p, s: (0, p)),
                pl.BlockSpec((2, length, 128), lambda p, s: (p, 0, 0)),
                full(cosine.shape),
                full(sine.shape),
            ],
            out_specs=[full((along, FACW, length))] * across + [full((QFW, length))],
            scratch_shapes=[
                pltpu.VMEM((n, 2 * KDW, length), BF),
                pltpu.VMEM((QHW, length), F32),
                pltpu.VMEM((n, 2 * KHW, length), F32),
                pltpu.VMEM((n, length, length), F32),
                pltpu.VMEM((n, 2 * KDW, length), F32),
                pltpu.VMEM((n, 2 * KHW, length), F32),
                pltpu.VMEM((QDW, length), F32),
                pltpu.VMEM((QHW, length), F32),
            ],
        ),
        compiler_params=pltpu.CompilerParams(
            dimension_semantics=("arbitrary",), vmem_limit_bytes=58 << 20
        ),
        cost_estimate=SMALL,
        name="attention_backward",
    )(scal, qfac, *facs, start, o, do, lse, cosine, sine)


def norm_of(values):
    inverse = lax.rsqrt(jnp.mean(values * values, axis=-1, keepdims=True) + EPS)
    return values * inverse, inverse


def turn(values, cosine, sine, sign):
    half = HEAD_DIM // 2
    parts = []
    for r in range(values.shape[0] // HEAD_DIM):
        first = values[r * HEAD_DIM : r * HEAD_DIM + half, :]
        second = values[r * HEAD_DIM + half : (r + 1) * HEAD_DIM, :]
        parts.append(first * cosine - sign * second * sine)
        parts.append(second * cosine + sign * first * sine)
    return jnp.concatenate(parts, axis=0)


def enter_kernel(gain_ref, cos_ref, sin_ref, *refs):
    sources, (xa_ref, qfac_ref, fac_ref) = refs[:7], refs[7:10]
    x_ref, qh, qd, kh, kd, vh, vd, sem = refs[10:]
    copies = [
        pltpu.make_async_copy(source, target, sem.at[k])
        for k, (source, target) in enumerate(zip(sources, (x_ref, qh, qd, kh, kd, vh, vd)))
    ]
    for copy in copies:
        copy.start()
    for copy in copies:
        copy.wait()
    normed = norm_of(x_ref[...].astype(F32))[0]
    xa = (normed * gain_ref[...]).astype(BF)
    xa_ref[...] = xa
    cosine, sine = cos_ref[...], sin_ref[...]
    kdims = turn(jnp.transpose(mm(xa, kd[...])), cosine, sine, 1.0)
    fac_ref[0:KDW, :] = kdims.astype(BF)
    fac_ref[KDW : 2 * KDW, :] = jnp.transpose(mm(xa, vd[...])).astype(BF)
    fac_ref[2 * KDW : 2 * KDW + KHW, :] = mm(kh[...], xa, 1, 1).astype(BF)
    fac_ref[2 * KDW + KHW :, :] = mm(vh[...], xa, 1, 1).astype(BF)
    qfac_ref[0:QHW, :] = mm(qh[...], xa, 1, 1).astype(BF)
    qdims = turn(jnp.transpose(mm(xa, qd[...])), cosine, sine, 1.0)
    qfac_ref[QHW:, :] = qdims.astype(BF)


WHOLE = pl.BlockSpec(memory_space=pltpu.VMEM)
RAW = pl.BlockSpec(memory_space=pl.ANY)
SCALAR = pl.BlockSpec(memory_space=pltpu.SMEM)
SMALL = pl.CostEstimate(flops=1000, transcendentals=0, bytes_accessed=1000)


def enter(x, gain, weights, cosine, sine):
    length, width = x.shape
    moved = (x,) + tuple(weights)
    return pl.pallas_call(
        enter_kernel,
        out_shape=(
            jax.ShapeDtypeStruct((length, width), BF),
            jax.ShapeDtypeStruct((QFW, length), BF),
            jax.ShapeDtypeStruct((FACW, length), BF),
        ),
        in_specs=[WHOLE] * 3 + [RAW] * 7,
        out_specs=[WHOLE] * 3,
        scratch_shapes=[pltpu.VMEM(v.shape, BF) for v in moved] + [pltpu.SemaphoreType.DMA((7,))],
        compiler_params=pltpu.CompilerParams(vmem_limit_bytes=40 << 20),
        name="enter",
    )(gain, cosine, sine, *moved)


def block_place(ids_ref, sizes, index, rows):
    place, scale = 0, 1
    for k in reversed(range(len(sizes))):
        place = place + ((index % sizes[k]) ^ ids_ref[k]) * scale
        index, scale = index // sizes[k], scale * sizes[k]
    return pl.multiple_of(place * rows, rows)


def deal(ids_ref, sizes, t_s, outs):
    blocks, rows = outs[0].shape[:2]
    for side in range(2):

        def one(i, carry, side=side):
            place = block_place(ids_ref, sizes, side * blocks + i, rows)
            outs[side][i] = t_s[pl.ds(place, rows), :].astype(BF)
            return carry

        lax.fori_loop(0, blocks, one, 0)


def collect(ids_ref, sizes, sources, write):
    blocks, rows = sources[0].shape[:2]
    for side in range(2):

        def one(i, carry, side=side):
            place = block_place(ids_ref, sizes, side * blocks + i, rows)
            write(pl.ds(place, rows), sources[side][i].astype(F32))
            return carry

        lax.fori_loop(0, blocks, one, 0)


def leave_out_kernel(sizes, ids_ref, o_ref, dhb_ref, kept_ref, sent_ref, t_s):
    t_s[...] = mm(jnp.transpose(o_ref[...]), dhb_ref[...])
    deal(ids_ref, sizes, t_s, (kept_ref, sent_ref))


SMALLS = 256
RESTW = 2 * KDW + QDW + SMALLS
GAINS = QHW + 2 * KHW
GAIN_COPIES = (SMALLS - GAINS) // 2


def leave_rest_kernel(
    sizes, ids_ref, x_ref, xa_ref, gain_ref, dres_ref, dq_ref, kg_ref, fgain_ref, cos_ref, sin_ref,
    qh, qd, kh, kd, vh, vd, tg_ref, kept_ref, sent_ref, out_ref
):
    normed, inverse = norm_of(x_ref[...].astype(F32))
    xa = xa_ref[...]
    g = kg_ref[...]
    dkd = turn(g[0:KDW, :], cos_ref[...], sin_ref[...], -1.0)
    d_kd = jnp.transpose(dkd).astype(BF)
    d_vd = jnp.transpose(g[KDW : 2 * KDW, :]).astype(BF)
    d_kh = jnp.transpose(g[2 * KDW : 2 * KDW + KHW, :]).astype(BF)
    d_vh = jnp.transpose(g[2 * KDW + KHW :, :]).astype(BF)
    dq = dq_ref[...].astype(F32)
    d_qh = jnp.transpose(dq[0:QHW, :]).astype(BF)
    d_qd = jnp.transpose(dq[QHW:, :]).astype(BF)
    xa_t = jnp.transpose(xa)
    out_ref[:, 0:KDW] = mm(xa_t, d_kd)
    out_ref[:, KDW : 2 * KDW] = mm(xa_t, d_vd)
    out_ref[:, 2 * KDW : 2 * KDW + QDW] = mm(xa_t, d_qd)
    dxa = mm(d_qd, qd[...], 1, 1) + mm(d_qh, qh[...])
    dxa = dxa + mm(d_kd, kd[...], 1, 1) + mm(d_vd, vd[...], 1, 1)
    dxa = dxa + mm(d_kh, kh[...]) + mm(d_vh, vh[...])
    scaled = dxa * gain_ref[...]
    mean = jnp.mean(scaled * normed, axis=-1, keepdims=True)
    tg_ref[...] = (dres_ref[...] + inverse * (scaled - normed * mean)).astype(BF)
    gain_part = jnp.sum(dxa * normed, axis=0, keepdims=True)
    low = g[2 * KDW :, :].astype(BF)
    small = [mm(dq_ref[0:QHW, :], xa), mm(low[0:KHW, :], xa), mm(low[KHW:, :], xa)]
    small += [gain_part] * GAIN_COPIES + [fgain_ref[...]] * GAIN_COPIES
    out_ref[:, 2 * KDW + QDW :] = jnp.transpose(jnp.concatenate(small, axis=0))
    deal(ids_ref, sizes, out_ref, (kept_ref, sent_ref))


def leave_out(sizes, ids, o, dhb):
    depth = o.shape[1]
    blocks = math.prod(sizes) // 2
    return pl.pallas_call(
        functools.partial(leave_out_kernel, sizes),
        out_shape=(jax.ShapeDtypeStruct((blocks, depth // (2 * blocks), depth), BF),) * 2,
        in_specs=[SCALAR] + [WHOLE] * 2,
        out_specs=[WHOLE] * 2,
        scratch_shapes=[pltpu.VMEM((depth, depth), F32)],
        compiler_params=pltpu.CompilerParams(vmem_limit_bytes=40 << 20),
        cost_estimate=SMALL,
        name="leave_out",
    )(ids, o, dhb)


def leave_rest(sizes, ids, x, xa, gain, dres, dq, kg, fgain, cosine, sine, weights):
    length, depth = x.shape
    blocks = math.prod(sizes) // 2
    return pl.pallas_call(
        functools.partial(leave_rest_kernel, sizes),
        out_shape=(jax.ShapeDtypeStruct((length, depth), BF),)
        + (jax.ShapeDtypeStruct((blocks, depth // (2 * blocks), RESTW), BF),) * 2,
        in_specs=[SCALAR] + [WHOLE] * (9 + len(weights)),
        out_specs=[WHOLE] * 3,
        scratch_shapes=[pltpu.VMEM((depth, RESTW), F32)],
        compiler_params=pltpu.CompilerParams(vmem_limit_bytes=40 << 20),
        cost_estimate=SMALL,
        name="leave_rest",
    )(ids, x, xa, gain, dres, dq, kg, fgain, cosine, sine, *weights)


def end_out_kernel(sizes, ids_ref, own_ref, got_ref, proj_ref):
    def write(rows, v):
        proj_ref[rows, :] = v

    collect(ids_ref, sizes, (own_ref, got_ref), write)


def end_out(sizes, ids, own, got):
    depth = own.shape[0] * own.shape[1] * 2
    return pl.pallas_call(
        functools.partial(end_out_kernel, sizes),
        out_shape=jax.ShapeDtypeStruct((depth, depth), F32),
        in_specs=[SCALAR] + [WHOLE] * 2,
        out_specs=WHOLE,
        compiler_params=pltpu.CompilerParams(vmem_limit_bytes=40 << 20),
        cost_estimate=SMALL,
        name="end_out",
    )(ids, own, got)


def end_rest_kernel(
    sizes, ids_ref, own_ref, got_ref, kd_ref, vd_ref, qd_ref, qh_ref, kh_ref, vh_ref, a_ref, f_ref, t_s
):
    def write(rows, v):
        kd_ref[rows, :] = v[:, 0:KDW]
        vd_ref[rows, :] = v[:, KDW : 2 * KDW]
        qd_ref[rows, :] = v[:, 2 * KDW : 2 * KDW + QDW]
        t_s[rows, :] = v[:, 2 * KDW + QDW :]

    collect(ids_ref, sizes, (own_ref, got_ref), write)
    turned = jnp.transpose(t_s[...])
    qh_ref[...] = turned[0:QHW, :]
    kh_ref[...] = turned[QHW : QHW + KHW, :]
    vh_ref[...] = turned[QHW + KHW : GAINS, :]
    a_ref[...] = turned[GAINS : GAINS + 1, :]
    f_ref[...] = turned[GAINS + GAIN_COPIES : GAINS + GAIN_COPIES + 1, :]


def end_rest(sizes, ids, own, got):
    depth = own.shape[0] * own.shape[1] * 2
    shapes = [(depth, KDW), (depth, KDW), (depth, QDW), (QHW, depth), (KHW, depth), (KHW, depth)]
    shapes += [(1, depth), (1, depth)]
    return pl.pallas_call(
        functools.partial(end_rest_kernel, sizes),
        out_shape=tuple(jax.ShapeDtypeStruct(v, F32) for v in shapes),
        in_specs=[SCALAR] + [WHOLE] * 2,
        out_specs=[WHOLE] * 8,
        scratch_shapes=[pltpu.VMEM((depth, SMALLS), F32)],
        compiler_params=pltpu.CompilerParams(vmem_limit_bytes=40 << 20),
        name="end_rest",
    )(ids, own, got)


def after(v, *others):
    return lax.optimization_barrier((v,) + others)[0]


class Grid:
    def __init__(self, dp, tensor):
        self.c = 2
        self.y = dp // 2
        self.x = self.y if tensor % self.y == 0 else 1
        self.z = tensor // self.x
        self.dp, self.tensor = dp, tensor
        self.axes = {
            "c": ("dp", 1, self.c),
            "y": ("dp", self.c, self.y),
            "x": ("tensor", 1, self.x),
            "z": ("tensor", self.x, self.z),
        }

    def size(self, g):
        return self.axes[g][2]

    def place(self, g):
        axis, stride, size = self.axes[g]
        return ((lax.axis_index(axis) // stride) % size).astype(jnp.int32)

    def swap(self, v, g, r):
        axis, stride, size = self.axes[g]
        total = self.dp if axis == "dp" else self.tensor
        return lax.ppermute(v, axis, [(i, i ^ (r * stride)) for i in range(total)])

    def bits(self, g):
        return [1 << k for k in range(self.size(g).bit_length() - 1)]

    def rels(self, g):
        order = [0]
        for bit in reversed(self.bits(g)):
            order = order + [r ^ bit for r in order]
        return order

    def stack(self, v, g):
        v = v[None]
        for bit in reversed(self.bits(g)):
            v = jnp.concatenate([v, self.swap(v, g, bit)], axis=0)
        return v

    def unstack(self, v, g, last=BF):
        bits = self.bits(g)
        for k, bit in enumerate(bits):
            rows = v.shape[0] // 2
            got = self.swap(v[rows:].astype(BF), g, bit)
            v = v[:rows].astype(F32) + got.astype(F32)
        return v[0].astype(last)

    def direct(self, v, g):
        return [v] + [self.swap(v, g, r) for r in self.rels(g)[1:]]

    def swap_masks(self, v, dp_mask, tensor_mask):
        if not tensor_mask:
            return lax.ppermute(v, "dp", [(i, i ^ dp_mask) for i in range(self.dp)])
        if not dp_mask:
            return lax.ppermute(v, "tensor", [(i, i ^ tensor_mask) for i in range(self.tensor)])
        mask = dp_mask * self.tensor + tensor_mask
        pairs = [(i, i ^ mask) for i in range(self.dp * self.tensor)]
        return lax.ppermute(v, ("dp", "tensor"), pairs)

    def levels(self, plan):
        out = []
        for letters in plan:
            masks = [(0, 0)]
            for g in letters:
                axis, stride, size = self.axes[g]
                masks = [
                    (d + r * stride, t) if axis == "dp" else (d, t + r * stride)
                    for d, t in masks
                    for r in range(size)
                ]
            out.append(masks)
        return out

    def numbers(self, plan):
        out = []
        for letters in plan:
            number = jnp.int32(0)
            for g in letters:
                number = number * self.size(g) + self.place(g)
            out.append(number)
        return jnp.stack(out)

    def swaps(self, low, masks):
        return [self.swap_masks(low[m], *masks[m]) for m in range(1, len(masks))]

    def swaps_whole(self, low, masks):
        return [self.swap_masks(low, *m) for m in masks[1:]]


def ffn_kernel(parts, plan, shards, blend, scal_ref, xf_ref, dy_ref, *refs):
    own, arrays = plan
    count = (3 if own else 0) + len(arrays)
    sources, refs = refs[:count], refs[count:]
    if blend:
        mixed_in, dxf_in = refs[:2]
        refs = refs[2:]
    mixed_ref, dxf_ref, inner_ref, dgate_ref, dup_ref, w_s, sem = refs
    width = w_s.shape[2]
    rows = w_s.shape[3] // parts
    copies = []

    def move(source, target):
        copies.append(pltpu.make_async_copy(source, target, sem.at[len(copies)]))

    if own:
        for k in range(3):
            move(sources[k], w_s.at[k, 0])
    for (slots, q), source in zip(arrays, sources[3 if own else 0 :]):
        place = pl.multiple_of((scal_ref[0] ^ q) * rows, rows)
        for i, slot in enumerate(slots):
            move(source.at[i], w_s.at[:, slot, :, pl.ds(place, rows)])
    for copy in copies:
        copy.start()
    for copy in copies:
        copy.wait()
    xf, dy = xf_ref[...], dy_ref[...]
    units, unused, hidden = inner_ref.shape
    for s in range(units):
        wg, wu, wd = ((w_s[k] if units == 1 else w_s[k, s]).reshape(hidden, -1) for k in range(3))
        gate = mm(xf, wg, 1, 1)
        up = mm(xf, wu, 1, 1)
        d_inner = mm(dy, wd, 1, 1)
        sig = 1.0 / (1.0 + jnp.exp(-gate))
        act = gate * sig
        inner = (act * up).astype(BF)
        d_gate = (d_inner * up * sig * (1.0 + gate * (1.0 - sig))).astype(BF)
        d_up = (d_inner * act).astype(BF)
        inner_ref[s] = inner
        dgate_ref[s] = d_gate
        dup_ref[s] = d_up
        dxf = mm(d_gate, wg) + mm(d_up, wu)
        mixed = mm(inner, wd)
        if s == 0 and blend:
            dxf, mixed = dxf + dxf_in[...], mixed + mixed_in[...]
        if s > 0:
            dxf, mixed = dxf + total[0], mixed + total[1]
        total = (dxf, mixed)
    dxf_ref[...] = total[0].astype(dxf_ref.dtype)
    mixed_ref[...] = total[1].astype(mixed_ref.dtype)


def ffn(mine, xf, dy, own, arrays, parts, width, before, out_type, name):
    length, depth = xf.shape
    shards = (1 if own else 0) + sum(len(slots) for slots, q, v in arrays if q == 0)
    hidden = (1, length, shards * width) if width % 16 == 0 else (shards, length, width)
    plan = (bool(own), [(slots, q) for slots, q, v in arrays])
    sources = list(own) + [v for slots, q, v in arrays]
    moves = (3 if own else 0) + sum(len(slots) for slots, q, v in arrays)
    return pl.pallas_call(
        functools.partial(ffn_kernel, parts, plan, shards, bool(before)),
        out_shape=(jax.ShapeDtypeStruct((length, depth), out_type),) * 2
        + (jax.ShapeDtypeStruct(hidden, BF),) * 3,
        in_specs=[SCALAR, WHOLE, WHOLE] + [RAW] * len(sources) + [WHOLE] * len(before),
        out_specs=[WHOLE] * 5,
        scratch_shapes=[
            pltpu.VMEM((3, shards, width, depth), BF),
            pltpu.SemaphoreType.DMA((moves,)),
        ],
        compiler_params=pltpu.CompilerParams(vmem_limit_bytes=58 << 20),
        cost_estimate=SMALL,
        name=name,
    )(mine, xf, dy, *sources, *before)


def products(lefts, rights, width, write):
    slot = 0
    for group in range(len(lefts[0])):
        units, unused, hidden = lefts[0][group].shape
        for s in range(units):
            total = None
            for b in range(len(rights)):
                term = mm(jnp.transpose(lefts[b][group][s]), rights[b][...])
                total = term if total is None else total + term
            for i in range(hidden // width):
                write(slot, total[i * width : (i + 1) * width, :])
                slot += 1


def divide(refs, blocks):
    each = len(refs) // blocks
    return [refs[b * each : (b + 1) * each] for b in range(blocks)]


def store(outs, scal_ref, t_s, slot, first, value):
    rows, lanes = value.shape[0], outs[0].shape[3]
    t_s[0:rows, :] = value
    for q in range(2 * outs[0].shape[0]):
        place = pl.multiple_of((scal_ref[0] ^ q) * lanes, lanes)
        part = t_s[0:rows, pl.ds(place, lanes)]
        outs[q % 2][q // 2, slot, first : first + rows, :] = part.astype(BF)


def gate_up_kernel(blocks, scal_ref, *refs):
    xfs, outs, t_s = refs[:blocks], refs[-3:-1], refs[-1]
    rest = refs[blocks:-3]
    width = outs[0].shape[2] // 2
    for k in range(2):
        lefts = divide(rest[k * len(rest) // 2 : (k + 1) * len(rest) // 2], blocks)

        def write(slot, value, k=k):
            store(outs, scal_ref, t_s, slot, k * width, value)

        products(lefts, xfs, width, write)


def down_kernel(blocks, scal_ref, *refs):
    dys, outs, t_s = refs[:blocks], refs[-3:-1], refs[-1]
    width = outs[0].shape[2]

    def write(slot, value):
        store(outs, scal_ref, t_s, slot, 0, value)

    products(divide(refs[blocks:-3], blocks), dys, width, write)


def grads(kernel, mine, wholes, parts, zs, rows, depth, scratch, name):
    return pl.pallas_call(
        kernel,
        out_shape=(jax.ShapeDtypeStruct((parts // 2, zs, rows, depth // parts), BF),) * 2,
        in_specs=[SCALAR] + [WHOLE] * len(wholes),
        out_specs=[WHOLE] * 2,
        scratch_shapes=scratch,
        compiler_params=pltpu.CompilerParams(vmem_limit_bytes=58 << 20),
        cost_estimate=SMALL,
        name=name,
    )(mine, *wholes)


def unpack_kernel(scal_ref, own_ref, got_ref, gate_ref, up_ref, down_ref):
    width = gate_ref.shape[0]
    for side, ref in enumerate((own_ref, got_ref)):

        @pl.when(pl.program_id(0) % 2 == side)
        def _(ref=ref):
            gate_ref[...] = ref[0, 0:width, :].astype(F32)
            up_ref[...] = ref[0, width : 2 * width, :].astype(F32)
            down_ref[...] = ref[0, 2 * width :, :].astype(F32)


def unpack(mine, own, got):
    half, rows, lanes = own.shape
    width, parts = rows // 3, 2 * half
    column = pl.BlockSpec((width, lanes), lambda q, s: (0, s[0] ^ q))
    return pl.pallas_call(
        unpack_kernel,
        out_shape=(jax.ShapeDtypeStruct((width, parts * lanes), F32),) * 3,
        grid_spec=pltpu.PrefetchScalarGridSpec(
            num_scalar_prefetch=1,
            grid=(parts,),
            in_specs=[pl.BlockSpec((1, rows, lanes), lambda q, s: (q // 2, 0, 0))] * 2,
            out_specs=[column] * 3,
        ),
        compiler_params=pltpu.CompilerParams(dimension_semantics=("arbitrary",)),
        cost_estimate=SMALL,
        name="unpack",
    )(mine, own, got)


def spread_pieces(grid, got, tie):
    entries = []
    for k in range(grid.y):
        piece = got if k == 0 else grid.swap(got, "y", k)
        entries += [(2 * k, piece), (2 * k + 1, grid.swap(after(piece, tie), "c", 1))]
    return entries


def reduce_core(grid, even, odd):
    got = grid.swap(odd, "c", 1)
    goes = [
        (even[k].astype(F32) + got[k].astype(F32)).astype(BF) for k in range(1, grid.y)
    ]
    return (even[0], got[0]), goes


def total_of(*terms):
    total = terms[0].astype(F32)
    for term in terms[1:]:
        total = total + term.astype(F32)
    return total


def contract(left, right, left_dim, right_dim):
    return lax.dot_general(
        left, right, (((left_dim,), (right_dim,)), ((), ())), preferred_element_type=jnp.float32
    )


def norm_back(grad_out, normed, inverse, gain):
    scaled = grad_out * gain
    gain_part = jnp.sum(grad_out * normed, axis=0)
    grad_in = inverse * (scaled - normed * jnp.mean(scaled * normed, axis=-1, keepdims=True))
    return (grad_in, gain_part)


def body(
    grid,
    tokens,
    cotangent,
    segments,
    positions,
    attngain,
    ffngain,
    queryheads,
    querydims,
    keyheads,
    keydims,
    valueheads,
    valuedims,
    outproj,
    gateproj,
    upproj,
    downproj,
):
    x = tokens[0]
    upstream = cotangent[0]
    length, depth = x.shape
    parts = grid.dp
    lanes = depth // parts
    me = lax.axis_index("tensor").astype(jnp.int32)
    spot = jnp.stack([lax.axis_index("dp").astype(jnp.int32), grid.place("z")])
    offset = me * length
    places = lax.dynamic_slice_in_dim(positions[0], offset, length)
    half = HEAD_DIM // 2
    freqs = 10000.0 ** (-jnp.arange(half, dtype=F32) * 2.0 / HEAD_DIM)
    angles = freqs[:, None] * places.astype(F32)[None, :]
    cosine, sine = jnp.cos(angles), jnp.sin(angles)
    start = (offset + jnp.arange(length, dtype=jnp.int32) - places)[:, None]
    scal = jnp.stack([jnp.maximum(offset - places[0], 0) // length, me]).astype(jnp.int32)
    weights = (queryheads.T, querydims, keyheads.T, keydims, valueheads.T, valuedims)

    own = (gateproj.T, upproj.T, downproj)
    width = downproj.shape[0]
    payload = jnp.stack(
        [lax.dynamic_slice_in_dim(v, spot[0] * lanes, lanes, 1) for v in own]
    )
    dys = [upstream] + [grid.swap(upstream, "x", r) for r in range(1, grid.x)]
    xa, qfac, fac = enter(x, attngain[None, :], weights, cosine, sine)
    rels = grid.rels("z")[1:]
    near = [fac] + [grid.swap(fac, "z", r) for r in rels[:-1]]
    near = near + [grid.swap(after(fac, *dys[1:]), "z", r) for r in rels[-1:]]
    near = jnp.stack(near)
    facs = [near] + [grid.swap(near, "x", r) for r in range(1, grid.x)]
    shards = [payload]
    for bit in grid.bits("z")[::-1]:
        got = [grid.swap(v, "z", bit) for v in shards]
        shards = shards + [after(v, near) for v in got]
    remote = shards[1:]

    nearby = jnp.stack(remote[:-1]) if len(remote) > 1 else None
    if len(remote) > 1:
        qfac = after(qfac, nearby)
    attn_out, lse = attention_forward(scal, qfac, facs, start)
    early, late = [], []
    if len(remote) > 1:
        slots = list(range(1, len(remote)))
        early = [(slots, q, v) for q, v in spread_pieces(grid, nearby, attn_out)]

    local = x.astype(F32)
    residual = local + jnp.dot(attn_out, outproj, preferred_element_type=jnp.float32)
    inverse_two = lax.rsqrt(jnp.mean(residual * residual, axis=-1, keepdims=True) + EPS)
    normed_two = residual * inverse_two
    input_two = (normed_two * ffngain).astype(jnp.bfloat16)
    xfs = [input_two] + [
        grid.swap(input_two, "x", r) for r in range(1, grid.x)
    ]

    across = xfs[-1]
    results = [None] * grid.x
    firsts = []
    for k in range(grid.x):
        kind = BF if k and not remote else F32
        if k:
            xfs[k] = after(xfs[k], firsts[0][0])
        firsts.append(
            ffn(spot, xfs[k], dys[k], own, early, parts, width, (), kind, "ffn_early")
        )
    if remote:
        last = after(remote[-1], attn_out)[None]
        late = [([0], q, v) for q, v in spread_pieces(grid, last, after(firsts[0][0], across))]
    for k in reversed(range(grid.x)):
        first = firsts[k]
        if late:
            second = ffn(
                spot, xfs[k], dys[k], (), late, parts, width, first[:2], BF if k else F32, "ffn_late"
            )
            results[k] = (second[0], second[1]) + tuple(
                [first[i], second[i]] for i in range(2, 5)
            )
        else:
            results[k] = (first[0], first[1]) + tuple([first[i]] for i in range(2, 5))
    d_norm_two, ffn_out = results[0][1], results[0][0]
    inners, dgates, dups = (
        [v for k in range(grid.x) for v in results[k][i]] for i in range(2, 5)
    )
    first_parts = grads(
        functools.partial(gate_up_kernel, grid.x),
        spot, xfs + dgates + dups, parts, grid.z, 2 * width, depth,
        [pltpu.VMEM((width, depth), F32)], "gate_up_grads",
    )
    second_parts = grads(
        functools.partial(down_kernel, grid.x),
        spot, dys + inners, parts, grid.z, width, depth,
        [pltpu.VMEM((width, depth), F32)], "down_grads",
    )
    first_kept, first_goes = reduce_core(grid, *first_parts)
    for r in range(1, grid.x):
        got = grid.swap(results[r][1], "x", r)
        d_norm_two = d_norm_two + after(got, second_parts[0], first_goes[0]).astype(F32)
    grad_through, ffngain_part = norm_back(d_norm_two, normed_two, inverse_two, ffngain)
    d_residual = upstream.astype(jnp.float32) + grad_through
    d_res_low = d_residual.astype(jnp.bfloat16)
    d_attended = contract(d_res_low, outproj, 1, 1).astype(jnp.bfloat16)

    plan, z_masks = ("c", "xy", "z"), grid.levels(("z",))[0]
    split_z = depth // (parts * grid.tensor) >= 16
    if not split_z:
        plan = ("c", "xy")
    levels = grid.levels(plan)
    core_masks, xy_masks = levels[0], levels[1]
    sizes = tuple(len(masks) for masks in levels)
    ids = grid.numbers(plan)
    shape = sizes[1:] + (depth // math.prod(sizes), -1)

    def along_z(v):
        low = v.astype(BF)
        if split_z:
            return total_of(v[0], *grid.swaps(low, z_masks)).astype(BF)
        return total_of(v, *grid.swaps_whole(low, z_masks)).astype(BF)

    def share_z(v):
        return jnp.stack([v] + grid.swaps_whole(v, z_masks)) if split_z else v

    second_kept, second_goes = reduce_core(grid, *second_parts)
    kept, sent = leave_out(sizes, ids, attn_out, d_res_low)
    out_sum = total_of(
        kept.reshape(shape), grid.swap_masks(sent.reshape(shape), *core_masks[1])
    )
    out_low = out_sum.astype(BF)
    d_attended = after(d_attended, first_goes[-1], second_goes[-1], out_low)
    back = attention_backward(
        scal, qfac, facs, start, attn_out, d_attended, lse, cosine, sine
    )
    terms, dq = list(back[:-1]), back[-1]

    first_got = [grid.swap(v, "y", k + 1) for k, v in enumerate(first_goes)]
    second_got = [grid.swap(v, "y", k + 1) for k, v in enumerate(second_goes)]
    out_got = grid.swaps(out_low, xy_masks)
    out_first = after(out_sum[0], dq)
    first_kept = (after(first_kept[0], dq), first_kept[1])
    second_kept = (after(second_kept[0], dq), second_kept[1])
    terms[1:] = [after(v, *second_got) for v in terms[1:]]
    out_mine = along_z(total_of(out_first, *out_got))
    out_mine = share_z(out_mine)
    near = terms[0].astype(F32)
    for r in range(1, grid.x):
        near = near + grid.swap(terms[r], "x", r).astype(F32)
    ffn_sum = jnp.concatenate(
        [total_of(*first_kept, *first_got), total_of(*second_kept, *second_got)], axis=1
    )
    low = after(near.astype(BF), out_mine, *first_got)
    key_grads = near[0]
    for i, r in enumerate(grid.rels("z")):
        if i:
            key_grads = key_grads + grid.swap(low[i], "z", r).astype(F32)
    for k, bit in enumerate(grid.bits("z")):
        rows = ffn_sum.shape[0] // 2
        goes = ffn_sum[rows:].astype(BF)
        if k == 0:
            goes = after(goes, key_grads)
        got = grid.swap(goes, "z", bit)
        if k == 0:
            first_z = got
        ffn_sum = ffn_sum[:rows] + got.astype(F32)
    out_mine = after(out_mine, key_grads)
    out_others = grid.swaps_whole(out_mine, xy_masks)
    out_own = jnp.stack([out_mine] + out_others)
    out_other = grid.swap_masks(out_own, *core_masks[1])

    def flat(v):
        return v.reshape(math.prod(sizes) // 2, -1, v.shape[-1])

    out_part = end_out(sizes, ids, flat(out_own), flat(out_other))
    tokens_grad, kept, sent = leave_rest(
        sizes, ids, x, xa, attngain[None, :], d_residual, dq, key_grads, ffngain_part[None, :],
        cosine, sine, weights,
    )
    rest = total_of(kept.reshape(shape), grid.swap_masks(sent.reshape(shape), *core_masks[1]))
    low = after(rest.astype(BF), *out_others)
    rest = total_of(rest[0], *grid.swaps(low, xy_masks))
    rest = after(rest, first_z)

    ffn_got = [grid.swap(after(results[r][0], rest), "x", r) for r in range(1, grid.x)]
    mixed = (residual + total_of(ffn_out, *ffn_got)).astype(jnp.bfloat16)

    rest = along_z(rest)
    mine = after(ffn_sum[0].astype(BF), rest)
    rest = after(share_z(rest), *ffn_got)
    rest = jnp.stack([rest] + grid.swaps_whole(rest, xy_masks))
    rest = after(rest, out_part)
    others = grid.swap_masks(rest, *core_masks[1])
    mine = jnp.stack([mine] + [grid.swap(mine, "y", k) for k in range(1, grid.y)])
    gate_part, up_part, down_part = unpack(spot, mine, grid.swap(mine, "c", 1))

    kd_grad, vd_grad, qd_grad, qh_grad, kh_grad, vh_grad, again_grad, fgain_grad = end_rest(
        sizes, ids, after(flat(rest), down_part), flat(others)
    )
    return (
        mixed[None],
        tokens_grad[None],
        again_grad[0],
        fgain_grad[0],
        qh_grad.T,
        qd_grad,
        kh_grad.T,
        kd_grad,
        vh_grad.T,
        vd_grad,
        out_part,
        gate_part.T,
        up_part.T,
        down_part,
    )


def solution(mesh):
    grid = Grid(mesh.shape["dp"], mesh.shape["tensor"])
    rows = P("dp", "tensor", None)
    placed = (rows, rows, P("dp", None), P("dp", None)) + (P(),) * 9
    halves = (P(None, "tensor"), P(None, "tensor"), P("tensor", None))
    return jax.shard_map(
        functools.partial(body, grid),
        mesh=mesh,
        in_specs=placed + halves,
        out_specs=(rows, rows) + (P(),) * 9 + halves,
        check_vma=False,
    )
```

```python
import functools
import math

import jax
import jax.numpy as jnp
from jax import lax
from jax.experimental import pallas as pl
from jax.experimental.pallas import tpu as pltpu

from jax.sharding import PartitionSpec as P

HEADS = 16
HEAD_DIM = 64
QRANK = 6
KRANK = 2
PAIRS = HEADS // 2
QHW = HEADS * QRANK
QDW = QRANK * HEAD_DIM
KDW = KRANK * HEAD_DIM
KHW = HEADS * KRANK
FACW = 2 * KDW + 2 * KHW
QFW = QHW + QDW
LOG2E = 1.4426950408889634
EPS = 1e-06
BF = jnp.bfloat16
F32 = jnp.float32


def mm(a, b, ca=1, cb=0):
    return lax.dot_general(a, b, (((ca,), (cb,)), ((), ())), preferred_element_type=F32)


def expand_pair(bk0, bk1, rows):
    first = rows[0] * bk0 + rows[1] * bk1
    second = rows[2] * bk0 + rows[3] * bk1
    return jnp.concatenate([first, second], axis=0) * (1.0 / KRANK)


def query_pair(qfac_ref, aq_s, pair):
    halves = []
    for h in range(2):
        acc = None
        for r in range(QRANK):
            row = aq_s[pl.ds(pair * (2 * QRANK) + h * QRANK + r, 1), :]
            term = row * qfac_ref[QHW + r * HEAD_DIM : QHW + (r + 1) * HEAD_DIM, :].astype(F32)
            acc = term if acc is None else acc + term
        halves.append(acc * (1.0 / QRANK))
    return jnp.concatenate(halves, axis=0).astype(BF)


def reverse_bits(r, size):
    total, bits = 0, size.bit_length() - 1
    for k in range(bits):
        total = total + (((r >> k) & 1) << (bits - 1 - k))
    return total


def fill_tables(scal_ref, qfac_ref, fac_refs, start_ref, fac_s, aq_s, kv_s, bias_s):
    length = qfac_ref.shape[1]
    me = scal_ref[1]
    across = len(fac_refs)
    aq_s[...] = qfac_ref[0:QHW, :].astype(F32)
    row = lax.broadcasted_iota(jnp.int32, (length, length), 0) + me * length
    column = lax.broadcasted_iota(jnp.int32, (length, length), 1)
    begin = start_ref[...]

    def fill(c, carry):
        for k, ref in enumerate(fac_refs):

            @pl.when(((c ^ me) % across) == k)
            def _(ref=ref):
                piece = ref[reverse_bits((c ^ me) // across, ref.shape[0])]
                fac_s[c] = piece[0 : 2 * KDW, :]
                kv_s[c] = piece[2 * KDW :, :].astype(F32)

        key = column + c * length
        keep = (key >= begin) & (key <= row)
        bias_s[c] = jnp.where(keep, 0.0, -1e30)
        return carry

    lax.fori_loop(scal_ref[0], me + 1, fill, 0)


def key_pair(fac_ref, kv_s, c, pair, which):
    base = which * KDW
    b0 = fac_ref[c, base : base + HEAD_DIM, :].astype(F32)
    b1 = fac_ref[c, base + HEAD_DIM : base + 2 * HEAD_DIM, :].astype(F32)
    rows = [kv_s[c, pl.ds(which * KHW + pair * 4 + j, 1), :] for j in range(4)]
    return expand_pair(b0, b1, rows), b0, b1, rows


def forward_kernel(across, scal_ref, qfac_ref, *refs):
    fac_refs, start_ref = refs[:across], refs[across]
    o_ref, lse_ref, fac_ref, aq_s, kv_s, bias_s, s_s = refs[across + 1 :]
    pair = pl.program_id(0)
    length = qfac_ref.shape[1]
    lo, me = scal_ref[0], scal_ref[1]

    @pl.when(pair == 0)
    def _():
        fill_tables(scal_ref, qfac_ref, fac_refs, start_ref, fac_ref, aq_s, kv_s, bias_s)

    query = jnp.transpose(query_pair(qfac_ref, aq_s, pair).astype(F32)) * (HEAD_DIM**-0.5)
    low_half = lax.broadcasted_iota(jnp.int32, (length, 2 * HEAD_DIM), 1) < HEAD_DIM
    queries = [
        jnp.where(low_half, query, 0.0).astype(BF),
        jnp.where(low_half, 0.0, query).astype(BF),
    ]
    lanes = 128
    pieces = length // lanes

    def score(c, tops):
        keys = key_pair(fac_ref, kv_s, c, pair, 0)[0].astype(BF)
        bias = bias_s[c]
        new = []
        for h in range(2):
            s = mm(queries[h], keys) * LOG2E + bias
            s_s[h, c] = s
            top = tops[h]
            for i in range(pieces):
                top = jnp.maximum(top, s[:, i * lanes : (i + 1) * lanes])
            new.append(top)
        return tuple(new)

    start = jnp.full((length, lanes), -1e30, F32)
    tops = lax.fori_loop(lo, me + 1, score, (start, start))
    tops = [jnp.max(top, axis=1, keepdims=True) for top in tops]

    def value(c, carry):
        values = key_pair(fac_ref, kv_s, c, pair, 1)[0].astype(BF)
        new = []
        for h in range(2):
            p = jnp.exp2(s_s[h, c] - tops[h])
            total = carry[2 * h]
            for i in range(pieces):
                total = total + p[:, i * lanes : (i + 1) * lanes]
            new += [total, carry[2 * h + 1] + mm(p.astype(BF), values, 1, 1)]
        return tuple(new)

    zero = jnp.zeros((length, lanes), F32)
    wide = jnp.zeros((length, 2 * HEAD_DIM), F32)
    done = lax.fori_loop(lo, me + 1, value, (zero, wide, zero, wide))
    outs = []
    for h in range(2):
        total = jnp.sum(done[2 * h], axis=1, keepdims=True)
        outs.append(done[2 * h + 1] / total)
        lse_ref[h] = jnp.broadcast_to(tops[h] + jnp.log2(total), (length, lanes))
    o_ref[...] = jnp.where(low_half, outs[0], outs[1]).astype(BF)


def full(shape):
    return pl.BlockSpec(shape, lambda p, s: (0,) * len(shape))


def attention_forward(scal, qfac, facs, start):
    length = qfac.shape[1]
    n = facs[0].shape[0] * len(facs)
    return pl.pallas_call(
        functools.partial(forward_kernel, len(facs)),
        out_shape=(
            jax.ShapeDtypeStruct((length, HEADS * HEAD_DIM), BF),
            jax.ShapeDtypeStruct((HEADS, length, 128), F32),
        ),
        grid_spec=pltpu.PrefetchScalarGridSpec(
            num_scalar_prefetch=1,
            grid=(PAIRS,),
            in_specs=[full(qfac.shape)] + [full(v.shape) for v in facs] + [full(start.shape)],
            out_specs=[
                pl.BlockSpec((length, 2 * HEAD_DIM), lambda p, s: (0, p)),
                pl.BlockSpec((2, length, 128), lambda p, s: (p, 0, 0)),
            ],
            scratch_shapes=[
                pltpu.VMEM((n, 2 * KDW, length), BF),
                pltpu.VMEM((QHW, length), F32),
                pltpu.VMEM((n, 2 * KHW, length), F32),
                pltpu.VMEM((n, length, length), F32),
                pltpu.VMEM((2, n, length, length), F32),
            ],
        ),
        compiler_params=pltpu.CompilerParams(
            dimension_semantics=("arbitrary",), vmem_limit_bytes=58 << 20
        ),
        cost_estimate=SMALL,
        name="attention_forward",
    )(scal, qfac, *facs, start)


def backward_kernel(across, scal_ref, qfac_ref, *refs):
    fac_refs = refs[:across]
    start_ref, o_ref, do_ref, lse_ref, cos_ref, sin_ref = refs[across : across + 6]
    terms_refs = refs[across + 6 : 2 * across + 6]
    dq_ref, fac_ref, aq_s, kv_s, bias_s, acc_s, heads_s, dbq_s, daq_s = refs[2 * across + 6 :]
    pair = pl.program_id(0)
    length = qfac_ref.shape[1]
    n = fac_ref.shape[0]
    lo, me = scal_ref[0], scal_ref[1]
    pieces = length // 128

    @pl.when(pair == 0)
    def _():
        fill_tables(scal_ref, qfac_ref, fac_refs, start_ref, fac_ref, aq_s, kv_s, bias_s)
        dbq_s[...] = jnp.zeros_like(dbq_s)

        def clear(c, carry):
            acc_s[c] = jnp.zeros((2 * KDW, length), F32)
            return carry

        lax.fori_loop(lo, me + 1, clear, 0)

    query_t = query_pair(qfac_ref, aq_s, pair).astype(F32) * (HEAD_DIM**-0.5)
    query = jnp.transpose(query_t)
    query_t = query_t.astype(BF)
    do = do_ref[...].astype(F32)
    do_t = jnp.transpose(do).astype(BF)
    low_half = lax.broadcasted_iota(jnp.int32, (length, 2 * HEAD_DIM), 1) < HEAD_DIM
    product = do * o_ref[...].astype(F32)
    queries, grads, deltas, stats = [], [], [], []
    for h in range(2):
        keep = low_half if h == 0 else jnp.logical_not(low_half)
        queries.append(jnp.where(keep, query, 0.0).astype(BF))
        grads.append(jnp.where(keep, do, 0.0).astype(BF))
        deltas.append(jnp.sum(jnp.where(keep, product, 0.0), axis=1, keepdims=True))
        stats.append(lse_ref[h])

    def step(c, dqs):
        keys, kb0, kb1, krows = key_pair(fac_ref, kv_s, c, pair, 0)
        values, vb0, vb1, vrows = key_pair(fac_ref, kv_s, c, pair, 1)
        keys, values = keys.astype(BF), values.astype(BF)
        bias = bias_s[c]
        new, sums, rows = [], [None] * 4, []
        for h in range(2):
            s = mm(queries[h], keys) * LOG2E + bias
            lse = jnp.concatenate([stats[h]] * pieces, axis=1)
            p = jnp.exp2(s - lse)
            dp = mm(grads[h], values)
            ds = (p * (dp - deltas[h])).astype(BF)
            pb = p.astype(BF)
            new.append(dqs[h] + mm(ds, keys, 1, 1))
            half = slice(h * HEAD_DIM, (h + 1) * HEAD_DIM)
            dk = mm(query_t[half, :], ds)
            dv = mm(do_t[half, :], pb)
            for which, d, b0, b1, a in ((0, dk, kb0, kb1, krows), (1, dv, vb0, vb1, vrows)):
                for r, b in ((0, b0), (1, b1)):
                    term = d * a[2 * h + r]
                    k = 2 * which + r
                    sums[k] = term if sums[k] is None else sums[k] + term
                    rows.append((which * 4 + 2 * h + r, jnp.sum(d * b, axis=0, keepdims=True)))
        for k in range(4):
            part = slice(k * HEAD_DIM, (k + 1) * HEAD_DIM)
            acc_s[c, part, :] = acc_s[c, part, :] + sums[k]
        for k, row in rows:
            where = (k // 4) * KHW + pair * 4 + k % 4
            heads_s[c, pl.ds(where, 1), :] = row
        return tuple(new)

    zero = jnp.zeros((length, 2 * HEAD_DIM), F32)
    dqs = lax.fori_loop(lo, me + 1, step, (zero, zero))
    dq_t = jnp.transpose(jnp.where(low_half, dqs[0], dqs[1])) * (HEAD_DIM**-0.5 / QRANK)
    for h in range(2):
        d = dq_t[h * HEAD_DIM : (h + 1) * HEAD_DIM, :]
        for r in range(QRANK):
            part = slice(r * HEAD_DIM, (r + 1) * HEAD_DIM)
            b = qfac_ref[QHW + r * HEAD_DIM : QHW + (r + 1) * HEAD_DIM, :].astype(F32)
            k = pl.ds(pair * (2 * QRANK) + h * QRANK + r, 1)
            daq_s[k, :] = jnp.sum(d * b, axis=0, keepdims=True)
            dbq_s[part, :] = dbq_s[part, :] + d * aq_s[k, :]

    @pl.when(pair == PAIRS - 1)
    def _():
        cosine, sine = cos_ref[...], sin_ref[...]
        half = HEAD_DIM // 2
        dq_ref[0:QHW, :] = daq_s[...].astype(BF)
        for r in range(QRANK):
            first = dbq_s[r * HEAD_DIM : r * HEAD_DIM + half, :]
            second = dbq_s[r * HEAD_DIM + half : (r + 1) * HEAD_DIM, :]
            turned = jnp.concatenate(
                [first * cosine + second * sine, second * cosine - first * sine], axis=0
            )
            dq_ref[QHW + r * HEAD_DIM : QHW + (r + 1) * HEAD_DIM, :] = turned.astype(BF)

        def flush(c, carry):
            inside = (c >= lo) & (c <= me)
            for k, ref in enumerate(terms_refs):

                @pl.when(inside & (((c ^ me) % across) == k))
                def _(ref=ref):
                    place = reverse_bits((c ^ me) // across, ref.shape[0])
                    ref[place, 0 : 2 * KDW, :] = (acc_s[c] * (1.0 / KRANK)).astype(BF)
                    ref[place, 2 * KDW :, :] = (heads_s[c] * (1.0 / KRANK)).astype(BF)

                @pl.when(jnp.logical_not(inside) & (((c ^ me) % across) == k))
                def _(ref=ref):
                    ref[reverse_bits((c ^ me) // across, ref.shape[0])] = jnp.zeros((FACW, length), BF)

            return carry

        lax.fori_loop(0, n, flush, 0)


def attention_backward(scal, qfac, facs, start, o, do, lse, cosine, sine):
    length = qfac.shape[1]
    across, along = len(facs), facs[0].shape[0]
    n = across * along
    return pl.pallas_call(
        functools.partial(backward_kernel, across),
        out_shape=(jax.ShapeDtypeStruct((along, FACW, length), BF),) * across
        + (jax.ShapeDtypeStruct((QFW, length), BF),),
        grid_spec=pltpu.PrefetchScalarGridSpec(
            num_scalar_prefetch=1,
            grid=(PAIRS,),
            in_specs=[
                full(qfac.shape),
            ]
            + [full(v.shape) for v in facs]
            + [
                full(start.shape),
                pl.BlockSpec((length, 2 * HEAD_DIM), lambda p, s: (0, p)),
                pl.BlockSpec((length, 2 * HEAD_DIM), lambda p, s: (0, p)),
                pl.BlockSpec((2, length, 128), lambda p, s: (p, 0, 0)),
                full(cosine.shape),
                full(sine.shape),
            ],
            out_specs=[full((along, FACW, length))] * across + [full((QFW, length))],
            scratch_shapes=[
                pltpu.VMEM((n, 2 * KDW, length), BF),
                pltpu.VMEM((QHW, length), F32),
                pltpu.VMEM((n, 2 * KHW, length), F32),
                pltpu.VMEM((n, length, length), F32),
                pltpu.VMEM((n, 2 * KDW, length), F32),
                pltpu.VMEM((n, 2 * KHW, length), F32),
                pltpu.VMEM((QDW, length), F32),
                pltpu.VMEM((QHW, length), F32),
            ],
        ),
        compiler_params=pltpu.CompilerParams(
            dimension_semantics=("arbitrary",), vmem_limit_bytes=58 << 20
        ),
        cost_estimate=SMALL,
        name="attention_backward",
    )(scal, qfac, *facs, start, o, do, lse, cosine, sine)


def norm_of(values):
    inverse = lax.rsqrt(jnp.mean(values * values, axis=-1, keepdims=True) + EPS)
    return values * inverse, inverse


def turn(values, cosine, sine, sign):
    half = HEAD_DIM // 2
    parts = []
    for r in range(values.shape[0] // HEAD_DIM):
        first = values[r * HEAD_DIM : r * HEAD_DIM + half, :]
        second = values[r * HEAD_DIM + half : (r + 1) * HEAD_DIM, :]
        parts.append(first * cosine - sign * second * sine)
        parts.append(second * cosine + sign * first * sine)
    return jnp.concatenate(parts, axis=0)


def enter_kernel(gain_ref, cos_ref, sin_ref, *refs):
    sources, (xa_ref, qfac_ref, fac_ref) = refs[:7], refs[7:10]
    x_ref, qh, qd, kh, kd, vh, vd, sem = refs[10:]
    copies = [
        pltpu.make_async_copy(source, target, sem.at[k])
        for k, (source, target) in enumerate(zip(sources, (x_ref, qh, qd, kh, kd, vh, vd)))
    ]
    for copy in copies:
        copy.start()
    for copy in copies:
        copy.wait()
    normed = norm_of(x_ref[...].astype(F32))[0]
    xa = (normed * gain_ref[...]).astype(BF)
    xa_ref[...] = xa
    cosine, sine = cos_ref[...], sin_ref[...]
    kdims = turn(jnp.transpose(mm(xa, kd[...])), cosine, sine, 1.0)
    fac_ref[0:KDW, :] = kdims.astype(BF)
    fac_ref[KDW : 2 * KDW, :] = jnp.transpose(mm(xa, vd[...])).astype(BF)
    fac_ref[2 * KDW : 2 * KDW + KHW, :] = mm(kh[...], xa, 1, 1).astype(BF)
    fac_ref[2 * KDW + KHW :, :] = mm(vh[...], xa, 1, 1).astype(BF)
    qfac_ref[0:QHW, :] = mm(qh[...], xa, 1, 1).astype(BF)
    qdims = turn(jnp.transpose(mm(xa, qd[...])), cosine, sine, 1.0)
    qfac_ref[QHW:, :] = qdims.astype(BF)


WHOLE = pl.BlockSpec(memory_space=pltpu.VMEM)
RAW = pl.BlockSpec(memory_space=pl.ANY)
SCALAR = pl.BlockSpec(memory_space=pltpu.SMEM)
SMALL = pl.CostEstimate(flops=1000, transcendentals=0, bytes_accessed=1000)


def enter(x, gain, weights, cosine, sine):
    length, width = x.shape
    moved = (x,) + tuple(weights)
    return pl.pallas_call(
        enter_kernel,
        out_shape=(
            jax.ShapeDtypeStruct((length, width), BF),
            jax.ShapeDtypeStruct((QFW, length), BF),
            jax.ShapeDtypeStruct((FACW, length), BF),
        ),
        in_specs=[WHOLE] * 3 + [RAW] * 7,
        out_specs=[WHOLE] * 3,
        scratch_shapes=[pltpu.VMEM(v.shape, BF) for v in moved] + [pltpu.SemaphoreType.DMA((7,))],
        compiler_params=pltpu.CompilerParams(vmem_limit_bytes=40 << 20),
        name="enter",
    )(gain, cosine, sine, *moved)


def block_place(ids_ref, sizes, index, rows):
    place, scale = 0, 1
    for k in reversed(range(len(sizes))):
        place = place + ((index % sizes[k]) ^ ids_ref[k]) * scale
        index, scale = index // sizes[k], scale * sizes[k]
    return pl.multiple_of(place * rows, rows)


def deal(ids_ref, sizes, t_s, outs):
    blocks, rows = outs[0].shape[:2]
    for side in range(2):

        def one(i, carry, side=side):
            place = block_place(ids_ref, sizes, side * blocks + i, rows)
            outs[side][i] = t_s[pl.ds(place, rows), :].astype(BF)
            return carry

        lax.fori_loop(0, blocks, one, 0)


def collect(ids_ref, sizes, sources, write):
    blocks, rows = sources[0].shape[:2]
    for side in range(2):

        def one(i, carry, side=side):
            place = block_place(ids_ref, sizes, side * blocks + i, rows)
            write(pl.ds(place, rows), sources[side][i].astype(F32))
            return carry

        lax.fori_loop(0, blocks, one, 0)


def leave_out_kernel(sizes, ids_ref, o_ref, dhb_ref, kept_ref, sent_ref, t_s):
    t_s[...] = mm(jnp.transpose(o_ref[...]), dhb_ref[...])
    deal(ids_ref, sizes, t_s, (kept_ref, sent_ref))


SMALLS = 256
RESTW = 2 * KDW + QDW + SMALLS
GAINS = QHW + 2 * KHW
GAIN_COPIES = (SMALLS - GAINS) // 2


def leave_rest_kernel(
    sizes, ids_ref, x_ref, xa_ref, gain_ref, dres_ref, dq_ref, kg_ref, fgain_ref, cos_ref, sin_ref,
    qh, qd, kh, kd, vh, vd, tg_ref, kept_ref, sent_ref, out_ref
):
    normed, inverse = norm_of(x_ref[...].astype(F32))
    xa = xa_ref[...]
    g = kg_ref[...]
    dkd = turn(g[0:KDW, :], cos_ref[...], sin_ref[...], -1.0)
    d_kd = jnp.transpose(dkd).astype(BF)
    d_vd = jnp.transpose(g[KDW : 2 * KDW, :]).astype(BF)
    d_kh = jnp.transpose(g[2 * KDW : 2 * KDW + KHW, :]).astype(BF)
    d_vh = jnp.transpose(g[2 * KDW + KHW :, :]).astype(BF)
    dq = dq_ref[...].astype(F32)
    d_qh = jnp.transpose(dq[0:QHW, :]).astype(BF)
    d_qd = jnp.transpose(dq[QHW:, :]).astype(BF)
    xa_t = jnp.transpose(xa)
    out_ref[:, 0:KDW] = mm(xa_t, d_kd)
    out_ref[:, KDW : 2 * KDW] = mm(xa_t, d_vd)
    out_ref[:, 2 * KDW : 2 * KDW + QDW] = mm(xa_t, d_qd)
    dxa = mm(d_qd, qd[...], 1, 1) + mm(d_qh, qh[...])
    dxa = dxa + mm(d_kd, kd[...], 1, 1) + mm(d_vd, vd[...], 1, 1)
    dxa = dxa + mm(d_kh, kh[...]) + mm(d_vh, vh[...])
    scaled = dxa * gain_ref[...]
    mean = jnp.mean(scaled * normed, axis=-1, keepdims=True)
    tg_ref[...] = (dres_ref[...] + inverse * (scaled - normed * mean)).astype(BF)
    gain_part = jnp.sum(dxa * normed, axis=0, keepdims=True)
    low = g[2 * KDW :, :].astype(BF)
    small = [mm(dq_ref[0:QHW, :], xa), mm(low[0:KHW, :], xa), mm(low[KHW:, :], xa)]
    small += [gain_part] * GAIN_COPIES + [fgain_ref[...]] * GAIN_COPIES
    out_ref[:, 2 * KDW + QDW :] = jnp.transpose(jnp.concatenate(small, axis=0))
    deal(ids_ref, sizes, out_ref, (kept_ref, sent_ref))


def leave_out(sizes, ids, o, dhb):
    depth = o.shape[1]
    blocks = math.prod(sizes) // 2
    return pl.pallas_call(
        functools.partial(leave_out_kernel, sizes),
        out_shape=(jax.ShapeDtypeStruct((blocks, depth // (2 * blocks), depth), BF),) * 2,
        in_specs=[SCALAR] + [WHOLE] * 2,
        out_specs=[WHOLE] * 2,
        scratch_shapes=[pltpu.VMEM((depth, depth), F32)],
        compiler_params=pltpu.CompilerParams(vmem_limit_bytes=40 << 20),
        cost_estimate=SMALL,
        name="leave_out",
    )(ids, o, dhb)


def leave_rest(sizes, ids, x, xa, gain, dres, dq, kg, fgain, cosine, sine, weights):
    length, depth = x.shape
    blocks = math.prod(sizes) // 2
    return pl.pallas_call(
        functools.partial(leave_rest_kernel, sizes),
        out_shape=(jax.ShapeDtypeStruct((length, depth), BF),)
        + (jax.ShapeDtypeStruct((blocks, depth // (2 * blocks), RESTW), BF),) * 2,
        in_specs=[SCALAR] + [WHOLE] * (9 + len(weights)),
        out_specs=[WHOLE] * 3,
        scratch_shapes=[pltpu.VMEM((depth, RESTW), F32)],
        compiler_params=pltpu.CompilerParams(vmem_limit_bytes=40 << 20),
        cost_estimate=SMALL,
        name="leave_rest",
    )(ids, x, xa, gain, dres, dq, kg, fgain, cosine, sine, *weights)


def end_out_kernel(sizes, ids_ref, own_ref, got_ref, proj_ref):
    def write(rows, v):
        proj_ref[rows, :] = v

    collect(ids_ref, sizes, (own_ref, got_ref), write)


def end_out(sizes, ids, own, got):
    depth = own.shape[0] * own.shape[1] * 2
    return pl.pallas_call(
        functools.partial(end_out_kernel, sizes),
        out_shape=jax.ShapeDtypeStruct((depth, depth), F32),
        in_specs=[SCALAR] + [WHOLE] * 2,
        out_specs=WHOLE,
        compiler_params=pltpu.CompilerParams(vmem_limit_bytes=40 << 20),
        cost_estimate=SMALL,
        name="end_out",
    )(ids, own, got)


def end_rest_kernel(
    sizes, ids_ref, own_ref, got_ref, kd_ref, vd_ref, qd_ref, qh_ref, kh_ref, vh_ref, a_ref, f_ref, t_s
):
    def write(rows, v):
        kd_ref[rows, :] = v[:, 0:KDW]
        vd_ref[rows, :] = v[:, KDW : 2 * KDW]
        qd_ref[rows, :] = v[:, 2 * KDW : 2 * KDW + QDW]
        t_s[rows, :] = v[:, 2 * KDW + QDW :]

    collect(ids_ref, sizes, (own_ref, got_ref), write)
    turned = jnp.transpose(t_s[...])
    qh_ref[...] = turned[0:QHW, :]
    kh_ref[...] = turned[QHW : QHW + KHW, :]
    vh_ref[...] = turned[QHW + KHW : GAINS, :]
    a_ref[...] = turned[GAINS : GAINS + 1, :]
    f_ref[...] = turned[GAINS + GAIN_COPIES : GAINS + GAIN_COPIES + 1, :]


def end_rest(sizes, ids, own, got):
    depth = own.shape[0] * own.shape[1] * 2
    shapes = [(depth, KDW), (depth, KDW), (depth, QDW), (QHW, depth), (KHW, depth), (KHW, depth)]
    shapes += [(1, depth), (1, depth)]
    return pl.pallas_call(
        functools.partial(end_rest_kernel, sizes),
        out_shape=tuple(jax.ShapeDtypeStruct(v, F32) for v in shapes),
        in_specs=[SCALAR] + [WHOLE] * 2,
        out_specs=[WHOLE] * 8,
        scratch_shapes=[pltpu.VMEM((depth, SMALLS), F32)],
        compiler_params=pltpu.CompilerParams(vmem_limit_bytes=40 << 20),
        name="end_rest",
    )(ids, own, got)


def after(v, *others):
    return lax.optimization_barrier((v,) + others)[0]


class Grid:
    def __init__(self, dp, tensor):
        self.c = 2
        self.y = dp // 2
        self.x = self.y if tensor % self.y == 0 else 1
        self.z = tensor // self.x
        self.dp, self.tensor = dp, tensor
        self.axes = {
            "c": ("dp", 1, self.c),
            "y": ("dp", self.c, self.y),
            "x": ("tensor", 1, self.x),
            "z": ("tensor", self.x, self.z),
        }

    def size(self, g):
        return self.axes[g][2]

    def place(self, g):
        axis, stride, size = self.axes[g]
        return ((lax.axis_index(axis) // stride) % size).astype(jnp.int32)

    def swap(self, v, g, r):
        axis, stride, size = self.axes[g]
        total = self.dp if axis == "dp" else self.tensor
        return lax.ppermute(v, axis, [(i, i ^ (r * stride)) for i in range(total)])

    def bits(self, g):
        return [1 << k for k in range(self.size(g).bit_length() - 1)]

    def rels(self, g):
        order = [0]
        for bit in reversed(self.bits(g)):
            order = order + [r ^ bit for r in order]
        return order

    def stack(self, v, g):
        v = v[None]
        for bit in reversed(self.bits(g)):
            v = jnp.concatenate([v, self.swap(v, g, bit)], axis=0)
        return v

    def unstack(self, v, g, last=BF):
        bits = self.bits(g)
        for k, bit in enumerate(bits):
            rows = v.shape[0] // 2
            got = self.swap(v[rows:].astype(BF), g, bit)
            v = v[:rows].astype(F32) + got.astype(F32)
        return v[0].astype(last)

    def direct(self, v, g):
        return [v] + [self.swap(v, g, r) for r in self.rels(g)[1:]]

    def swap_masks(self, v, dp_mask, tensor_mask):
        if not tensor_mask:
            return lax.ppermute(v, "dp", [(i, i ^ dp_mask) for i in range(self.dp)])
        if not dp_mask:
            return lax.ppermute(v, "tensor", [(i, i ^ tensor_mask) for i in range(self.tensor)])
        mask = dp_mask * self.tensor + tensor_mask
        pairs = [(i, i ^ mask) for i in range(self.dp * self.tensor)]
        return lax.ppermute(v, ("dp", "tensor"), pairs)

    def levels(self, plan):
        out = []
        for letters in plan:
            masks = [(0, 0)]
            for g in letters:
                axis, stride, size = self.axes[g]
                masks = [
                    (d + r * stride, t) if axis == "dp" else (d, t + r * stride)
                    for d, t in masks
                    for r in range(size)
                ]
            out.append(masks)
        return out

    def numbers(self, plan):
        out = []
        for letters in plan:
            number = jnp.int32(0)
            for g in letters:
                number = number * self.size(g) + self.place(g)
            out.append(number)
        return jnp.stack(out)

    def swaps(self, low, masks):
        return [self.swap_masks(low[m], *masks[m]) for m in range(1, len(masks))]

    def swaps_whole(self, low, masks):
        return [self.swap_masks(low, *m) for m in masks[1:]]


def ffn_kernel(parts, plan, shards, blend, scal_ref, xf_ref, dy_ref, *refs):
    own, arrays = plan
    count = (3 if own else 0) + len(arrays)
    sources, refs = refs[:count], refs[count:]
    if blend:
        mixed_in, dxf_in = refs[:2]
        refs = refs[2:]
    mixed_ref, dxf_ref, inner_ref, dgate_ref, dup_ref, w_s, sem = refs
    width = w_s.shape[2]
    rows = w_s.shape[3] // parts
    copies = []

    def move(source, target):
        copies.append(pltpu.make_async_copy(source, target, sem.at[len(copies)]))

    if own:
        for k in range(3):
            move(sources[k], w_s.at[k, 0])
    for (slots, q), source in zip(arrays, sources[3 if own else 0 :]):
        place = pl.multiple_of((scal_ref[0] ^ q) * rows, rows)
        for i, slot in enumerate(slots):
            move(source.at[i], w_s.at[:, slot, :, pl.ds(place, rows)])
    for copy in copies:
        copy.start()
    for copy in copies:
        copy.wait()
    xf, dy = xf_ref[...], dy_ref[...]
    units, unused, hidden = inner_ref.shape
    for s in range(units):
        wg, wu, wd = ((w_s[k] if units == 1 else w_s[k, s]).reshape(hidden, -1) for k in range(3))
        gate = mm(xf, wg, 1, 1)
        up = mm(xf, wu, 1, 1)
        d_inner = mm(dy, wd, 1, 1)
        sig = 1.0 / (1.0 + jnp.exp(-gate))
        act = gate * sig
        inner = (act * up).astype(BF)
        d_gate = (d_inner * up * sig * (1.0 + gate * (1.0 - sig))).astype(BF)
        d_up = (d_inner * act).astype(BF)
        inner_ref[s] = inner
        dgate_ref[s] = d_gate
        dup_ref[s] = d_up
        dxf = mm(d_gate, wg) + mm(d_up, wu)
        mixed = mm(inner, wd)
        if s == 0 and blend:
            dxf, mixed = dxf + dxf_in[...], mixed + mixed_in[...]
        if s > 0:
            dxf, mixed = dxf + total[0], mixed + total[1]
        total = (dxf, mixed)
    dxf_ref[...] = total[0].astype(dxf_ref.dtype)
    mixed_ref[...] = total[1].astype(mixed_ref.dtype)


def ffn(mine, xf, dy, own, arrays, parts, width, before, out_type, name):
    length, depth = xf.shape
    shards = (1 if own else 0) + sum(len(slots) for slots, q, v in arrays if q == 0)
    hidden = (1, length, shards * width) if width % 16 == 0 else (shards, length, width)
    plan = (bool(own), [(slots, q) for slots, q, v in arrays])
    sources = list(own) + [v for slots, q, v in arrays]
    moves = (3 if own else 0) + sum(len(slots) for slots, q, v in arrays)
    return pl.pallas_call(
        functools.partial(ffn_kernel, parts, plan, shards, bool(before)),
        out_shape=(jax.ShapeDtypeStruct((length, depth), out_type),) * 2
        + (jax.ShapeDtypeStruct(hidden, BF),) * 3,
        in_specs=[SCALAR, WHOLE, WHOLE] + [RAW] * len(sources) + [WHOLE] * len(before),
        out_specs=[WHOLE] * 5,
        scratch_shapes=[
            pltpu.VMEM((3, shards, width, depth), BF),
            pltpu.SemaphoreType.DMA((moves,)),
        ],
        compiler_params=pltpu.CompilerParams(vmem_limit_bytes=58 << 20),
        cost_estimate=SMALL,
        name=name,
    )(mine, xf, dy, *sources, *before)


def products(lefts, rights, width, write):
    slot = 0
    for group in range(len(lefts[0])):
        units, unused, hidden = lefts[0][group].shape
        for s in range(units):
            total = None
            for b in range(len(rights)):
                term = mm(jnp.transpose(lefts[b][group][s]), rights[b][...])
                total = term if total is None else total + term
            for i in range(hidden // width):
                write(slot, total[i * width : (i + 1) * width, :])
                slot += 1


def divide(refs, blocks):
    each = len(refs) // blocks
    return [refs[b * each : (b + 1) * each] for b in range(blocks)]


def store(outs, scal_ref, t_s, slot, first, value):
    rows, lanes = value.shape[0], outs[0].shape[3]
    t_s[0:rows, :] = value
    for q in range(2 * outs[0].shape[0]):
        place = pl.multiple_of((scal_ref[0] ^ q) * lanes, lanes)
        part = t_s[0:rows, pl.ds(place, lanes)]
        outs[q % 2][q // 2, slot, first : first + rows, :] = part.astype(BF)


def gate_up_kernel(blocks, scal_ref, *refs):
    xfs, outs, t_s = refs[:blocks], refs[-3:-1], refs[-1]
    rest = refs[blocks:-3]
    width = outs[0].shape[2] // 2
    for k in range(2):
        lefts = divide(rest[k * len(rest) // 2 : (k + 1) * len(rest) // 2], blocks)

        def write(slot, value, k=k):
            store(outs, scal_ref, t_s, slot, k * width, value)

        products(lefts, xfs, width, write)


def down_kernel(blocks, scal_ref, *refs):
    dys, outs, t_s = refs[:blocks], refs[-3:-1], refs[-1]
    width = outs[0].shape[2]

    def write(slot, value):
        store(outs, scal_ref, t_s, slot, 0, value)

    products(divide(refs[blocks:-3], blocks), dys, width, write)


def grads(kernel, mine, wholes, parts, zs, rows, depth, scratch, name):
    return pl.pallas_call(
        kernel,
        out_shape=(jax.ShapeDtypeStruct((parts // 2, zs, rows, depth // parts), BF),) * 2,
        in_specs=[SCALAR] + [WHOLE] * len(wholes),
        out_specs=[WHOLE] * 2,
        scratch_shapes=scratch,
        compiler_params=pltpu.CompilerParams(vmem_limit_bytes=58 << 20),
        cost_estimate=SMALL,
        name=name,
    )(mine, *wholes)


def unpack_kernel(scal_ref, own_ref, got_ref, gate_ref, up_ref, down_ref):
    width = gate_ref.shape[0]
    for side, ref in enumerate((own_ref, got_ref)):

        @pl.when(pl.program_id(0) % 2 == side)
        def _(ref=ref):
            gate_ref[...] = ref[0, 0:width, :].astype(F32)
            up_ref[...] = ref[0, width : 2 * width, :].astype(F32)
            down_ref[...] = ref[0, 2 * width :, :].astype(F32)


def unpack(mine, own, got):
    half, rows, lanes = own.shape
    width, parts = rows // 3, 2 * half
    column = pl.BlockSpec((width, lanes), lambda q, s: (0, s[0] ^ q))
    return pl.pallas_call(
        unpack_kernel,
        out_shape=(jax.ShapeDtypeStruct((width, parts * lanes), F32),) * 3,
        grid_spec=pltpu.PrefetchScalarGridSpec(
            num_scalar_prefetch=1,
            grid=(parts,),
            in_specs=[pl.BlockSpec((1, rows, lanes), lambda q, s: (q // 2, 0, 0))] * 2,
            out_specs=[column] * 3,
        ),
        compiler_params=pltpu.CompilerParams(dimension_semantics=("arbitrary",)),
        cost_estimate=SMALL,
        name="unpack",
    )(mine, own, got)


def spread_pieces(grid, got, tie):
    entries = []
    for k in range(grid.y):
        piece = got if k == 0 else grid.swap(got, "y", k)
        entries += [(2 * k, piece), (2 * k + 1, grid.swap(after(piece, tie), "c", 1))]
    return entries


def reduce_core(grid, even, odd):
    got = grid.swap(odd, "c", 1)
    goes = [
        (even[k].astype(F32) + got[k].astype(F32)).astype(BF) for k in range(1, grid.y)
    ]
    return (even[0], got[0]), goes


def total_of(*terms):
    total = terms[0].astype(F32)
    for term in terms[1:]:
        total = total + term.astype(F32)
    return total


def contract(left, right, left_dim, right_dim):
    return lax.dot_general(
        left, right, (((left_dim,), (right_dim,)), ((), ())), preferred_element_type=jnp.float32
    )


def norm_back(grad_out, normed, inverse, gain):
    scaled = grad_out * gain
    gain_part = jnp.sum(grad_out * normed, axis=0)
    grad_in = inverse * (scaled - normed * jnp.mean(scaled * normed, axis=-1, keepdims=True))
    return (grad_in, gain_part)


def body(
    grid,
    tokens,
    cotangent,
    segments,
    positions,
    attngain,
    ffngain,
    queryheads,
    querydims,
    keyheads,
    keydims,
    valueheads,
    valuedims,
    outproj,
    gateproj,
    upproj,
    downproj,
):
    x = tokens[0]
    upstream = cotangent[0]
    length, depth = x.shape
    parts = grid.dp
    lanes = depth // parts
    me = lax.axis_index("tensor").astype(jnp.int32)
    spot = jnp.stack([lax.axis_index("dp").astype(jnp.int32), grid.place("z")])
    offset = me * length
    places = lax.dynamic_slice_in_dim(positions[0], offset, length)
    half = HEAD_DIM // 2
    freqs = 10000.0 ** (-jnp.arange(half, dtype=F32) * 2.0 / HEAD_DIM)
    angles = freqs[:, None] * places.astype(F32)[None, :]
    cosine, sine = jnp.cos(angles), jnp.sin(angles)
    start = (offset + jnp.arange(length, dtype=jnp.int32) - places)[:, None]
    scal = jnp.stack([jnp.maximum(offset - places[0], 0) // length, me]).astype(jnp.int32)
    weights = (queryheads.T, querydims, keyheads.T, keydims, valueheads.T, valuedims)

    own = (gateproj.T, upproj.T, downproj)
    width = downproj.shape[0]
    payload = jnp.stack(
        [lax.dynamic_slice_in_dim(v, spot[0] * lanes, lanes, 1) for v in own]
    )
    dys = [upstream] + [grid.swap(upstream, "x", r) for r in range(1, grid.x)]
    xa, qfac, fac = enter(x, attngain[None, :], weights, cosine, sine)
    rels = grid.rels("z")[1:]
    near = [fac] + [grid.swap(fac, "z", r) for r in rels[:-1]]
    near = near + [grid.swap(after(fac, *dys[1:]), "z", r) for r in rels[-1:]]
    near = jnp.stack(near)
    facs = [near] + [grid.swap(near, "x", r) for r in range(1, grid.x)]
    shards = [payload]
    for bit in grid.bits("z")[::-1]:
        got = [grid.swap(v, "z", bit) for v in shards]
        shards = shards + [after(v, near) for v in got]
    remote = shards[1:]

    nearby = jnp.stack(remote[:-1]) if len(remote) > 1 else None
    if len(remote) > 1:
        qfac = after(qfac, nearby)
    attn_out, lse = attention_forward(scal, qfac, facs, start)
    early, late = [], []
    if len(remote) > 1:
        slots = list(range(1, len(remote)))
        early = [(slots, q, v) for q, v in spread_pieces(grid, nearby, attn_out)]

    local = x.astype(F32)
    residual = local + jnp.dot(attn_out, outproj, preferred_element_type=jnp.float32)
    inverse_two = lax.rsqrt(jnp.mean(residual * residual, axis=-1, keepdims=True) + EPS)
    normed_two = residual * inverse_two
    input_two = (normed_two * ffngain).astype(jnp.bfloat16)
    xfs = [input_two] + [
        grid.swap(input_two, "x", r) for r in range(1, grid.x)
    ]

    across = xfs[-1]
    results = [None] * grid.x
    firsts = []
    for k in range(grid.x):
        kind = BF if k and not remote else F32
        if k:
            xfs[k] = after(xfs[k], firsts[0][0])
        firsts.append(
            ffn(spot, xfs[k], dys[k], own, early, parts, width, (), kind, "ffn_early")
        )
    if remote:
        last = after(remote[-1], attn_out)[None]
        late = [([0], q, v) for q, v in spread_pieces(grid, last, after(firsts[0][0], across))]
    for k in reversed(range(grid.x)):
        first = firsts[k]
        if late:
            second = ffn(
                spot, xfs[k], dys[k], (), late, parts, width, first[:2], BF if k else F32, "ffn_late"
            )
            results[k] = (second[0], second[1]) + tuple(
                [first[i], second[i]] for i in range(2, 5)
            )
        else:
            results[k] = (first[0], first[1]) + tuple([first[i]] for i in range(2, 5))
    d_norm_two, ffn_out = results[0][1], results[0][0]
    inners, dgates, dups = (
        [v for k in range(grid.x) for v in results[k][i]] for i in range(2, 5)
    )
    first_parts = grads(
        functools.partial(gate_up_kernel, grid.x),
        spot, xfs + dgates + dups, parts, grid.z, 2 * width, depth,
        [pltpu.VMEM((width, depth), F32)], "gate_up_grads",
    )
    second_parts = grads(
        functools.partial(down_kernel, grid.x),
        spot, dys + inners, parts, grid.z, width, depth,
        [pltpu.VMEM((width, depth), F32)], "down_grads",
    )
    first_kept, first_goes = reduce_core(grid, *first_parts)
    for r in range(1, grid.x):
        got = grid.swap(results[r][1], "x", r)
        d_norm_two = d_norm_two + after(got, second_parts[0], first_goes[0]).astype(F32)
    grad_through, ffngain_part = norm_back(d_norm_two, normed_two, inverse_two, ffngain)
    d_residual = upstream.astype(jnp.float32) + grad_through
    d_res_low = d_residual.astype(jnp.bfloat16)
    d_attended = contract(d_res_low, outproj, 1, 1).astype(jnp.bfloat16)

    plan, z_masks = ("c", "xy", "z"), grid.levels(("z",))[0]
    split_z = depth // (parts * grid.tensor) >= 16
    if not split_z:
        plan = ("c", "xy")
    levels = grid.levels(plan)
    core_masks, xy_masks = levels[0], levels[1]
    sizes = tuple(len(masks) for masks in levels)
    ids = grid.numbers(plan)
    shape = sizes[1:] + (depth // math.prod(sizes), -1)

    def along_z(v):
        low = v.astype(BF)
        if split_z:
            return total_of(v[0], *grid.swaps(low, z_masks)).astype(BF)
        return total_of(v, *grid.swaps_whole(low, z_masks)).astype(BF)

    def share_z(v):
        return jnp.stack([v] + grid.swaps_whole(v, z_masks)) if split_z else v

    second_kept, second_goes = reduce_core(grid, *second_parts)
    kept, sent = leave_out(sizes, ids, attn_out, d_res_low)
    out_sum = total_of(
        kept.reshape(shape), grid.swap_masks(sent.reshape(shape), *core_masks[1])
    )
    out_low = out_sum.astype(BF)
    d_attended = after(d_attended, first_goes[-1], second_goes[-1], out_low)
    back = attention_backward(
        scal, qfac, facs, start, attn_out, d_attended, lse, cosine, sine
    )
    terms, dq = list(back[:-1]), back[-1]

    first_got = [grid.swap(v, "y", k + 1) for k, v in enumerate(first_goes)]
    second_got = [grid.swap(v, "y", k + 1) for k, v in enumerate(second_goes)]
    out_got = grid.swaps(out_low, xy_masks)
    out_first = after(out_sum[0], dq)
    first_kept = (after(first_kept[0], dq), first_kept[1])
    second_kept = (after(second_kept[0], dq), second_kept[1])
    terms[1:] = [after(v, *second_got) for v in terms[1:]]
    out_mine = along_z(total_of(out_first, *out_got))
    out_mine = share_z(out_mine)
    near = terms[0].astype(F32)
    for r in range(1, grid.x):
        near = near + grid.swap(terms[r], "x", r).astype(F32)
    ffn_sum = jnp.concatenate(
        [total_of(*first_kept, *first_got), total_of(*second_kept, *second_got)], axis=1
    )
    low = after(near.astype(BF), out_mine, *first_got)
    key_grads = near[0]
    for i, r in enumerate(grid.rels("z")):
        if i:
            key_grads = key_grads + grid.swap(low[i], "z", r).astype(F32)
    for k, bit in enumerate(grid.bits("z")):
        rows = ffn_sum.shape[0] // 2
        goes = ffn_sum[rows:].astype(BF)
        if k == 0:
            goes = after(goes, key_grads)
            dq = after(dq, goes)
        got = grid.swap(goes, "z", bit)
        if k == 0:
            first_z = got
        ffn_sum = ffn_sum[:rows] + got.astype(F32)
    out_mine = after(out_mine, key_grads)
    out_others = grid.swaps_whole(out_mine, xy_masks)
    out_own = jnp.stack([out_mine] + out_others)
    out_other = grid.swap_masks(out_own, *core_masks[1])

    def flat(v):
        return v.reshape(math.prod(sizes) // 2, -1, v.shape[-1])

    out_part = end_out(sizes, ids, flat(out_own), flat(out_other))
    tokens_grad, kept, sent = leave_rest(
        sizes, ids, x, xa, attngain[None, :], d_residual, dq, key_grads, ffngain_part[None, :],
        cosine, sine, weights,
    )
    rest = total_of(kept.reshape(shape), grid.swap_masks(sent.reshape(shape), *core_masks[1]))
    low = after(rest.astype(BF), *out_others)
    rest = total_of(rest[0], *grid.swaps(low, xy_masks))
    rest = after(rest, first_z)

    ffn_got = [grid.swap(after(results[r][0], rest), "x", r) for r in range(1, grid.x)]
    mixed = (residual + total_of(ffn_out, *ffn_got)).astype(jnp.bfloat16)

    rest = along_z(rest)
    mine = after(ffn_sum[0].astype(BF), rest)
    rest = after(share_z(rest), *ffn_got)
    rest = jnp.stack([rest] + grid.swaps_whole(rest, xy_masks))
    rest = after(rest, out_part)
    others = grid.swap_masks(rest, *core_masks[1])
    mine = jnp.stack([mine] + [grid.swap(mine, "y", k) for k in range(1, grid.y)])
    gate_part, up_part, down_part = unpack(spot, mine, grid.swap(mine, "c", 1))

    kd_grad, vd_grad, qd_grad, qh_grad, kh_grad, vh_grad, again_grad, fgain_grad = end_rest(
        sizes, ids, after(flat(rest), down_part), flat(others)
    )
    return (
        mixed[None],
        tokens_grad[None],
        again_grad[0],
        fgain_grad[0],
        qh_grad.T,
        qd_grad,
        kh_grad.T,
        kd_grad,
        vh_grad.T,
        vd_grad,
        out_part,
        gate_part.T,
        up_part.T,
        down_part,
    )


def solution(mesh):
    grid = Grid(mesh.shape["dp"], mesh.shape["tensor"])
    rows = P("dp", "tensor", None)
    placed = (rows, rows, P("dp", None), P("dp", None)) + (P(),) * 9
    halves = (P(None, "tensor"), P(None, "tensor"), P("tensor", None))
    return jax.shard_map(
        functools.partial(body, grid),
        mesh=mesh,
        in_specs=placed + halves,
        out_specs=(rows, rows) + (P(),) * 9 + halves,
        check_vma=False,
    )
```
